32 devices in a mesh: groups: 2 (over x), mp: 16 (over z, y, core).
Axes of the slice: x: 2, y: 2, z: 4, core: 2. Of those that a mesh axis runs over, the one named last changes fastest.
Arguments:
- tokens: bfloat16 [256, 4096], P('groups'), parts along dimension 0, may hold values from -6 to 6
- up_values: bfloat16 [4096, 16384], P(None, 'mp'), may hold values from -0.09375 to 0.09375
- up_scale: int32 [32, 128], P(None, 'mp'), may hold values from -1 to 1
- diag_blocks: bfloat16 [128, 128, 128], P('mp'), may hold values from -0.5 to 0.5
- partner_blocks: bfloat16 [7, 128, 128, 128], P(None, 'mp'), may hold values from -0.1875 to 0.1875
- pattern: int32 [7, 128], P(None, 'mp'), may hold values 0 or 1
- down_values: bfloat16 [16384, 4096], P('mp'), may hold values from -0.046875 to 0.046875
- down_scale: int32 [128, 32], P('mp'), may hold values from -1 to 1
- norm_gain: float32 [4096], replicated, may hold values from 0.5 to 1.5
- vocab_table: bfloat16 [32768, 4096], P('mp'), may hold values from -0.359375 to 0.359375
- teacher_ids: int32 [256, 8], P('groups'), parts along dimension 0, may hold values from 0 to 32767, as said below
- teacher_logits: float32 [256, 8], P('groups'), parts along dimension 0, may hold values from -12 to 12
Outputs:
- mean_loss: float32 [2], P('groups'), parts along dimension 0
- grad_up: float32 [8192, 16384], P('groups', 'mp'), parts along dimension 0
- grad_down: float32 [32768, 4096], P(('groups', 'mp')), parts along dimension 0
- grad_diag: float32 [256, 128, 128], P(('groups', 'mp')), parts along dimension 0
- grad_partner: float32 [14, 128, 128, 128], P('groups', 'mp'), parts along dimension 0
The draws below stay inside these ranges and needn't reach their ends.
There are 2 independent parts, one for each index of `groups`. The reference program is written for one: setup_inputs(seed, part) draws one part's arguments, and reference() takes and returns one part's arrays. A program takes and returns all parts, laid end to end along the dimension named above; an argument that names none is the same for every part. Nothing has to cross between parts.
Inputs may be any that keep to these rules, and one draw needn't show every extreme that they name: `teacher_ids`: the 8 ids of one token are distinct.
All inputs are finite; a program needn't handle non-finite values. No bound on the sum of `pattern` on one device may be relied on, other than what follows from the above.
Results may differ from the reference program's by a relative error of at most 0.012.
Values may be sent and summed in bfloat16 or wider, within the bound.
No kernel may reach another device: no remote copies, remote signals or barrier semaphores. Data moves between devices by JAX's collectives and lax.ppermute only.
A program may use at most 192 MiB of HBM per device.

```python
import jax
import jax.numpy as jnp
from jax import lax

D = 4096
FF = 16384
BS = 128
V = 32768
K = 8
LEVELS = 7
TOK = 128
NBLK = 128


def draw_teacher_ids(key, part):
    random_scores = jax.random.randint(key, (TOK, V), 0, 16384, dtype=jnp.int32)
    column_number = lax.broadcasted_iota(jnp.int32, (TOK, V), 1)
    row_number = lax.broadcasted_iota(jnp.int32, (TOK, V), 0)
    forced = (row_number == 0) & (column_number == V - 1) | (row_number == 1) & (column_number == 0)
    random_scores = jnp.where(forced, 16384, random_scores)
    random_scores = random_scores * V + column_number
    return lax.top_k(random_scores, K)[1].astype(jnp.int32)


def set_ends(drawn, key, low, top_value):
    longest = drawn.shape.index(max(drawn.shape))
    spots = []
    for shift in (0, 1):
        where = [jax.random.randint(jax.random.fold_in(key, axis), (), 0, length) for axis, length in enumerate(drawn.shape)]
        where[longest] = (where[longest] + shift) % drawn.shape[longest]
        spots.append(tuple(where))
    return drawn.at[spots[0]].set(low).at[spots[1]].set(top_value)


def block_levels(stream_key, extent, cuts, least, top_value):
    def one(axis_at, parts):
        draws = jax.random.uniform(jax.random.fold_in(jax.random.fold_in(stream_key, 6), axis_at), (parts,), jnp.float32, least / len(cuts), top_value / len(cuts))
        return jnp.repeat(jnp.exp(draws), extent[axis_at] // parts).reshape((-1,) + (1,) * (len(extent) - axis_at - 1))

    loudness = one(*cuts[0])
    for cut in cuts[1:]:
        loudness = loudness * one(*cut)
    return loudness


def centred(key, shape, width, reach, split=(), kind=jnp.bfloat16):
    entries = width * jax.random.normal(key, shape, jnp.float32)
    if split:
        entries = entries * block_levels(key, shape, split, -0.22, 0.18)
    return jnp.clip(entries, -reach, reach).astype(kind)


def setup_inputs(seed: int = 0, part: int = 0) -> dict:
    key_list = jax.random.split(jax.random.key(seed), 13)
    part_keys = jax.random.split(jax.random.fold_in(key_list[12], part), 13)
    return {
        "tokens": centred(part_keys[0], (TOK, D), 1.0, 6.0),
        "up_values": centred(key_list[1], (D, FF), D ** -0.5, 0.09375, ((1, 16),)),
        "up_scale": set_ends(jax.random.randint(key_list[2], (D // BS, NBLK), -1, 2), jax.random.fold_in(key_list[2], 1), -1, 1).astype(jnp.int32),
        "diag_blocks": centred(key_list[3], (NBLK, BS, BS), BS ** -0.5, 0.5, ((0, 16),)),
        "partner_blocks": centred(key_list[4], (LEVELS, NBLK, BS, BS), (BS * LEVELS) ** -0.5, 0.1875, ((1, 16),)),
        "pattern": set_ends((jax.random.randint(key_list[5], (LEVELS, NBLK), 0, 4) < 3).astype(jnp.int32), jax.random.fold_in(key_list[5], 1), 0, 1),
        "down_values": centred(key_list[6], (FF, D), FF ** -0.5, 0.046875, ((0, 16),)),
        "down_scale": set_ends(jax.random.randint(key_list[7], (NBLK, D // BS), -1, 2), jax.random.fold_in(key_list[7], 1), -1, 1).astype(jnp.int32),
        "norm_gain": jnp.clip(1.0 + 0.1 * jax.random.normal(key_list[8], (D,), jnp.float32), 0.5, 1.5),
        "vocab_table": centred(key_list[9], (V, D), 0.06, 0.359375, ((0, 16),)),
        "teacher_ids": draw_teacher_ids(jax.random.fold_in(jax.random.fold_in(key_list[12], part), 71), part),
        "teacher_logits": centred(part_keys[11], (TOK, K), 3.0, 12.0, (), jnp.float32),
    }


def scaled_weight(values, exponents, block_width):
    factors = jnp.exp2(exponents.astype(jnp.float32))
    factors = jnp.repeat(jnp.repeat(factors, block_width, axis=0), block_width, axis=1)
    return (values.astype(jnp.float32) * factors).astype(jnp.bfloat16)

def flip_blocks(blocks, bit_level, position):
    old_shape = blocks.shape
    block_count = old_shape[position]
    split_shape = old_shape[:position] + (block_count >> bit_level + 1, 2, 1 << bit_level) + old_shape[position + 1:]
    return jnp.flip(blocks.reshape(split_shape), position + 1).reshape(old_shape)

def silu_slope(pre_value):
    sigmoid_value = jax.nn.sigmoid(pre_value)
    return sigmoid_value * (1.0 + pre_value * (1.0 - sigmoid_value))

def normalize(stream, norm_gain):
    values = stream.astype(jnp.float32)
    inverse = lax.rsqrt(lax.optimization_barrier(jnp.mean(values * values, axis=1, keepdims=True)) + 1e-05)
    return (values * inverse * norm_gain.astype(jnp.float32)).astype(jnp.bfloat16)

def normalize_back(stream, norm_gain, upstream):
    values = stream.astype(jnp.float32)
    inverse = lax.rsqrt(lax.optimization_barrier(jnp.mean(values * values, axis=1, keepdims=True)) + 1e-05)
    unit_rows = values * inverse
    scaled = upstream * norm_gain.astype(jnp.float32)
    return (inverse * (scaled - unit_rows * lax.optimization_barrier(jnp.mean(scaled * unit_rows, axis=1, keepdims=True)))).astype(jnp.bfloat16)

def reference(tokens, up_values, up_scale, diag_blocks, partner_blocks, pattern, down_values, down_scale, norm_gain, vocab_table, teacher_ids, teacher_logits):
    up_eff = scaled_weight(up_values, up_scale, BS)
    down_eff = scaled_weight(down_values, down_scale, BS)
    masked = (partner_blocks.astype(jnp.float32) * pattern.astype(jnp.float32)[:, :, None, None]).astype(jnp.bfloat16)
    pre_act = jnp.dot(tokens, up_eff, preferred_element_type=jnp.float32)
    activated = jax.nn.silu(pre_act).astype(jnp.bfloat16)
    act_blocks = activated.reshape(TOK, NBLK, BS).astype(jnp.float32)
    mixed_blocks = jnp.einsum('tlb,lbc->tlc', act_blocks, diag_blocks.astype(jnp.float32))
    partners = []
    for bit_level in range(LEVELS):
        partner = flip_blocks(act_blocks, bit_level, 1)
        partners.append(partner)
        mixed_blocks = mixed_blocks + jnp.einsum('tlb,lbc->tlc', partner, masked[bit_level].astype(jnp.float32))
    mixed = mixed_blocks.astype(jnp.bfloat16).reshape(TOK, FF)
    delta = jnp.dot(mixed, down_eff, preferred_element_type=jnp.float32)
    stream = (tokens.astype(jnp.float32) + delta).astype(jnp.bfloat16)
    normed = normalize(stream, norm_gain)
    picked_rows = vocab_table[teacher_ids].astype(jnp.float32)
    scores = jnp.einsum('td,tkd->tk', normed.astype(jnp.float32), picked_rows)
    log_student = scores - jnp.log(lax.optimization_barrier(jnp.sum(jnp.exp(scores), axis=1, keepdims=True)))
    teacher_exp = jnp.exp(teacher_logits)
    teacher = teacher_exp / lax.optimization_barrier(jnp.sum(teacher_exp, axis=1, keepdims=True))
    mean_loss = (-jnp.sum(teacher * log_student) / TOK).reshape(1)
    score_grad = (jnp.exp(log_student) - teacher).astype(jnp.bfloat16)
    upstream = jnp.einsum('tk,tkd->td', score_grad.astype(jnp.float32), picked_rows)
    stream_grad = normalize_back(stream, norm_gain, upstream)
    grad_down = jnp.dot(mixed.T, stream_grad, preferred_element_type=jnp.float32)
    mixed_grad = jnp.dot(stream_grad, down_eff.T, preferred_element_type=jnp.float32).astype(jnp.bfloat16)
    grad_blocks = mixed_grad.reshape(TOK, NBLK, BS).astype(jnp.float32)
    grad_diag = jnp.einsum('tlb,tlc->lbc', act_blocks, grad_blocks)
    act_grad = jnp.einsum('tlc,lbc->tlb', grad_blocks, diag_blocks.astype(jnp.float32))
    partner_grads = []
    for bit_level in range(LEVELS):
        partner_grads.append(jnp.einsum('tlb,tlc->lbc', partners[bit_level], grad_blocks) * pattern[bit_level].astype(jnp.float32)[:, None, None])
        outgoing = jnp.einsum('tlc,lbc->tlb', grad_blocks, masked[bit_level].astype(jnp.float32))
        act_grad = act_grad + flip_blocks(outgoing, bit_level, 1)
    pre_grad = (act_grad.reshape(TOK, FF) * silu_slope(pre_act)).astype(jnp.bfloat16)
    grad_up = jnp.dot(tokens.T, pre_grad, preferred_element_type=jnp.float32)
    return (mean_loss, grad_up, grad_down, grad_diag, jnp.stack(partner_grads))
```

```python
import functools

import jax
import jax.numpy as jnp
from jax import lax
from jax.experimental import pallas as pl
from jax.experimental.pallas import tpu as pltpu
from jax.sharding import PartitionSpec as P

F32, BF16 = jnp.float32, jnp.bfloat16
VMEM_LIMIT = 48 << 20
EPS = 1e-05


def bit_groups(bits):
    if bits == 4:
        return [[0], [1], [2, 3]]
    return [[b] for b in range(bits)]


def group_masks(group):
    return [sum(1 << b for i, b in enumerate(group) if j >> i & 1) for j in range(1 << len(group))]


def swap(block, mask):
    if mask == 0:
        return block
    count = lax.axis_size("mp")
    return lax.ppermute(block, "mp", [(i, i ^ mask) for i in range(count)])


def reduce_rows(keep, send, groups):
    received = swap(send, group_masks(groups[0])[1])
    total = (keep.astype(F32) + received.astype(F32)).astype(BF16)
    terms = None
    for n, group in enumerate(groups[1:]):
        masks = group_masks(group)
        rows = total.shape[0] // len(masks)
        terms = [total[:rows]] + [
            swap(total[j * rows : (j + 1) * rows], masks[j]) for j in range(1, len(masks))
        ]
        if n < len(groups) - 2:
            total = sum(t.astype(F32) for t in terms).astype(BF16)
    return terms


def gather_rows(rows, groups):
    for group in reversed(groups):
        masks = group_masks(group)
        rows = jnp.concatenate([rows] + [swap(rows, m) for m in masks[1:]], 0)
    return rows


def row_order(me, tokens, rows, groups, transposed):
    rel = lax.broadcasted_iota(jnp.int32, (tokens, tokens), 1 if transposed else 0)
    whole = lax.broadcasted_iota(jnp.int32, (tokens, tokens), 0 if transposed else 1)
    slot = rel // rows
    mask = jnp.zeros_like(slot)
    place = tokens // rows
    for group in groups:
        place >>= len(group)
        part = slot // place
        for i, b in enumerate(group):
            mask = mask | ((part >> i & 1) << b)
    source = ((me ^ mask) * rows) + rel % rows
    return (source == whole).astype(F32).astype(BF16)


def dot(a, b):
    return jnp.dot(a, b, preferred_element_type=F32)


def dot_nt(a, b):
    return lax.dot_general(a, b, (((1,), (1,)), ((), ())), preferred_element_type=F32)


def dot_tn(a, b):
    return lax.dot_general(a, b, (((0,), (0,)), ((), ())), preferred_element_type=F32)


def spread_factors(scale, width, first, count):
    blocks = scale.shape[1]
    column = lax.broadcasted_iota(jnp.int32, (blocks, count), 1) // width + first
    row = lax.broadcasted_iota(jnp.int32, (blocks, count), 0)
    pick = (column == row).astype(F32).astype(BF16)
    return dot(jnp.exp2(scale.astype(F32)).astype(BF16), pick).astype(BF16)


def params():
    return pltpu.CompilerParams(vmem_limit_bytes=VMEM_LIMIT)


def whole(shape):
    return pl.BlockSpec(shape, lambda i: (0,) * len(shape))


SMEM = pl.BlockSpec(memory_space=pltpu.SMEM)


def cost(flops, nbytes):
    return pl.CostEstimate(flops=int(flops), bytes_accessed=int(nbytes), transcendentals=0)


def up_phase(tokens, values, scale, width):
    token_count, depth = tokens.shape
    hidden = values.shape[1]
    chunk = min(512, depth)
    blocks = chunk // width

    def kernel(tok, val, sc, pre, act, acc):
        i = pl.program_id(0)
        factors = spread_factors(sc[pl.ds(i * blocks, blocks), :], width, 0, hidden)
        weight = jnp.concatenate(
            [val[b * width : (b + 1) * width, :] * factors[b : b + 1, :] for b in range(blocks)], 0
        )
        part = dot(tok[...], weight)

        @pl.when(i == 0)
        def _():
            acc[...] = part

        @pl.when(i > 0)
        def _():
            acc[...] += part

        @pl.when(i == pl.num_programs(0) - 1)
        def _():
            total = acc[...]
            pre[...] = total
            act[...] = (total * jax.nn.sigmoid(total)).astype(BF16)

    return pl.pallas_call(
        kernel,
        grid=(depth // chunk,),
        in_specs=[
            pl.BlockSpec((token_count, chunk), lambda i: (0, i)),
            pl.BlockSpec((chunk, hidden), lambda i: (i, 0)),
            whole(scale.shape),
        ],
        out_specs=[whole((token_count, hidden))] * 2,
        out_shape=[
            jax.ShapeDtypeStruct((token_count, hidden), F32),
            jax.ShapeDtypeStruct((token_count, hidden), BF16),
        ],
        scratch_shapes=[pltpu.VMEM((token_count, hidden), F32)],
        compiler_params=params(),
        cost_estimate=cost(2 * token_count * depth * hidden, depth * hidden * 2),
        name="up_phase",
    )(tokens, values, scale)


def mix_phase(me, pattern, act, received, diag, partner, down, scale, rows, groups):
    token_count, hidden = act.shape
    width = diag.shape[-1]
    levels, blocks = pattern.shape
    features = down.shape[1]
    chunk = min(512, features)
    crossing = len(received)
    local = levels - crossing
    half = token_count // 2

    def kernel(me_ref, pat, act_ref, *refs):
        recv = refs[:crossing]
        diag_ref, part_ref, down_ref, sc, mixed, keep, send = refs[crossing:]
        c = pl.program_id(0)

        @pl.when(c == 0)
        def _():
            order = row_order(me_ref[0], token_count, rows, groups, False)
            for h in range(blocks):
                here = slice(h * width, (h + 1) * width)
                total = dot(act_ref[:, here], diag_ref[h])
                for k in range(levels):
                    if k < local:
                        other = h ^ (1 << k)
                        source = act_ref[:, other * width : (other + 1) * width]
                    else:
                        source = recv[k - local][:, here]
                    keeps = pat[k, h].astype(F32).astype(BF16)
                    total = total + dot(source, part_ref[k, h] * keeps)
                mixed[:, here] = dot(order, total.astype(BF16)).astype(BF16)

        factors = spread_factors(sc[...], width, c * (chunk // width), chunk)
        weight = jnp.concatenate(
            [down_ref[h * width : (h + 1) * width, :] * factors[h : h + 1, :] for h in range(blocks)], 0
        )
        result = dot(mixed[...], weight).astype(BF16)
        keep[...] = result[:half]
        send[...] = result[half:]

    return pl.pallas_call(
        kernel,
        grid=(features // chunk,),
        in_specs=[SMEM, SMEM]
        + [whole((token_count, hidden))] * (1 + crossing)
        + [
            whole(diag.shape),
            whole(partner.shape),
            pl.BlockSpec((hidden, chunk), lambda i: (0, i)),
            whole(scale.shape),
        ],
        out_specs=[whole((token_count, hidden))] + [pl.BlockSpec((half, chunk), lambda i: (0, i))] * 2,
        out_shape=[jax.ShapeDtypeStruct((token_count, hidden), BF16)]
        + [jax.ShapeDtypeStruct((half, features), BF16)] * 2,
        compiler_params=params(),
        cost_estimate=cost(2 * token_count * features * hidden, features * hidden * 2),
        name="mix_phase",
    )(me, pattern, act, *received, diag, partner, down, scale)


def norm_phase(terms, own, gain):
    rows, features = own.shape

    def kernel(*refs):
        n = len(terms)
        own_ref, gain_ref, stream_ref, normed_ref = refs[n:]
        total = refs[0][...].astype(F32)
        for r in refs[1:n]:
            total = total + r[...].astype(F32)
        stream = (own_ref[...].astype(F32) + total).astype(BF16)
        values = stream.astype(F32)
        inverse = lax.rsqrt(jnp.mean(values * values, axis=1, keepdims=True) + EPS)
        stream_ref[...] = stream
        normed_ref[...] = (values * inverse * gain_ref[...]).astype(BF16)

    return pl.pallas_call(
        kernel,
        out_shape=[jax.ShapeDtypeStruct((rows, features), BF16)] * 2,
        compiler_params=params(),
        name="norm_phase",
    )(*terms, own, gain)


def score_phase(me, normed, vocab, ids, rows, groups):
    token_count, features = normed.shape
    entries = vocab.shape[0]
    picks = ids.shape[1]
    chunk = min(256, entries)

    def kernel(me_ref, normed_ref, vocab_ref, ids_ref, out, ordered):
        i = pl.program_id(0)

        @pl.when(i == 0)
        def _():
            order = row_order(me_ref[0], token_count, rows, groups, True)
            ordered[...] = dot(order, normed_ref[...]).astype(BF16)
            out[...] = jnp.zeros_like(out)

        scores = dot_nt(ordered[...], vocab_ref[...])
        offset = ids_ref[...] - (me_ref[0] * entries + i * chunk)
        number = lax.broadcasted_iota(jnp.int32, (token_count, chunk), 1)
        picked = [
            jnp.sum(jnp.where(offset[:, j : j + 1] == number, scores, 0.0), axis=1, keepdims=True)
            for j in range(picks)
        ]
        out[...] += jnp.concatenate(picked, 1)

    return pl.pallas_call(
        kernel,
        grid=(entries // chunk,),
        in_specs=[
            SMEM,
            whole((token_count, features)),
            pl.BlockSpec((chunk, features), lambda i: (i, 0)),
            whole(ids.shape),
        ],
        out_specs=whole((token_count, picks)),
        out_shape=jax.ShapeDtypeStruct((token_count, picks), F32),
        scratch_shapes=[pltpu.VMEM((token_count, features), BF16)],
        compiler_params=params(),
        cost_estimate=cost(2 * token_count * features * entries, features * entries * 2),
        name="score_phase",
    )(me, normed, vocab, ids)


def loss_phase(me, scores, logits, ids, vocab, rows, groups):
    token_count, picks = scores.shape
    entries, features = vocab.shape
    chunk = min(512, features)
    half = token_count // 2

    def kernel(me_ref, scores_ref, logits_ref, ids_ref, vocab_ref, loss, keep, send, spread):
        i = pl.program_id(0)

        @pl.when(i == 0)
        def _():
            values = scores_ref[...]
            log_student = values - jnp.log(jnp.sum(jnp.exp(values), axis=1, keepdims=True))
            weights = jnp.exp(logits_ref[...])
            teacher = weights / jnp.sum(weights, axis=1, keepdims=True)
            each = jnp.sum(teacher * log_student, axis=1, keepdims=True)
            loss[...] = -jnp.sum(each, axis=0, keepdims=True) / token_count
            grad = (jnp.exp(log_student) - teacher).astype(BF16).astype(F32)
            offset = ids_ref[...] - me_ref[0] * entries
            number = lax.broadcasted_iota(jnp.int32, (token_count, entries), 1)
            total = jnp.zeros((token_count, entries), F32)
            for j in range(picks):
                total = jnp.where(offset[:, j : j + 1] == number, grad[:, j : j + 1], total)
            order = row_order(me_ref[0], token_count, rows, groups, False)
            spread[...] = dot(order, total.astype(BF16)).astype(BF16)

        result = dot(spread[...], vocab_ref[...]).astype(BF16)
        keep[...] = result[:half]
        send[...] = result[half:]

    return pl.pallas_call(
        kernel,
        grid=(features // chunk,),
        in_specs=[
            SMEM,
            whole(scores.shape),
            whole(logits.shape),
            whole(ids.shape),
            pl.BlockSpec((entries, chunk), lambda i: (0, i)),
        ],
        out_specs=[whole((1, 1))] + [pl.BlockSpec((half, chunk), lambda i: (0, i))] * 2,
        out_shape=[jax.ShapeDtypeStruct((1, 1), F32)]
        + [jax.ShapeDtypeStruct((half, features), BF16)] * 2,
        scratch_shapes=[pltpu.VMEM((token_count, entries), BF16)],
        compiler_params=params(),
        cost_estimate=cost(2 * token_count * features * entries, features * entries * 2),
        name="loss_phase",
    )(me, scores, logits, ids, vocab)


def norm_back_phase(terms, stream, gain):
    rows, features = stream.shape

    def kernel(*refs):
        n = len(terms)
        stream_ref, gain_ref, out = refs[n:]
        upstream = refs[0][...].astype(F32)
        for r in refs[1:n]:
            upstream = upstream + r[...].astype(F32)
        values = stream_ref[...].astype(F32)
        inverse = lax.rsqrt(jnp.mean(values * values, axis=1, keepdims=True) + EPS)
        unit = values * inverse
        scaled = upstream * gain_ref[...]
        out[...] = (
            inverse * (scaled - unit * jnp.mean(scaled * unit, axis=1, keepdims=True))
        ).astype(BF16)

    return pl.pallas_call(
        kernel,
        out_shape=jax.ShapeDtypeStruct((rows, features), BF16),
        compiler_params=params(),
        name="norm_back_phase",
    )(*terms, stream, gain)


def mixed_grad_phase(me, pattern, grad, down, scale, partner, rows, groups, local):
    token_count, features = grad.shape
    hidden = down.shape[0]
    levels, blocks = pattern.shape
    width = partner.shape[-1]
    crossing = levels - local

    def kernel(me_ref, pat, grad_ref, down_ref, sc, part_ref, mixed_grad, *refs):
        outgoing, factors, order = refs[:crossing], refs[crossing], refs[crossing + 1]
        h = pl.program_id(0)

        @pl.when(h == 0)
        def _():
            factors[...] = spread_factors(sc[...], width, 0, features).astype(F32)
            order[...] = row_order(me_ref[0], token_count, rows, groups, True)

        weight = down_ref[...] * factors[pl.ds(h, 1), :].astype(BF16)
        result = dot_nt(grad_ref[...], weight).astype(BF16)
        result = dot(order[...], result).astype(BF16)
        mixed_grad[...] = result
        for n in range(crossing):
            keeps = pat[local + n, h].astype(F32).astype(BF16)
            outgoing[n][...] = dot_nt(result, part_ref[local + n, 0] * keeps).astype(BF16)

    block = pl.BlockSpec((token_count, width), lambda i: (0, i))
    return pl.pallas_call(
        kernel,
        grid=(blocks,),
        in_specs=[
            SMEM,
            SMEM,
            whole((token_count, features)),
            pl.BlockSpec((width, features), lambda i: (i, 0)),
            whole(scale.shape),
            pl.BlockSpec((levels, 1, width, width), lambda i: (0, i, 0, 0)),
        ],
        out_specs=[block] * (1 + crossing),
        out_shape=[jax.ShapeDtypeStruct((token_count, hidden), BF16)] * (1 + crossing),
        scratch_shapes=[
            pltpu.VMEM((blocks, features), F32),
            pltpu.VMEM((token_count, token_count), BF16),
        ],
        compiler_params=params(),
        cost_estimate=cost(2 * token_count * features * hidden, features * hidden * 2),
        name="mixed_grad_phase",
    )(me, pattern, grad, down, scale, partner)


def block_grad_phase(pattern, act, received, mixed_grad, diag, partner):
    token_count, hidden = act.shape
    levels, blocks = pattern.shape
    width = diag.shape[-1]
    crossing = len(received)
    local = levels - crossing

    def kernel(pat, act_ref, mg, *refs):
        recv = refs[:crossing]
        diag_ref, part_ref, grad_diag, grad_part, act_grad = refs[crossing:]
        h = pl.program_id(0)

        def columns(index):
            return pl.ds(pl.multiple_of(index * width, width), width)

        grad = mg[:, columns(h)]
        grad_diag[0] = dot_tn(act_ref[:, columns(h)], grad)
        total = dot_nt(grad, diag_ref[h])
        for k in range(levels):
            keeps = pat[k, h].astype(F32)
            if k < local:
                other = h ^ (1 << k)
                source = act_ref[:, columns(other)]
                kept = pat[k, other].astype(F32).astype(BF16)
                total = total + dot_nt(mg[:, columns(other)], part_ref[k, other] * kept)
            else:
                source = recv[k - local][:, columns(h)]
            grad_part[k, 0] = dot_tn(source, grad) * keeps
        act_grad[...] = total

    return pl.pallas_call(
        kernel,
        grid=(blocks,),
        in_specs=[SMEM]
        + [whole((token_count, hidden))] * (2 + crossing)
        + [whole(diag.shape), whole(partner.shape)],
        out_specs=[
            pl.BlockSpec((1, width, width), lambda i: (i, 0, 0)),
            pl.BlockSpec((levels, 1, width, width), lambda i: (0, i, 0, 0)),
            pl.BlockSpec((token_count, width), lambda i: (0, i)),
        ],
        out_shape=[
            jax.ShapeDtypeStruct(diag.shape, F32),
            jax.ShapeDtypeStruct(partner.shape, F32),
            jax.ShapeDtypeStruct((token_count, hidden), F32),
        ],
        compiler_params=params(),
        cost_estimate=cost(2 * token_count * hidden * width * 12, 12 << 20),
        name="block_grad_phase",
    )(pattern, act, mixed_grad, *received, diag, partner)


def down_grad_phase(mixed, grad):
    token_count, hidden = mixed.shape
    features = grad.shape[1]
    chunk = min(512, features)

    def kernel(mixed_ref, grad_ref, out, turned):
        @pl.when(pl.program_id(0) == 0)
        def _():
            turned[...] = mixed_ref[...].T

        out[...] = dot(turned[...], grad_ref[...])

    return pl.pallas_call(
        kernel,
        grid=(features // chunk,),
        in_specs=[
            whole((token_count, hidden)),
            pl.BlockSpec((token_count, chunk), lambda i: (0, i)),
        ],
        out_specs=pl.BlockSpec((hidden, chunk), lambda i: (0, i)),
        out_shape=jax.ShapeDtypeStruct((hidden, features), F32),
        scratch_shapes=[pltpu.VMEM((hidden, token_count), BF16)],
        compiler_params=params(),
        cost_estimate=cost(2 * token_count * features * hidden, features * hidden * 4),
        name="down_grad_phase",
    )(mixed, grad)


def up_grad_phase(tokens, pre, act_grad, received):
    token_count, depth = tokens.shape
    hidden = pre.shape[1]
    chunk = min(512, depth)

    def kernel(tok, pre_ref, grad_ref, *refs):
        recv, (out, pre_grad) = refs[: len(received)], refs[len(received) :]

        @pl.when(pl.program_id(0) == 0)
        def _():
            total = grad_ref[...]
            for r in recv:
                total = total + r[...].astype(F32)
            value = pre_ref[...]
            gate = jax.nn.sigmoid(value)
            pre_grad[...] = (total * (gate * (1.0 + value * (1.0 - gate)))).astype(BF16)

        out[...] = dot_tn(tok[...], pre_grad[...])

    return pl.pallas_call(
        kernel,
        grid=(depth // chunk,),
        in_specs=[pl.BlockSpec((token_count, chunk), lambda i: (0, i))]
        + [whole((token_count, hidden))] * (2 + len(received)),
        out_specs=pl.BlockSpec((chunk, hidden), lambda i: (i, 0)),
        out_shape=jax.ShapeDtypeStruct((depth, hidden), F32),
        scratch_shapes=[pltpu.VMEM((token_count, hidden), BF16)],
        compiler_params=params(),
        cost_estimate=cost(2 * token_count * depth * hidden, depth * hidden * 4),
        name="up_grad_phase",
    )(tokens, pre, act_grad, *received)


def on_device(
    tokens,
    up_values,
    up_scale,
    diag_blocks,
    partner_blocks,
    pattern,
    down_values,
    down_scale,
    norm_gain,
    vocab_table,
    teacher_ids,
    teacher_logits,
):
    width = diag_blocks.shape[-1]
    token_count = tokens.shape[0]
    blocks = diag_blocks.shape[0]
    levels = partner_blocks.shape[0]
    local = blocks.bit_length() - 1
    count = lax.axis_size("mp")
    bits = count.bit_length() - 1
    groups = bit_groups(bits)
    rows = token_count // count
    me = lax.axis_index("mp").astype(jnp.int32).reshape(1)
    gain = norm_gain.reshape(1, -1)
    own = lax.dynamic_slice_in_dim(tokens, me[0] * rows, rows, 0)

    pre, act = up_phase(tokens, up_values, up_scale, width)
    received = [swap(act, 1 << k - local) for k in range(local, levels)]
    mixed, keep, send = mix_phase(
        me, pattern, act, received, diag_blocks, partner_blocks, down_values, down_scale, rows, groups
    )
    stream, normed = norm_phase(reduce_rows(keep, send, groups), own, gain)
    normed = gather_rows(normed, groups)
    scores = score_phase(me, normed, vocab_table, teacher_ids, rows, groups)
    for b in range(bits):
        scores = scores + swap(scores, 1 << b)
    loss, keep, send = loss_phase(me, scores, teacher_logits, teacher_ids, vocab_table, rows, groups)
    grad = norm_back_phase(reduce_rows(keep, send, groups), stream, gain)
    grad = gather_rows(grad, groups)
    mixed_grad, *outgoing = mixed_grad_phase(
        me, pattern, grad, down_values, down_scale, partner_blocks, rows, groups, local
    )
    incoming = [swap(block, 1 << n) for n, block in enumerate(outgoing)]
    grad_diag, grad_partner, act_grad = block_grad_phase(
        pattern, act, received, mixed_grad, diag_blocks, partner_blocks
    )
    grad_down = down_grad_phase(mixed, grad)
    grad_up = up_grad_phase(tokens, pre, act_grad, incoming)
    return (loss.reshape(1), grad_up, grad_down, grad_diag, grad_partner)


def solution(mesh):
    return jax.shard_map(
        on_device,
        mesh=mesh,
        in_specs=(
            P("groups", None),
            P(None, "mp"),
            P(None, "mp"),
            P("mp", None, None),
            P(None, "mp", None, None),
            P(None, "mp"),
            P("mp", None),
            P("mp", None),
            P(),
            P("mp", None),
            P("groups", None),
            P("groups", None),
        ),
        out_specs=(
            P("groups"),
            P("groups", "mp"),
            P(("groups", "mp"), None),
            P(("groups", "mp"), None, None),
            P("groups", "mp", None, None),
        ),
        check_vma=False,
    )
```

```python
import functools

import jax
import jax.numpy as jnp
from jax import lax
from jax.experimental import pallas as pl
from jax.experimental.pallas import tpu as pltpu
from jax.sharding import PartitionSpec as P

F32, BF16 = jnp.float32, jnp.bfloat16
EPS = 1e-05
LANES = 128
SHARED = 2
SLOTS = 32
HELD = 128


def bit_groups(bits):
    if bits == 4:
        return [[0], [1], [2, 3]]
    return [[b] for b in range(bits)]


def group_masks(group):
    return [sum(1 << b for i, b in enumerate(group) if j >> i & 1) for j in range(1 << len(group))]


def swap(block, mask):
    if mask == 0:
        return block
    count = lax.axis_size("mp")
    return lax.ppermute(block, "mp", [(i, i ^ mask) for i in range(count)])


def reduce_rows(keep, send, groups, after=None):
    for n, group in enumerate(groups):
        masks = group_masks(group)
        if n == len(groups) - 1:
            return [keep] + [swap(s, m) for s, m in zip(send, masks[1:])]
        total = swap(send if n == 0 else send[0], masks[1])
        parts = 1 << len(groups[n + 1])
        keep, *send = add_phase(keep, total, parts, after[n] if after else [])


def gather_rows(rows, groups):
    for group in reversed(groups):
        masks = group_masks(group)
        rows = jnp.concatenate([rows] + [swap(rows, m) for m in masks[1:]], 0)
    return rows


def row_order(me, tokens, rows, groups, transposed):
    rel = lax.broadcasted_iota(jnp.int32, (tokens, tokens), 1 if transposed else 0)
    whole = lax.broadcasted_iota(jnp.int32, (tokens, tokens), 0 if transposed else 1)
    slot = rel // rows
    mask = jnp.zeros_like(slot)
    place = tokens // rows
    for group in groups:
        place >>= len(group)
        part = slot // place
        for i, b in enumerate(group):
            mask = mask | ((part >> i & 1) << b)
    source = ((me ^ mask) * rows) + rel % rows
    return (source == whole).astype(F32).astype(BF16)


def dot(a, b):
    return jnp.dot(a, b, preferred_element_type=F32)


def dot_nt(a, b):
    return lax.dot_general(a, b, (((1,), (1,)), ((), ())), preferred_element_type=F32)


def dot_tn(a, b):
    return lax.dot_general(a, b, (((0,), (0,)), ((), ())), preferred_element_type=F32)


def spread_factors(scale, width, first, count):
    blocks = scale.shape[1]
    column = lax.broadcasted_iota(jnp.int32, (blocks, count), 1) // width + first
    row = lax.broadcasted_iota(jnp.int32, (blocks, count), 0)
    pick = (column == row).astype(F32).astype(BF16)
    return dot(jnp.exp2(scale.astype(F32)).astype(BF16), pick).astype(BF16)


def params(mebibytes=16):
    return pltpu.CompilerParams(vmem_limit_bytes=mebibytes << 20)


def whole(shape):
    return pl.BlockSpec(shape, lambda i: (0,) * len(shape))


SMEM = pl.BlockSpec(memory_space=pltpu.SMEM)
UNREAD = pl.BlockSpec(memory_space=pl.ANY)
VMEM = pl.BlockSpec(memory_space=pltpu.VMEM)
HBM = pl.BlockSpec(memory_space=pltpu.HBM)


def columns(index, width):
    return pl.ds(pl.multiple_of(index * width, width), width)


def cost(flops, nbytes):
    return pl.CostEstimate(flops=int(flops), bytes_accessed=int(nbytes), transcendentals=0)


def up_phase(tokens, values, scale, width, after):
    token_count, depth = tokens.shape
    hidden = values.shape[1]
    chunk = min(512, depth)
    blocks = chunk // width
    steps = depth // chunk

    def kernel(tok, val, sc, *refs):
        pre, act, factors, table, arrived = refs[len(after) :]

        def fetch(i):
            return pltpu.make_async_copy(val.at[columns(i, chunk), :], table.at[i], arrived.at[i])

        for i in range(steps):
            fetch(i).start()
        factors[...] = spread_factors(sc[...], width, 0, hidden).astype(F32)

        def step(i, carry):
            fetch(i).wait()
            weight = jnp.concatenate(
                [
                    table[i, b * width : (b + 1) * width, :]
                    * factors[pl.ds(i * blocks + b, 1), :].astype(BF16)
                    for b in range(blocks)
                ],
                0,
            )
            part = dot(tok[:, columns(i, chunk)], weight)
            pre[...] = jnp.where(i == 0, part, pre[...] + part)
            return carry

        lax.fori_loop(0, steps, step, 0)
        total = pre[...]
        act[...] = (total * jax.nn.sigmoid(total)).astype(BF16)

    return pl.pallas_call(
        kernel,
        in_specs=[VMEM, HBM, VMEM] + [UNREAD] * len(after),
        out_specs=[VMEM] * 2,
        out_shape=[
            jax.ShapeDtypeStruct((token_count, hidden), F32),
            jax.ShapeDtypeStruct((token_count, hidden), BF16),
        ],
        scratch_shapes=[
            pltpu.VMEM((depth // width, hidden), F32),
            pltpu.VMEM((steps, chunk, hidden), BF16),
            pltpu.SemaphoreType.DMA((steps,)),
        ],
        compiler_params=params(52),
        cost_estimate=cost(2 * token_count * depth * hidden, depth * hidden * 2),
        name="up_phase",
    )(tokens, values, scale, *after)


def own_mix_phase(pattern, act, diag, partner, local, after):
    token_count, hidden = act.shape
    width = diag.shape[-1]
    levels, blocks = pattern.shape

    def kernel(pat, act_ref, diag_ref, part_ref, *refs):
        out = refs[-1]

        def mix(h):
            source = [act_ref[:, columns(h, width)]]
            weight = [diag_ref[h]]
            for k in range(local):
                source.append(act_ref[:, columns(h ^ (1 << k), width)])
                weight.append(part_ref[k, h] * pat[k, h].astype(F32).astype(BF16))
            out[:, columns(h, width)] = dot(
                jnp.concatenate(source, 1), jnp.concatenate(weight, 0)
            )

        for h in range(blocks):
            mix(h)

    return pl.pallas_call(
        kernel,
        in_specs=[SMEM] + [VMEM] * 3 + [UNREAD] * len(after),
        out_specs=VMEM,
        out_shape=jax.ShapeDtypeStruct((token_count, hidden), F32),
        compiler_params=params(),
        cost_estimate=cost(2 * token_count * hidden * width * 4, 4 << 20),
        name="own_mix_phase",
    )(pattern, act, diag, partner, *after)


def mix_phase(me, pattern, own, received, partner, down, scale, rows, groups, after):
    token_count, hidden = own.shape
    width = partner.shape[-1]
    levels, blocks = pattern.shape
    features = down.shape[1]
    chunk = min(512, features)
    steps = features // chunk
    crossing = len(received)
    local = levels - crossing
    half = token_count // 2

    def kernel(me_ref, pat, own_ref, *refs):
        recv = refs[:crossing]
        part_ref, down_ref, sc = refs[crossing : crossing + 3]
        mixed, keep, send, factors, table, arrived = refs[-6:]

        def fetch(c):
            return pltpu.make_async_copy(
                down_ref.at[:, columns(c, chunk)], table.at[c], arrived.at[c]
            )

        for c in range(steps):
            fetch(c).start()
        factors[...] = spread_factors(sc[...], width, 0, features).astype(F32)
        order = row_order(me_ref[0], token_count, rows, groups, False)

        def mix(h):
            here = columns(h, width)
            source = jnp.concatenate([r[:, here] for r in recv], 1)
            weight = jnp.concatenate(
                [
                    part_ref[k, h] * pat[k, h].astype(F32).astype(BF16)
                    for k in range(local, levels)
                ],
                0,
            )
            total = own_ref[:, here] + dot(source, weight)
            mixed[:, here] = dot(order, total.astype(BF16)).astype(BF16)

        for h in range(blocks):
            mix(h)

        def project(c, carry):
            fetch(c).wait()
            weight = jnp.concatenate(
                [
                    table[c, h * width : (h + 1) * width, :]
                    * factors[h : h + 1, columns(c, chunk)].astype(BF16)
                    for h in range(blocks)
                ],
                0,
            )
            result = dot(mixed[...], weight).astype(BF16)
            keep[:, columns(c, chunk)] = result[:half]
            send[:, columns(c, chunk)] = result[half:]
            return carry

        lax.fori_loop(0, steps, project, 0, unroll=2)

    return pl.pallas_call(
        kernel,
        in_specs=[SMEM, SMEM] + [VMEM] * (2 + crossing) + [HBM, VMEM] + [UNREAD] * len(after),
        out_specs=[VMEM] * 3,
        out_shape=[jax.ShapeDtypeStruct((token_count, hidden), BF16)]
        + [jax.ShapeDtypeStruct((half, features), BF16)] * 2,
        scratch_shapes=[
            pltpu.VMEM((blocks, features), F32),
            pltpu.VMEM((steps, hidden, chunk), BF16),
            pltpu.SemaphoreType.DMA((steps,)),
        ],
        compiler_params=params(52),
        cost_estimate=cost(2 * token_count * features * hidden, features * hidden * 2),
        name="mix_phase",
    )(me, pattern, own, *received, partner, down, scale, *after)


def add_phase(keep, received, parts, after):
    rows, features = keep.shape
    rows //= parts

    def kernel(a, b, *refs):
        outs = refs[len(after) :]
        for n, out in enumerate(outs):
            here = slice(n * rows, (n + 1) * rows)
            out[...] = (a[here, :].astype(F32) + b[here, :].astype(F32)).astype(BF16)

    return pl.pallas_call(
        kernel,
        in_specs=[VMEM] * 2 + [UNREAD] * len(after),
        out_specs=[VMEM] * parts,
        out_shape=[jax.ShapeDtypeStruct((rows, features), BF16)] * parts,
        compiler_params=params(),
        name="add_phase",
    )(keep, received, *after)


def norm_phase(terms, own, gain):
    rows, features = own.shape

    def kernel(*refs):
        n = len(terms)
        own_ref, gain_ref, stream_ref, normed_ref = refs[n:]
        total = refs[0][...].astype(F32)
        for r in refs[1:n]:
            total = total + r[...].astype(F32)
        stream = (own_ref[...].astype(F32) + total).astype(BF16)
        values = stream.astype(F32)
        inverse = lax.rsqrt(jnp.mean(values * values, axis=1, keepdims=True) + EPS)
        stream_ref[...] = stream
        normed_ref[...] = (values * inverse * gain_ref[...]).astype(BF16)

    return pl.pallas_call(
        kernel,
        out_shape=[jax.ShapeDtypeStruct((rows, features), BF16)] * 2,
        compiler_params=params(),
        name="norm_phase",
    )(*terms, own, gain)


def score_phase(me, normed, vocab, ids, rows, groups):
    token_count, features = normed.shape
    entries = vocab.shape[0]
    picks = ids.shape[1]
    chunk = min(256, entries)

    def kernel(me_ref, normed_ref, vocab_ref, ids_ref, out, ordered):
        i = pl.program_id(0)

        @pl.when(i == 0)
        def _():
            order = row_order(me_ref[0], token_count, rows, groups, True)
            ordered[...] = dot(order, normed_ref[...]).astype(BF16)
            out[...] = jnp.zeros_like(out)

        scores = dot_nt(ordered[...], vocab_ref[...])
        offset = ids_ref[...] - (me_ref[0] * entries + i * chunk)
        number = lax.broadcasted_iota(jnp.int32, (token_count, chunk), 1)
        picked = [
            jnp.sum(jnp.where(offset[:, j : j + 1] == number, scores, 0.0), axis=1, keepdims=True)
            for j in range(picks)
        ]
        out[...] += jnp.concatenate(picked, 1)

    return pl.pallas_call(
        kernel,
        grid=(entries // chunk,),
        in_specs=[
            SMEM,
            whole((token_count, features)),
            pl.BlockSpec((chunk, features), lambda i: (i, 0)),
            whole(ids.shape),
        ],
        out_specs=whole((token_count, picks)),
        out_shape=jax.ShapeDtypeStruct((token_count, picks), F32),
        scratch_shapes=[pltpu.VMEM((token_count, features), BF16)],
        compiler_params=params(24),
        cost_estimate=cost(2 * token_count * features * entries, features * entries * 2),
        name="score_phase",
    )(me, normed, vocab, ids)


def loss_phase(me, scores, logits, ids, vocab, rows, groups):
    token_count, picks = scores.shape
    entries, features = vocab.shape
    chunk = min(512, features)
    half = token_count // 2

    def kernel(me_ref, scores_ref, logits_ref, ids_ref, vocab_ref, loss, keep, send, spread):
        i = pl.program_id(0)

        @pl.when(i == 0)
        def _():
            values = scores_ref[...]
            log_student = values - jnp.log(jnp.sum(jnp.exp(values), axis=1, keepdims=True))
            weights = jnp.exp(logits_ref[...])
            teacher = weights / jnp.sum(weights, axis=1, keepdims=True)
            each = jnp.sum(teacher * log_student, axis=1, keepdims=True)
            loss[...] = -jnp.sum(each, axis=0, keepdims=True) / token_count
            grad = (jnp.exp(log_student) - teacher).astype(BF16).astype(F32)
            offset = ids_ref[...] - me_ref[0] * entries
            number = lax.broadcasted_iota(jnp.int32, (token_count, entries), 1)
            total = jnp.zeros((token_count, entries), F32)
            for j in range(picks):
                total = jnp.where(offset[:, j : j + 1] == number, grad[:, j : j + 1], total)
            order = row_order(me_ref[0], token_count, rows, groups, False)
            spread[...] = dot(order, total.astype(BF16)).astype(BF16)

        result = dot(spread[...], vocab_ref[...]).astype(BF16)
        keep[...] = result[:half]
        send[...] = result[half:]

    return pl.pallas_call(
        kernel,
        grid=(features // chunk,),
        in_specs=[
            SMEM,
            whole(scores.shape),
            whole(logits.shape),
            whole(ids.shape),
            pl.BlockSpec((entries, chunk), lambda i: (0, i)),
        ],
        out_specs=[whole((1, 1))] + [pl.BlockSpec((half, chunk), lambda i: (0, i))] * 2,
        out_shape=[jax.ShapeDtypeStruct((1, 1), F32)]
        + [jax.ShapeDtypeStruct((half, features), BF16)] * 2,
        scratch_shapes=[pltpu.VMEM((token_count, entries), BF16)],
        compiler_params=params(24),
        cost_estimate=cost(2 * token_count * features * entries, features * entries * 2),
        name="loss_phase",
    )(me, scores, logits, ids, vocab)


def split_loss(loss):
    lane = lax.broadcasted_iota(jnp.int32, (loss.shape[0], LANES), 1)
    high = loss.astype(BF16).astype(F32)
    middle = (loss - high).astype(BF16).astype(F32)
    low = loss - high - middle
    return jnp.where(lane == 0, high, jnp.where(lane == 1, middle, jnp.where(lane == 2, low, 0.0)))


def norm_back_phase(terms, stream, gain, loss):
    rows, features = stream.shape

    def kernel(*refs):
        n = len(terms)
        stream_ref, gain_ref, loss_ref, out = refs[n:]
        upstream = refs[0][...].astype(F32)
        for r in refs[1:n]:
            upstream = upstream + r[...].astype(F32)
        values = stream_ref[...].astype(F32)
        inverse = lax.rsqrt(jnp.mean(values * values, axis=1, keepdims=True) + EPS)
        unit = values * inverse
        scaled = upstream * gain_ref[...]
        out[:, :features] = (
            inverse * (scaled - unit * jnp.mean(scaled * unit, axis=1, keepdims=True))
        ).astype(BF16)
        out[:, features:] = split_loss(jnp.broadcast_to(loss_ref[...], (rows, 1))).astype(BF16)

    return pl.pallas_call(
        kernel,
        out_shape=jax.ShapeDtypeStruct((rows, features + LANES), BF16),
        compiler_params=params(),
        name="norm_back_phase",
    )(*terms, stream, gain, loss)


def slot_of(index, count, groups):
    slot = jnp.zeros_like(index)
    place = count
    for group in groups:
        place >>= len(group)
        for i, b in enumerate(group):
            slot = slot | ((index >> b & 1) << i) * place
    return slot


def pick_phase(me, ids, vocab, rows, groups):
    token_count, picks = ids.shape
    entries, features = vocab.shape
    count = token_count // rows
    sharers = count >> SHARED
    chunk = min(512, features)
    half = count * SLOTS // 2
    wide = picks * sharers

    def ones(mask):
        return mask.astype(F32).astype(BF16)

    def iota(shape, axis):
        return lax.broadcasted_iota(jnp.int32, shape, axis)

    def kernel(me_ref, ids_ref, vocab_ref, rank_ref, flag_ref, keep, send, chosen, layout, table, arrived):
        def fetch(c):
            return pltpu.make_async_copy(
                vocab_ref.at[:, columns(c, chunk)], table.at[c], arrived.at[c]
            )

        for c in range(features // chunk):
            fetch(c).start()

        mine = me_ref[0]
        wanted = ids_ref[...]
        shard = wanted // entries
        lane = iota((token_count, wide), 1)
        sharer = jnp.full((token_count, wide), -1, jnp.int32)
        for j in range(picks):
            sharer = jnp.where(lane // sharers == j, shard[:, j : j + 1] >> SHARED, sharer)
        asks = (sharer == lane % sharers).astype(F32)
        row, column = iota((token_count, token_count), 0), iota((token_count, token_count), 1)
        together = row // rows == column // rows
        earlier = dot(ones(together & (column < row)), asks.astype(BF16))
        total = dot(ones(together), asks.astype(BF16)).astype(BF16)
        a, b = iota((wide, wide), 0), iota((wide, wide), 1)
        before = dot(total, ones((a % sharers == b % sharers) & (a // sharers < b // sharers)))
        gathered = (asks * (earlier + before)).astype(BF16)
        rank = dot(gathered, ones(iota((wide, picks), 0) // sharers == iota((wide, picks), 1)))
        rank_ref[...] = rank.astype(jnp.int32)

        held = jnp.zeros((token_count, count), F32)
        for j in range(picks):
            held = held + (shard[:, j : j + 1] == iota((token_count, count), 1)).astype(F32)
        held = jnp.sum(held, axis=0, keepdims=True)
        over = (jnp.max(rank, keepdims=True) >= SLOTS) | (jnp.max(held, keepdims=True) > HELD)
        flag_ref[...] = jnp.broadcast_to(over.astype(F32), flag_ref.shape)

        here = (shard == mine).astype(F32)
        local = here.astype(BF16)
        place = dot(ones(column < row), local) + dot(
            dot(jnp.ones((token_count, token_count), BF16), local).astype(BF16),
            ones(iota((picks, picks), 0) < iota((picks, picks), 1)),
        )
        place = jnp.where(here > 0, place, -1.0).astype(jnp.int32)
        index = wanted - mine * entries + 1
        owner = iota((token_count, picks), 0) // rows
        target = slot_of(owner ^ mine, count, groups) * SLOTS + rank.astype(jnp.int32) + 1
        source_high = jnp.zeros((HELD, 1), F32)
        source_low = jnp.zeros((HELD, 1), F32)
        target_high = jnp.zeros((1, HELD), F32)
        target_low = jnp.zeros((1, HELD), F32)
        for j in range(picks):
            at = ones(place[:, j : j + 1] == iota((token_count, HELD), 1))
            one = slice(j, j + 1)

            def part(value):
                return value[:, one].astype(F32).astype(BF16)

            source_high += dot_tn(at, part(index >> 7))
            source_low += dot_tn(at, part(index & 127))
            target_high += dot_tn(part(target >> 7), at)
            target_low += dot_tn(part(target & 127), at)
        source = (source_high * 128 + source_low).astype(jnp.int32) - 1
        aim = (target_high * 128 + target_low).astype(jnp.int32) - 1
        chosen[...] = ones(source == iota((HELD, entries), 1))
        layout[...] = ones(iota((2 * half, HELD), 0) == aim)

        def lay(c, carry):
            fetch(c).wait()
            found = dot(chosen[...], table[c]).astype(BF16)
            laid = dot(layout[...], found).astype(BF16)
            keep[:, columns(c, chunk)] = laid[:half]
            send[:, columns(c, chunk)] = laid[half:]
            return carry

        lax.fori_loop(0, features // chunk, lay, 0)

    return pl.pallas_call(
        kernel,
        in_specs=[SMEM, VMEM, pl.BlockSpec(memory_space=pltpu.HBM)],
        out_specs=[VMEM] * 4,
        out_shape=[
            jax.ShapeDtypeStruct(ids.shape, jnp.int32),
            jax.ShapeDtypeStruct((8, LANES), F32),
        ]
        + [jax.ShapeDtypeStruct((half, features), BF16)] * 2,
        scratch_shapes=[
            pltpu.VMEM((HELD, entries), BF16),
            pltpu.VMEM((2 * half, HELD), BF16),
            pltpu.VMEM((features // chunk, entries, chunk), BF16),
            pltpu.SemaphoreType.DMA((features // chunk,)),
        ],
        compiler_params=params(32),
        cost_estimate=cost(4 * token_count * features * entries, features * entries * 2),
        name="pick_phase",
    )(me, ids, vocab)


def token_phase(me, terms, own, gain, picked, ids, rank, logits, entries):
    rows, features = own.shape
    picks = ids.shape[1]
    span = len(picked) * SLOTS

    def kernel(me_ref, *refs):
        n, p = len(terms), len(picked)
        sources = refs[n : n + p]
        own_ref, gain_ref, ids_ref, rank_ref, logits_ref, out, table, arrived = refs[n + p :]
        mine = pl.ds(pl.multiple_of(me_ref[0] * rows, rows), rows)
        copies = [
            pltpu.make_async_copy(source, table.at[m], arrived.at[m])
            for m, source in enumerate(sources)
        ]
        for copy in copies:
            copy.start()
        total = refs[0][...].astype(F32)
        for r in refs[1:n]:
            total = total + r[...].astype(F32)
        values = (own_ref[...].astype(F32) + total).astype(BF16).astype(F32)
        inverse = lax.rsqrt(jnp.mean(values * values, axis=1, keepdims=True) + EPS)
        unit = values * inverse
        normed = (unit * gain_ref[...]).astype(BF16)
        for copy in copies:
            copy.wait()
        dense = jnp.concatenate([dot_nt(normed, table[m]) for m in range(p)], 1)
        piece = (ids_ref[mine, :] // entries >> SHARED) ^ (me_ref[0] >> SHARED)
        place = piece * SLOTS + rank_ref[mine, :]
        number = lax.broadcasted_iota(jnp.int32, (rows, span), 1)
        hits = [place[:, j : j + 1] == number for j in range(picks)]
        scores = jnp.concatenate(
            [jnp.sum(jnp.where(hit, dense, 0.0), axis=1, keepdims=True) for hit in hits], 1
        )
        log_student = scores - jnp.log(jnp.sum(jnp.exp(scores), axis=1, keepdims=True))
        weights = jnp.exp(logits_ref[mine, :])
        teacher = weights / jnp.sum(weights, axis=1, keepdims=True)
        loss = -jnp.sum(teacher * log_student, axis=1, keepdims=True)
        grad = (jnp.exp(log_student) - teacher).astype(BF16).astype(F32)
        spread = jnp.zeros((rows, span), F32)
        for j in range(picks):
            spread = jnp.where(hits[j], grad[:, j : j + 1], spread)
        spread = spread.astype(BF16)
        upstream = dot(spread[:, :SLOTS], table[0])
        for m in range(1, p):
            upstream = upstream + dot(spread[:, m * SLOTS : (m + 1) * SLOTS], table[m])
        scaled = upstream * gain_ref[...]
        out[:, :features] = (
            inverse * (scaled - unit * jnp.mean(scaled * unit, axis=1, keepdims=True))
        ).astype(BF16)
        out[:, features:] = split_loss(loss).astype(BF16)

    return pl.pallas_call(
        kernel,
        in_specs=[SMEM] + [VMEM] * len(terms) + [UNREAD] * len(picked) + [VMEM] * 5,
        scratch_shapes=[
            pltpu.VMEM((len(picked), SLOTS, features), BF16),
            pltpu.SemaphoreType.DMA((len(picked),)),
        ],
        out_shape=jax.ShapeDtypeStruct((rows, features + LANES), BF16),
        compiler_params=params(),
        name="token_phase",
    )(me, *terms, *picked, own, gain, ids, rank, logits)


def mixed_grad_phase(me, pattern, grad, down, scale, partner, rows, groups, local):
    token_count = grad.shape[0]
    hidden, features = down.shape
    levels, blocks = pattern.shape
    width = partner.shape[-1]
    crossing = levels - local
    pair = 2 if blocks % 2 == 0 else 1

    def kernel(me_ref, pat, grad_ref, down_ref, sc, part_ref, loss, mixed_grad, *refs):
        outgoing, (factors, result, table, arrived) = refs[:crossing], refs[crossing:]

        def fetch(i):
            return pltpu.make_async_copy(
                down_ref.at[columns(i, pair * width), :], table.at[i], arrived.at[i]
            )

        for i in range(blocks // pair):
            fetch(i).start()
        factors[...] = spread_factors(sc[...], width, 0, features).astype(F32)
        order = row_order(me_ref[0], token_count, rows, groups, True)
        each = jnp.sum(grad_ref[:, features:].astype(F32), axis=1, keepdims=True)
        loss[...] = jnp.sum(each, axis=0, keepdims=True) / token_count

        def step(i, carry):
            fetch(i).wait()
            weight = jnp.concatenate(
                [
                    table[i, b * width : (b + 1) * width, :]
                    * factors[pl.ds(i * pair + b, 1), :].astype(BF16)
                    for b in range(pair)
                ],
                0,
            )
            result[:, columns(i, pair * width)] = dot_nt(grad_ref[:, :features], weight).astype(BF16)
            return carry

        lax.fori_loop(0, blocks // pair, step, 0, unroll=2)
        mixed_grad[...] = dot(order, result[...]).astype(BF16)
        for h in range(blocks):
            here = slice(h * width, (h + 1) * width)
            weights = jnp.concatenate(
                [part_ref[k, h] * pat[k, h].astype(F32).astype(BF16) for k in range(local, levels)], 0
            )
            terms = dot_nt(mixed_grad[:, here], weights).astype(BF16)
            for n in range(crossing):
                outgoing[n][:, here] = terms[:, n * width : (n + 1) * width]

    return pl.pallas_call(
        kernel,
        in_specs=[SMEM, SMEM, VMEM, HBM, VMEM, VMEM],
        out_specs=[VMEM] * (2 + crossing),
        out_shape=[jax.ShapeDtypeStruct((1, 1), F32)]
        + [jax.ShapeDtypeStruct((token_count, hidden), BF16)] * (1 + crossing),
        scratch_shapes=[
            pltpu.VMEM((blocks, features), F32),
            pltpu.VMEM((token_count, hidden), BF16),
            pltpu.VMEM((blocks // pair, pair * width, features), BF16),
            pltpu.SemaphoreType.DMA((blocks // pair,)),
        ],
        compiler_params=params(52),
        cost_estimate=cost(2 * token_count * features * hidden, features * hidden * 2),
        name="mixed_grad_phase",
    )(me, pattern, grad, down, scale, partner)


def block_grad_phase(pattern, act, received, mixed_grad, diag, partner):
    token_count, hidden = act.shape
    levels, blocks = pattern.shape
    width = diag.shape[-1]
    crossing = len(received)
    local = levels - crossing

    def kernel(pat, act_ref, mg, *refs):
        recv = refs[:crossing]
        diag_ref, part_ref, grad_diag, grad_part, act_grad = refs[crossing:]
        h = pl.program_id(0)

        grad = mg[:, columns(h, width)]
        grad_diag[0] = dot_tn(act_ref[:, columns(h, width)], grad)
        total = dot_nt(grad, diag_ref[h])
        for k in range(levels):
            keeps = pat[k, h].astype(F32)
            if k < local:
                other = h ^ (1 << k)
                source = act_ref[:, columns(other, width)]
                kept = pat[k, other].astype(F32).astype(BF16)
                total = total + dot_nt(mg[:, columns(other, width)], part_ref[k, other] * kept)
            else:
                source = recv[k - local][:, columns(h, width)]
            grad_part[k, 0] = dot_tn(source, grad) * keeps
        act_grad[...] = total

    return pl.pallas_call(
        kernel,
        grid=(blocks,),
        in_specs=[SMEM]
        + [whole((token_count, hidden))] * (2 + crossing)
        + [whole(diag.shape), whole(partner.shape)],
        out_specs=[
            pl.BlockSpec((1, width, width), lambda i: (i, 0, 0)),
            pl.BlockSpec((levels, 1, width, width), lambda i: (0, i, 0, 0)),
            pl.BlockSpec((token_count, width), lambda i: (0, i)),
        ],
        out_shape=[
            jax.ShapeDtypeStruct(diag.shape, F32),
            jax.ShapeDtypeStruct(partner.shape, F32),
            jax.ShapeDtypeStruct((token_count, hidden), F32),
        ],
        compiler_params=params(),
        cost_estimate=cost(2 * token_count * hidden * width * 12, 12 << 20),
        name="block_grad_phase",
    )(pattern, act, mixed_grad, *received, diag, partner)


def down_grad_phase(mixed, grad, features):
    token_count, hidden = mixed.shape
    chunk = min(512, features)
    steps = features // chunk

    def kernel(mixed_ref, grad_ref, out, turned, table, left):
        def store(c):
            return pltpu.make_async_copy(table.at[c], out.at[:, columns(c, chunk)], left.at[c])

        turned[...] = mixed_ref[...].T

        def step(c, carry):
            table[c] = dot(turned[...], grad_ref[:, columns(c, chunk)])
            store(c).start()
            return carry

        lax.fori_loop(0, steps, step, 0)
        for c in range(steps):
            store(c).wait()

    return pl.pallas_call(
        kernel,
        in_specs=[VMEM] * 2,
        out_specs=HBM,
        out_shape=jax.ShapeDtypeStruct((hidden, features), F32),
        scratch_shapes=[
            pltpu.VMEM((hidden, token_count), BF16),
            pltpu.VMEM((steps, hidden, chunk), F32),
            pltpu.SemaphoreType.DMA((steps,)),
        ],
        compiler_params=params(28),
        cost_estimate=cost(2 * token_count * features * hidden, features * hidden * 4),
        name="down_grad_phase",
    )(mixed, grad)


def up_grad_phase(tokens, pre, act_grad, received):
    token_count, depth = tokens.shape
    hidden = pre.shape[1]
    chunk = min(512, depth)
    steps = depth // chunk

    def kernel(tok, pre_ref, grad_ref, *refs):
        recv, (out, pre_grad, table, left) = refs[: len(received)], refs[len(received) :]

        def store(i):
            return pltpu.make_async_copy(table.at[i], out.at[columns(i, chunk), :], left.at[i])

        total = grad_ref[...]
        for r in recv:
            total = total + r[...].astype(F32)
        value = pre_ref[...]
        gate = jax.nn.sigmoid(value)
        pre_grad[...] = (total * (gate * (1.0 + value * (1.0 - gate)))).astype(BF16)

        def step(i, carry):
            table[i] = dot_tn(tok[:, columns(i, chunk)], pre_grad[...])
            store(i).start()
            return carry

        lax.fori_loop(0, steps, step, 0)
        for i in range(steps):
            store(i).wait()

    return pl.pallas_call(
        kernel,
        in_specs=[VMEM] * (3 + len(received)),
        out_specs=HBM,
        out_shape=jax.ShapeDtypeStruct((depth, hidden), F32),
        scratch_shapes=[
            pltpu.VMEM((token_count, hidden), BF16),
            pltpu.VMEM((steps, chunk, hidden), F32),
            pltpu.SemaphoreType.DMA((steps,)),
        ],
        compiler_params=params(28),
        cost_estimate=cost(2 * token_count * depth * hidden, depth * hidden * 4),
        name="up_grad_phase",
    )(tokens, pre, act_grad, *received)


def on_device(
    tokens,
    up_values,
    up_scale,
    diag_blocks,
    partner_blocks,
    pattern,
    down_values,
    down_scale,
    norm_gain,
    vocab_table,
    teacher_ids,
    teacher_logits,
):
    width = diag_blocks.shape[-1]
    token_count = tokens.shape[0]
    blocks = diag_blocks.shape[0]
    levels = partner_blocks.shape[0]
    local = blocks.bit_length() - 1
    count = lax.axis_size("mp")
    bits = count.bit_length() - 1
    groups = bit_groups(bits)
    rows = token_count // count
    me = lax.axis_index("mp").astype(jnp.int32).reshape(1)
    gain = norm_gain.reshape(1, -1)
    own = lax.dynamic_slice_in_dim(tokens, me[0] * rows, rows, 0)

    sparse = groups[:SHARED] == [[b] for b in range(SHARED)] and len(groups) == SHARED + 1
    if sparse:
        rank, flag, kept, sent = pick_phase(me, teacher_ids, vocab_table, rows, groups)
        pre, act = up_phase(tokens, up_values, up_scale, width, [flag])
        received = [swap(act, 1 << k - local) for k in range(local, levels)]
        own_mix = own_mix_phase(pattern, act, diag_blocks, partner_blocks, local, ())
        kept, sent = add_phase(kept, swap(sent, group_masks(groups[0])[1]), 2, [own_mix, *received[1:2]])
        parts = lax.axis_size("groups")
        turned = flag
        for _ in range(parts - 1):
            turned = lax.ppermute(turned, "groups", [(i, (i + 1) % parts) for i in range(parts)])
            flag = flag + turned
        crowded = flag[0, 0] > 0
        laid = swap(sent, group_masks(groups[1])[1])
    else:
        pre, act = up_phase(tokens, up_values, up_scale, width, [])
        received = [swap(act, 1 << k - local) for k in range(local, levels)]
        own_mix = own_mix_phase(pattern, act, diag_blocks, partner_blocks, local, ())
    mixed, keep, send = mix_phase(
        me, pattern, own_mix, received, partner_blocks, down_values, down_scale, rows, groups, []
    )
    if sparse:
        masks = group_masks(groups[SHARED])
        pieces = add_phase(kept, laid, len(masks), [])
        picked = [swap(piece, m) for piece, m in zip(pieces, masks)]
        terms = reduce_rows(keep, send, groups, [pieces[1:], picked[1:]])
    else:
        terms = reduce_rows(keep, send, groups)

    def dense_tokens(*terms):
        stream, normed = norm_phase(terms, own, gain)
        normed = gather_rows(normed, groups)
        scores = score_phase(me, normed, vocab_table, teacher_ids, rows, groups)
        for b in range(bits):
            scores = scores + swap(scores, 1 << b)
        loss, keep, send = loss_phase(
            me, scores, teacher_logits, teacher_ids, vocab_table, rows, groups
        )
        return norm_back_phase(reduce_rows(keep, send, groups), stream, gain, loss)

    if sparse:
        grad = token_phase(
            me, terms, own, gain, picked, teacher_ids, rank, teacher_logits, vocab_table.shape[0]
        )
        grad = lax.cond(crowded, lambda grad, *terms: dense_tokens(*terms), lambda grad, *terms: grad, grad, *terms)
    else:
        grad = dense_tokens(*terms)
    grad = gather_rows(grad, groups)
    loss, mixed_grad, *outgoing = mixed_grad_phase(
        me, pattern, grad, down_values, down_scale, partner_blocks, rows, groups, local
    )
    incoming = [swap(block, 1 << n) for n, block in enumerate(outgoing)]
    grad_diag, grad_partner, act_grad = block_grad_phase(
        pattern, act, received, mixed_grad, diag_blocks, partner_blocks
    )
    grad_down = down_grad_phase(mixed, grad, down_values.shape[1])
    grad_up = up_grad_phase(tokens, pre, act_grad, incoming)
    return (loss.reshape(1), grad_up, grad_down, grad_diag, grad_partner)


def solution(mesh):
    return jax.shard_map(
        on_device,
        mesh=mesh,
        in_specs=(
            P("groups", None),
            P(None, "mp"),
            P(None, "mp"),
            P("mp", None, None),
            P(None, "mp", None, None),
            P(None, "mp"),
            P("mp", None),
            P("mp", None),
            P(),
            P("mp", None),
            P("groups", None),
            P("groups", None),
        ),
        out_specs=(
            P("groups"),
            P("groups", "mp"),
            P(("groups", "mp"), None),
            P(("groups", "mp"), None, None),
            P("groups", "mp", None, None),
        ),
        check_vma=False,
    )
```

```python
import functools

import jax
import jax.numpy as jnp
from jax import lax
from jax.experimental import pallas as pl
from jax.experimental.pallas import tpu as pltpu
from jax.sharding import PartitionSpec as P

F32, BF16 = jnp.float32, jnp.bfloat16
EPS = 1e-05
LANES = 128
SHARED = 2
SLOTS = 32
HELD = 128


def bit_groups(bits):
    if bits == 4:
        return [[0], [1], [2, 3]]
    return [[b] for b in range(bits)]


def group_masks(group):
    return [sum(1 << b for i, b in enumerate(group) if j >> i & 1) for j in range(1 << len(group))]


def swap(block, mask):
    if mask == 0:
        return block
    count = lax.axis_size("mp")
    return lax.ppermute(block, "mp", [(i, i ^ mask) for i in range(count)])


def reduce_rows(keep, send, groups, after=None):
    for n, group in enumerate(groups):
        masks = group_masks(group)
        if n == len(groups) - 1:
            return [keep] + [swap(s, m) for s, m in zip(send, masks[1:])]
        total = swap(send if n == 0 else send[0], masks[1])
        parts = 1 << len(groups[n + 1])
        keep, *send = add_phase(keep, total, parts, after[n] if after else [])


def gather_rows(rows, groups):
    for group in reversed(groups):
        masks = group_masks(group)
        rows = jnp.concatenate([rows] + [swap(rows, m) for m in masks[1:]], 0)
    return rows


def row_order(me, tokens, rows, groups, transposed):
    rel = lax.broadcasted_iota(jnp.int32, (tokens, tokens), 1 if transposed else 0)
    whole = lax.broadcasted_iota(jnp.int32, (tokens, tokens), 0 if transposed else 1)
    slot = rel // rows
    mask = jnp.zeros_like(slot)
    place = tokens // rows
    for group in groups:
        place >>= len(group)
        part = slot // place
        for i, b in enumerate(group):
            mask = mask | ((part >> i & 1) << b)
    source = ((me ^ mask) * rows) + rel % rows
    return (source == whole).astype(F32).astype(BF16)


def dot(a, b):
    return jnp.dot(a, b, preferred_element_type=F32)


def dot_nt(a, b):
    return lax.dot_general(a, b, (((1,), (1,)), ((), ())), preferred_element_type=F32)


def dot_tn(a, b):
    return lax.dot_general(a, b, (((0,), (0,)), ((), ())), preferred_element_type=F32)


def spread_factors(scale, width, first, count):
    blocks = scale.shape[1]
    column = lax.broadcasted_iota(jnp.int32, (blocks, count), 1) // width + first
    row = lax.broadcasted_iota(jnp.int32, (blocks, count), 0)
    pick = (column == row).astype(F32).astype(BF16)
    return dot(jnp.exp2(scale.astype(F32)).astype(BF16), pick).astype(BF16)


def params(mebibytes=16):
    return pltpu.CompilerParams(vmem_limit_bytes=mebibytes << 20)


def whole(shape):
    return pl.BlockSpec(shape, lambda i: (0,) * len(shape))


SMEM = pl.BlockSpec(memory_space=pltpu.SMEM)
UNREAD = pl.BlockSpec(memory_space=pl.ANY)
VMEM = pl.BlockSpec(memory_space=pltpu.VMEM)
HBM = pl.BlockSpec(memory_space=pltpu.HBM)


def columns(index, width):
    return pl.ds(pl.multiple_of(index * width, width), width)


def cost(flops, nbytes):
    return pl.CostEstimate(flops=int(flops), bytes_accessed=int(nbytes), transcendentals=0)


def up_phase(tokens, values, scale, width, after):
    token_count, depth = tokens.shape
    hidden = values.shape[1]
    chunk = min(512, depth)
    blocks = chunk // width
    steps = depth // chunk

    def kernel(tok, val, sc, *refs):
        pre, act, factors, table, arrived = refs[len(after) :]

        def fetch(i):
            return pltpu.make_async_copy(val.at[columns(i, chunk), :], table.at[i], arrived.at[i])

        for i in range(steps):
            fetch(i).start()
        factors[...] = spread_factors(sc[...], width, 0, hidden).astype(F32)

        def step(i, carry):
            fetch(i).wait()
            weight = jnp.concatenate(
                [
                    table[i, b * width : (b + 1) * width, :]
                    * factors[pl.ds(i * blocks + b, 1), :].astype(BF16)
                    for b in range(blocks)
                ],
                0,
            )
            part = dot(tok[:, columns(i, chunk)], weight)
            pre[...] = jnp.where(i == 0, part, pre[...] + part)
            return carry

        lax.fori_loop(0, steps, step, 0)
        total = pre[...]
        act[...] = (total * jax.nn.sigmoid(total)).astype(BF16)

    return pl.pallas_call(
        kernel,
        in_specs=[VMEM, HBM, VMEM] + [UNREAD] * len(after),
        out_specs=[VMEM] * 2,
        out_shape=[
            jax.ShapeDtypeStruct((token_count, hidden), F32),
            jax.ShapeDtypeStruct((token_count, hidden), BF16),
        ],
        scratch_shapes=[
            pltpu.VMEM((depth // width, hidden), F32),
            pltpu.VMEM((steps, chunk, hidden), BF16),
            pltpu.SemaphoreType.DMA((steps,)),
        ],
        compiler_params=params(52),
        cost_estimate=cost(2 * token_count * depth * hidden, depth * hidden * 2),
        name="up_phase",
    )(tokens, values, scale, *after)


def own_mix_phase(pattern, act, diag, partner, local, after):
    token_count, hidden = act.shape
    width = diag.shape[-1]
    levels, blocks = pattern.shape

    def kernel(pat, act_ref, diag_ref, part_ref, *refs):
        out = refs[-1]

        def mix(h):
            source = [act_ref[:, columns(h, width)]]
            weight = [diag_ref[h]]
            for k in range(local):
                source.append(act_ref[:, columns(h ^ (1 << k), width)])
                weight.append(part_ref[k, h] * pat[k, h].astype(F32).astype(BF16))
            out[:, columns(h, width)] = dot(
                jnp.concatenate(source, 1), jnp.concatenate(weight, 0)
            )

        for h in range(blocks):
            mix(h)

    return pl.pallas_call(
        kernel,
        in_specs=[SMEM] + [VMEM] * 3 + [UNREAD] * len(after),
        out_specs=VMEM,
        out_shape=jax.ShapeDtypeStruct((token_count, hidden), F32),
        compiler_params=params(),
        cost_estimate=cost(2 * token_count * hidden * width * 4, 4 << 20),
        name="own_mix_phase",
    )(pattern, act, diag, partner, *after)


def mix_phase(me, pattern, own, received, partner, down, scale, rows, groups, after):
    token_count, hidden = own.shape
    width = partner.shape[-1]
    levels, blocks = pattern.shape
    features = down.shape[1]
    chunk = min(512, features)
    steps = features // chunk
    crossing = len(received)
    local = levels - crossing
    half = token_count // 2

    def kernel(me_ref, pat, own_ref, *refs):
        recv = refs[:crossing]
        part_ref, down_ref, sc = refs[crossing : crossing + 3]
        mixed, keep, send, factors, table, arrived = refs[-6:]

        def fetch(c):
            return pltpu.make_async_copy(
                down_ref.at[:, columns(c, chunk)], table.at[c], arrived.at[c]
            )

        for c in range(steps):
            fetch(c).start()
        factors[...] = spread_factors(sc[...], width, 0, features).astype(F32)
        order = row_order(me_ref[0], token_count, rows, groups, False)

        def mix(h):
            here = columns(h, width)
            source = jnp.concatenate([r[:, here] for r in recv], 1)
            weight = jnp.concatenate(
                [
                    part_ref[k, h] * pat[k, h].astype(F32).astype(BF16)
                    for k in range(local, levels)
                ],
                0,
            )
            total = own_ref[:, here] + dot(source, weight)
            mixed[:, here] = dot(order, total.astype(BF16)).astype(BF16)

        for h in range(blocks):
            mix(h)

        def project(c, carry):
            fetch(c).wait()
            weight = jnp.concatenate(
                [
                    table[c, h * width : (h + 1) * width, :]
                    * factors[h : h + 1, columns(c, chunk)].astype(BF16)
                    for h in range(blocks)
                ],
                0,
            )
            result = dot(mixed[...], weight).astype(BF16)
            keep[:, columns(c, chunk)] = result[:half]
            send[:, columns(c, chunk)] = result[half:]
            return carry

        lax.fori_loop(0, steps, project, 0)

    return pl.pallas_call(
        kernel,
        in_specs=[SMEM, SMEM] + [VMEM] * (2 + crossing) + [HBM, VMEM] + [UNREAD] * len(after),
        out_specs=[VMEM] * 3,
        out_shape=[jax.ShapeDtypeStruct((token_count, hidden), BF16)]
        + [jax.ShapeDtypeStruct((half, features), BF16)] * 2,
        scratch_shapes=[
            pltpu.VMEM((blocks, features), F32),
            pltpu.VMEM((steps, hidden, chunk), BF16),
            pltpu.SemaphoreType.DMA((steps,)),
        ],
        compiler_params=params(52),
        cost_estimate=cost(2 * token_count * features * hidden, features * hidden * 2),
        name="mix_phase",
    )(me, pattern, own, *received, partner, down, scale, *after)


def add_phase(keep, received, parts, after):
    rows, features = keep.shape
    rows //= parts

    def kernel(a, b, *refs):
        outs = refs[len(after) :]
        for n, out in enumerate(outs):
            here = slice(n * rows, (n + 1) * rows)
            out[...] = (a[here, :].astype(F32) + b[here, :].astype(F32)).astype(BF16)

    return pl.pallas_call(
        kernel,
        in_specs=[VMEM] * 2 + [UNREAD] * len(after),
        out_specs=[VMEM] * parts,
        out_shape=[jax.ShapeDtypeStruct((rows, features), BF16)] * parts,
        compiler_params=params(),
        name="add_phase",
    )(keep, received, *after)


def norm_phase(terms, own, gain):
    rows, features = own.shape

    def kernel(*refs):
        n = len(terms)
        own_ref, gain_ref, stream_ref, normed_ref = refs[n:]
        total = refs[0][...].astype(F32)
        for r in refs[1:n]:
            total = total + r[...].astype(F32)
        stream = (own_ref[...].astype(F32) + total).astype(BF16)
        values = stream.astype(F32)
        inverse = lax.rsqrt(jnp.mean(values * values, axis=1, keepdims=True) + EPS)
        stream_ref[...] = stream
        normed_ref[...] = (values * inverse * gain_ref[...]).astype(BF16)

    return pl.pallas_call(
        kernel,
        out_shape=[jax.ShapeDtypeStruct((rows, features), BF16)] * 2,
        compiler_params=params(),
        name="norm_phase",
    )(*terms, own, gain)


def score_phase(me, normed, vocab, ids, rows, groups):
    token_count, features = normed.shape
    entries = vocab.shape[0]
    picks = ids.shape[1]
    chunk = min(256, entries)

    def kernel(me_ref, normed_ref, vocab_ref, ids_ref, out, ordered):
        i = pl.program_id(0)

        @pl.when(i == 0)
        def _():
            order = row_order(me_ref[0], token_count, rows, groups, True)
            ordered[...] = dot(order, normed_ref[...]).astype(BF16)
            out[...] = jnp.zeros_like(out)

        scores = dot_nt(ordered[...], vocab_ref[...])
        offset = ids_ref[...] - (me_ref[0] * entries + i * chunk)
        number = lax.broadcasted_iota(jnp.int32, (token_count, chunk), 1)
        picked = [
            jnp.sum(jnp.where(offset[:, j : j + 1] == number, scores, 0.0), axis=1, keepdims=True)
            for j in range(picks)
        ]
        out[...] += jnp.concatenate(picked, 1)

    return pl.pallas_call(
        kernel,
        grid=(entries // chunk,),
        in_specs=[
            SMEM,
            whole((token_count, features)),
            pl.BlockSpec((chunk, features), lambda i: (i, 0)),
            whole(ids.shape),
        ],
        out_specs=whole((token_count, picks)),
        out_shape=jax.ShapeDtypeStruct((token_count, picks), F32),
        scratch_shapes=[pltpu.VMEM((token_count, features), BF16)],
        compiler_params=params(24),
        cost_estimate=cost(2 * token_count * features * entries, features * entries * 2),
        name="score_phase",
    )(me, normed, vocab, ids)


def loss_phase(me, scores, logits, ids, vocab, rows, groups):
    token_count, picks = scores.shape
    entries, features = vocab.shape
    chunk = min(512, features)
    half = token_count // 2

    def kernel(me_ref, scores_ref, logits_ref, ids_ref, vocab_ref, loss, keep, send, spread):
        i = pl.program_id(0)

        @pl.when(i == 0)
        def _():
            values = scores_ref[...]
            log_student = values - jnp.log(jnp.sum(jnp.exp(values), axis=1, keepdims=True))
            weights = jnp.exp(logits_ref[...])
            teacher = weights / jnp.sum(weights, axis=1, keepdims=True)
            each = jnp.sum(teacher * log_student, axis=1, keepdims=True)
            loss[...] = -jnp.sum(each, axis=0, keepdims=True) / token_count
            grad = (jnp.exp(log_student) - teacher).astype(BF16).astype(F32)
            offset = ids_ref[...] - me_ref[0] * entries
            number = lax.broadcasted_iota(jnp.int32, (token_count, entries), 1)
            total = jnp.zeros((token_count, entries), F32)
            for j in range(picks):
                total = jnp.where(offset[:, j : j + 1] == number, grad[:, j : j + 1], total)
            order = row_order(me_ref[0], token_count, rows, groups, False)
            spread[...] = dot(order, total.astype(BF16)).astype(BF16)

        result = dot(spread[...], vocab_ref[...]).astype(BF16)
        keep[...] = result[:half]
        send[...] = result[half:]

    return pl.pallas_call(
        kernel,
        grid=(features // chunk,),
        in_specs=[
            SMEM,
            whole(scores.shape),
            whole(logits.shape),
            whole(ids.shape),
            pl.BlockSpec((entries, chunk), lambda i: (0, i)),
        ],
        out_specs=[whole((1, 1))] + [pl.BlockSpec((half, chunk), lambda i: (0, i))] * 2,
        out_shape=[jax.ShapeDtypeStruct((1, 1), F32)]
        + [jax.ShapeDtypeStruct((half, features), BF16)] * 2,
        scratch_shapes=[pltpu.VMEM((token_count, entries), BF16)],
        compiler_params=params(24),
        cost_estimate=cost(2 * token_count * features * entries, features * entries * 2),
        name="loss_phase",
    )(me, scores, logits, ids, vocab)


def split_loss(loss):
    lane = lax.broadcasted_iota(jnp.int32, (loss.shape[0], LANES), 1)
    high = loss.astype(BF16).astype(F32)
    middle = (loss - high).astype(BF16).astype(F32)
    low = loss - high - middle
    return jnp.where(lane == 0, high, jnp.where(lane == 1, middle, jnp.where(lane == 2, low, 0.0)))


def norm_back_phase(terms, stream, gain, loss):
    rows, features = stream.shape

    def kernel(*refs):
        n = len(terms)
        stream_ref, gain_ref, loss_ref, out = refs[n:]
        upstream = refs[0][...].astype(F32)
        for r in refs[1:n]:
            upstream = upstream + r[...].astype(F32)
        values = stream_ref[...].astype(F32)
        inverse = lax.rsqrt(jnp.mean(values * values, axis=1, keepdims=True) + EPS)
        unit = values * inverse
        scaled = upstream * gain_ref[...]
        out[:, :features] = (
            inverse * (scaled - unit * jnp.mean(scaled * unit, axis=1, keepdims=True))
        ).astype(BF16)
        out[:, features:] = split_loss(jnp.broadcast_to(loss_ref[...], (rows, 1))).astype(BF16)

    return pl.pallas_call(
        kernel,
        out_shape=jax.ShapeDtypeStruct((rows, features + LANES), BF16),
        compiler_params=params(),
        name="norm_back_phase",
    )(*terms, stream, gain, loss)


def slot_of(index, count, groups):
    slot = jnp.zeros_like(index)
    place = count
    for group in groups:
        place >>= len(group)
        for i, b in enumerate(group):
            slot = slot | ((index >> b & 1) << i) * place
    return slot


def pick_phase(me, ids, vocab, rows, groups):
    token_count, picks = ids.shape
    entries, features = vocab.shape
    count = token_count // rows
    sharers = count >> SHARED
    chunk = min(512, features)
    half = count * SLOTS // 2
    wide = picks * sharers

    def ones(mask):
        return mask.astype(F32).astype(BF16)

    def iota(shape, axis):
        return lax.broadcasted_iota(jnp.int32, shape, axis)

    def kernel(me_ref, ids_ref, vocab_ref, rank_ref, flag_ref, keep, send, chosen, layout, table, arrived):
        def fetch(c):
            return pltpu.make_async_copy(
                vocab_ref.at[:, columns(c, chunk)], table.at[c], arrived.at[c]
            )

        for c in range(features // chunk):
            fetch(c).start()

        mine = me_ref[0]
        wanted = ids_ref[...]
        shard = wanted // entries
        lane = iota((token_count, wide), 1)
        sharer = jnp.full((token_count, wide), -1, jnp.int32)
        for j in range(picks):
            sharer = jnp.where(lane // sharers == j, shard[:, j : j + 1] >> SHARED, sharer)
        asks = (sharer == lane % sharers).astype(F32)
        row, column = iota((token_count, token_count), 0), iota((token_count, token_count), 1)
        together = row // rows == column // rows
        earlier = dot(ones(together & (column < row)), asks.astype(BF16))
        total = dot(ones(together), asks.astype(BF16)).astype(BF16)
        a, b = iota((wide, wide), 0), iota((wide, wide), 1)
        before = dot(total, ones((a % sharers == b % sharers) & (a // sharers < b // sharers)))
        gathered = (asks * (earlier + before)).astype(BF16)
        rank = dot(gathered, ones(iota((wide, picks), 0) // sharers == iota((wide, picks), 1)))
        rank_ref[...] = rank.astype(jnp.int32)

        held = jnp.zeros((token_count, count), F32)
        for j in range(picks):
            held = held + (shard[:, j : j + 1] == iota((token_count, count), 1)).astype(F32)
        held = jnp.sum(held, axis=0, keepdims=True)
        over = (jnp.max(rank, keepdims=True) >= SLOTS) | (jnp.max(held, keepdims=True) > HELD)
        flag_ref[...] = jnp.broadcast_to(over.astype(F32), flag_ref.shape)

        here = (shard == mine).astype(F32)
        local = here.astype(BF16)
        place = dot(ones(column < row), local) + dot(
            dot(jnp.ones((token_count, token_count), BF16), local).astype(BF16),
            ones(iota((picks, picks), 0) < iota((picks, picks), 1)),
        )
        place = jnp.where(here > 0, place, -1.0).astype(jnp.int32)
        index = wanted - mine * entries + 1
        owner = iota((token_count, picks), 0) // rows
        target = slot_of(owner ^ mine, count, groups) * SLOTS + rank.astype(jnp.int32) + 1
        source_high = jnp.zeros((HELD, 1), F32)
        source_low = jnp.zeros((HELD, 1), F32)
        target_high = jnp.zeros((1, HELD), F32)
        target_low = jnp.zeros((1, HELD), F32)
        for j in range(picks):
            at = ones(place[:, j : j + 1] == iota((token_count, HELD), 1))
            one = slice(j, j + 1)

            def part(value):
                return value[:, one].astype(F32).astype(BF16)

            source_high += dot_tn(at, part(index >> 7))
            source_low += dot_tn(at, part(index & 127))
            target_high += dot_tn(part(target >> 7), at)
            target_low += dot_tn(part(target & 127), at)
        source = (source_high * 128 + source_low).astype(jnp.int32) - 1
        aim = (target_high * 128 + target_low).astype(jnp.int32) - 1
        chosen[...] = ones(source == iota((HELD, entries), 1))
        layout[...] = ones(iota((2 * half, HELD), 0) == aim)

        def lay(c, carry):
            fetch(c).wait()
            found = dot(chosen[...], table[c]).astype(BF16)
            laid = dot(layout[...], found).astype(BF16)
            keep[:, columns(c, chunk)] = laid[:half]
            send[:, columns(c, chunk)] = laid[half:]
            return carry

        lax.fori_loop(0, features // chunk, lay, 0)

    return pl.pallas_call(
        kernel,
        in_specs=[SMEM, VMEM, pl.BlockSpec(memory_space=pltpu.HBM)],
        out_specs=[VMEM] * 4,
        out_shape=[
            jax.ShapeDtypeStruct(ids.shape, jnp.int32),
            jax.ShapeDtypeStruct((8, LANES), F32),
        ]
        + [jax.ShapeDtypeStruct((half, features), BF16)] * 2,
        scratch_shapes=[
            pltpu.VMEM((HELD, entries), BF16),
            pltpu.VMEM((2 * half, HELD), BF16),
            pltpu.VMEM((features // chunk, entries, chunk), BF16),
            pltpu.SemaphoreType.DMA((features // chunk,)),
        ],
        compiler_params=params(32),
        cost_estimate=cost(4 * token_count * features * entries, features * entries * 2),
        name="pick_phase",
    )(me, ids, vocab)


def token_phase(me, terms, own, gain, picked, ids, rank, logits, entries):
    rows, features = own.shape
    picks = ids.shape[1]
    span = len(picked) * SLOTS

    def kernel(me_ref, *refs):
        n, p = len(terms), len(picked)
        sources = refs[n : n + p]
        own_ref, gain_ref, ids_ref, rank_ref, logits_ref, out, table, arrived = refs[n + p :]
        mine = pl.ds(pl.multiple_of(me_ref[0] * rows, rows), rows)
        copies = [
            pltpu.make_async_copy(source, table.at[m], arrived.at[m])
            for m, source in enumerate(sources)
        ]
        for copy in copies:
            copy.start()
        total = refs[0][...].astype(F32)
        for r in refs[1:n]:
            total = total + r[...].astype(F32)
        values = (own_ref[...].astype(F32) + total).astype(BF16).astype(F32)
        inverse = lax.rsqrt(jnp.mean(values * values, axis=1, keepdims=True) + EPS)
        unit = values * inverse
        normed = (unit * gain_ref[...]).astype(BF16)
        for copy in copies:
            copy.wait()
        dense = jnp.concatenate([dot_nt(normed, table[m]) for m in range(p)], 1)
        piece = (ids_ref[mine, :] // entries >> SHARED) ^ (me_ref[0] >> SHARED)
        place = piece * SLOTS + rank_ref[mine, :]
        number = lax.broadcasted_iota(jnp.int32, (rows, span), 1)
        hits = [place[:, j : j + 1] == number for j in range(picks)]
        scores = jnp.concatenate(
            [jnp.sum(jnp.where(hit, dense, 0.0), axis=1, keepdims=True) for hit in hits], 1
        )
        log_student = scores - jnp.log(jnp.sum(jnp.exp(scores), axis=1, keepdims=True))
        weights = jnp.exp(logits_ref[mine, :])
        teacher = weights / jnp.sum(weights, axis=1, keepdims=True)
        loss = -jnp.sum(teacher * log_student, axis=1, keepdims=True)
        grad = (jnp.exp(log_student) - teacher).astype(BF16).astype(F32)
        spread = jnp.zeros((rows, span), F32)
        for j in range(picks):
            spread = jnp.where(hits[j], grad[:, j : j + 1], spread)
        spread = spread.astype(BF16)
        upstream = dot(spread[:, :SLOTS], table[0])
        for m in range(1, p):
            upstream = upstream + dot(spread[:, m * SLOTS : (m + 1) * SLOTS], table[m])
        scaled = upstream * gain_ref[...]
        out[:, :features] = (
            inverse * (scaled - unit * jnp.mean(scaled * unit, axis=1, keepdims=True))
        ).astype(BF16)
        out[:, features:] = split_loss(loss).astype(BF16)

    return pl.pallas_call(
        kernel,
        in_specs=[SMEM] + [VMEM] * len(terms) + [UNREAD] * len(picked) + [VMEM] * 5,
        scratch_shapes=[
            pltpu.VMEM((len(picked), SLOTS, features), BF16),
            pltpu.SemaphoreType.DMA((len(picked),)),
        ],
        out_shape=jax.ShapeDtypeStruct((rows, features + LANES), BF16),
        compiler_params=params(),
        name="token_phase",
    )(me, *terms, *picked, own, gain, ids, rank, logits)


def mixed_grad_phase(me, pattern, grad, down, scale, partner, rows, groups, local):
    token_count = grad.shape[0]
    hidden, features = down.shape
    levels, blocks = pattern.shape
    width = partner.shape[-1]
    crossing = levels - local
    pair = 2 if blocks % 2 == 0 else 1

    def kernel(me_ref, pat, grad_ref, down_ref, sc, part_ref, loss, mixed_grad, *refs):
        outgoing, (factors, result, table, arrived) = refs[:crossing], refs[crossing:]

        def fetch(i):
            return pltpu.make_async_copy(
                down_ref.at[columns(i, pair * width), :], table.at[i], arrived.at[i]
            )

        for i in range(blocks // pair):
            fetch(i).start()
        factors[...] = spread_factors(sc[...], width, 0, features).astype(F32)
        order = row_order(me_ref[0], token_count, rows, groups, True)
        each = jnp.sum(grad_ref[:, features:].astype(F32), axis=1, keepdims=True)
        loss[...] = jnp.sum(each, axis=0, keepdims=True) / token_count

        def step(i, carry):
            fetch(i).wait()
            weight = jnp.concatenate(
                [
                    table[i, b * width : (b + 1) * width, :]
                    * factors[pl.ds(i * pair + b, 1), :].astype(BF16)
                    for b in range(pair)
                ],
                0,
            )
            result[:, columns(i, pair * width)] = dot_nt(grad_ref[:, :features], weight).astype(BF16)
            return carry

        lax.fori_loop(0, blocks // pair, step, 0)
        mixed_grad[...] = dot(order, result[...]).astype(BF16)
        for h in range(blocks):
            here = slice(h * width, (h + 1) * width)
            weights = jnp.concatenate(
                [part_ref[k, h] * pat[k, h].astype(F32).astype(BF16) for k in range(local, levels)], 0
            )
            terms = dot_nt(mixed_grad[:, here], weights).astype(BF16)
            for n in range(crossing):
                outgoing[n][:, here] = terms[:, n * width : (n + 1) * width]

    return pl.pallas_call(
        kernel,
        in_specs=[SMEM, SMEM, VMEM, HBM, VMEM, VMEM],
        out_specs=[VMEM] * (2 + crossing),
        out_shape=[jax.ShapeDtypeStruct((1, 1), F32)]
        + [jax.ShapeDtypeStruct((token_count, hidden), BF16)] * (1 + crossing),
        scratch_shapes=[
            pltpu.VMEM((blocks, features), F32),
            pltpu.VMEM((token_count, hidden), BF16),
            pltpu.VMEM((blocks // pair, pair * width, features), BF16),
            pltpu.SemaphoreType.DMA((blocks // pair,)),
        ],
        compiler_params=params(52),
        cost_estimate=cost(2 * token_count * features * hidden, features * hidden * 2),
        name="mixed_grad_phase",
    )(me, pattern, grad, down, scale, partner)


def block_grad_phase(pattern, act, received, mixed_grad, diag, partner):
    token_count, hidden = act.shape
    levels, blocks = pattern.shape
    width = diag.shape[-1]
    crossing = len(received)
    local = levels - crossing

    def kernel(pat, act_ref, mg, *refs):
        recv = refs[:crossing]
        diag_ref, part_ref, grad_diag, grad_part, act_grad = refs[crossing:]
        h = pl.program_id(0)

        grad = mg[:, columns(h, width)]
        grad_diag[0] = dot_tn(act_ref[:, columns(h, width)], grad)
        total = dot_nt(grad, diag_ref[h])
        for k in range(levels):
            keeps = pat[k, h].astype(F32)
            if k < local:
                other = h ^ (1 << k)
                source = act_ref[:, columns(other, width)]
                kept = pat[k, other].astype(F32).astype(BF16)
                total = total + dot_nt(mg[:, columns(other, width)], part_ref[k, other] * kept)
            else:
                source = recv[k - local][:, columns(h, width)]
            grad_part[k, 0] = dot_tn(source, grad) * keeps
        act_grad[...] = total

    return pl.pallas_call(
        kernel,
        grid=(blocks,),
        in_specs=[SMEM]
        + [whole((token_count, hidden))] * (2 + crossing)
        + [whole(diag.shape), whole(partner.shape)],
        out_specs=[
            pl.BlockSpec((1, width, width), lambda i: (i, 0, 0)),
            pl.BlockSpec((levels, 1, width, width), lambda i: (0, i, 0, 0)),
            pl.BlockSpec((token_count, width), lambda i: (0, i)),
        ],
        out_shape=[
            jax.ShapeDtypeStruct(diag.shape, F32),
            jax.ShapeDtypeStruct(partner.shape, F32),
            jax.ShapeDtypeStruct((token_count, hidden), F32),
        ],
        compiler_params=params(),
        cost_estimate=cost(2 * token_count * hidden * width * 12, 12 << 20),
        name="block_grad_phase",
    )(pattern, act, mixed_grad, *received, diag, partner)


def down_grad_phase(mixed, grad, features):
    token_count, hidden = mixed.shape
    chunk = min(512, features)
    steps = features // chunk

    def kernel(mixed_ref, grad_ref, out, turned, table, left):
        def store(c):
            return pltpu.make_async_copy(table.at[c], out.at[:, columns(c, chunk)], left.at[c])

        turned[...] = mixed_ref[...].T

        def step(c, carry):
            table[c] = dot(turned[...], grad_ref[:, columns(c, chunk)])
            store(c).start()
            return carry

        lax.fori_loop(0, steps, step, 0)
        for c in range(steps):
            store(c).wait()

    return pl.pallas_call(
        kernel,
        in_specs=[VMEM] * 2,
        out_specs=HBM,
        out_shape=jax.ShapeDtypeStruct((hidden, features), F32),
        scratch_shapes=[
            pltpu.VMEM((hidden, token_count), BF16),
            pltpu.VMEM((steps, hidden, chunk), F32),
            pltpu.SemaphoreType.DMA((steps,)),
        ],
        compiler_params=params(28),
        cost_estimate=cost(2 * token_count * features * hidden, features * hidden * 4),
        name="down_grad_phase",
    )(mixed, grad)


def up_grad_phase(tokens, pre, act_grad, received):
    token_count, depth = tokens.shape
    hidden = pre.shape[1]
    chunk = min(512, depth)
    steps = depth // chunk

    def kernel(tok, pre_ref, grad_ref, *refs):
        recv, (out, pre_grad, table, left) = refs[: len(received)], refs[len(received) :]

        def store(i):
            return pltpu.make_async_copy(table.at[i], out.at[columns(i, chunk), :], left.at[i])

        total = grad_ref[...]
        for r in recv:
            total = total + r[...].astype(F32)
        value = pre_ref[...]
        gate = jax.nn.sigmoid(value)
        pre_grad[...] = (total * (gate * (1.0 + value * (1.0 - gate)))).astype(BF16)

        def step(i, carry):
            table[i] = dot_tn(tok[:, columns(i, chunk)], pre_grad[...])
            store(i).start()
            return carry

        lax.fori_loop(0, steps, step, 0)
        for i in range(steps):
            store(i).wait()

    return pl.pallas_call(
        kernel,
        in_specs=[VMEM] * (3 + len(received)),
        out_specs=HBM,
        out_shape=jax.ShapeDtypeStruct((depth, hidden), F32),
        scratch_shapes=[
            pltpu.VMEM((token_count, hidden), BF16),
            pltpu.VMEM((steps, chunk, hidden), F32),
            pltpu.SemaphoreType.DMA((steps,)),
        ],
        compiler_params=params(28),
        cost_estimate=cost(2 * token_count * depth * hidden, depth * hidden * 4),
        name="up_grad_phase",
    )(tokens, pre, act_grad, *received)


def on_device(
    tokens,
    up_values,
    up_scale,
    diag_blocks,
    partner_blocks,
    pattern,
    down_values,
    down_scale,
    norm_gain,
    vocab_table,
    teacher_ids,
    teacher_logits,
):
    width = diag_blocks.shape[-1]
    token_count = tokens.shape[0]
    blocks = diag_blocks.shape[0]
    levels = partner_blocks.shape[0]
    local = blocks.bit_length() - 1
    count = lax.axis_size("mp")
    bits = count.bit_length() - 1
    groups = bit_groups(bits)
    rows = token_count // count
    me = lax.axis_index("mp").astype(jnp.int32).reshape(1)
    gain = norm_gain.reshape(1, -1)
    own = lax.dynamic_slice_in_dim(tokens, me[0] * rows, rows, 0)

    sparse = groups[:SHARED] == [[b] for b in range(SHARED)] and len(groups) == SHARED + 1
    if sparse:
        rank, flag, kept, sent = pick_phase(me, teacher_ids, vocab_table, rows, groups)
        pre, act = up_phase(tokens, up_values, up_scale, width, [flag])
        received = [swap(act, 1 << k - local) for k in range(local, levels)]
        own_mix = own_mix_phase(pattern, act, diag_blocks, partner_blocks, local, ())
        near, far, near_sent, far_sent = add_phase(
            kept, swap(sent, group_masks(groups[0])[1]), 4, [own_mix, *received[1:2]]
        )
        parts = lax.axis_size("groups")
        turned = flag
        for _ in range(parts - 1):
            turned = lax.ppermute(turned, "groups", [(i, (i + 1) % parts) for i in range(parts)])
            flag = flag + turned
        crowded = flag[0, 0] > 0
        far_laid = swap(far_sent, group_masks(groups[1])[1])
        near_laid = swap(near_sent, group_masks(groups[1])[1])
    else:
        pre, act = up_phase(tokens, up_values, up_scale, width, [])
        received = [swap(act, 1 << k - local) for k in range(local, levels)]
        own_mix = own_mix_phase(pattern, act, diag_blocks, partner_blocks, local, ())
    mixed, keep, send = mix_phase(
        me, pattern, own_mix, received, partner_blocks, down_values, down_scale, rows, groups, []
    )
    if sparse:
        masks = group_masks(groups[SHARED])
        far = add_phase(far, far_laid, len(masks) // 2, [])
        near = add_phase(near, near_laid, len(masks) // 2, far[:1])
        picked = [swap(piece, m) for piece, m in zip([*near, *far], masks)]
        terms = reduce_rows(keep, send, groups, [far, picked[1:]])
    else:
        terms = reduce_rows(keep, send, groups)

    def dense_tokens(*terms):
        stream, normed = norm_phase(terms, own, gain)
        normed = gather_rows(normed, groups)
        scores = score_phase(me, normed, vocab_table, teacher_ids, rows, groups)
        for b in range(bits):
            scores = scores + swap(scores, 1 << b)
        loss, keep, send = loss_phase(
            me, scores, teacher_logits, teacher_ids, vocab_table, rows, groups
        )
        return norm_back_phase(reduce_rows(keep, send, groups), stream, gain, loss)

    if sparse:
        grad = token_phase(
            me, terms, own, gain, picked, teacher_ids, rank, teacher_logits, vocab_table.shape[0]
        )
        grad = lax.cond(crowded, lambda grad, *terms: dense_tokens(*terms), lambda grad, *terms: grad, grad, *terms)
    else:
        grad = dense_tokens(*terms)
    grad = gather_rows(grad, groups)
    loss, mixed_grad, *outgoing = mixed_grad_phase(
        me, pattern, grad, down_values, down_scale, partner_blocks, rows, groups, local
    )
    incoming = [swap(block, 1 << n) for n, block in enumerate(outgoing)]
    grad_diag, grad_partner, act_grad = block_grad_phase(
        pattern, act, received, mixed_grad, diag_blocks, partner_blocks
    )
    grad_down = down_grad_phase(mixed, grad, down_values.shape[1])
    grad_up = up_grad_phase(tokens, pre, act_grad, incoming)
    return (loss.reshape(1), grad_up, grad_down, grad_diag, grad_partner)


def solution(mesh):
    return jax.shard_map(
        on_device,
        mesh=mesh,
        in_specs=(
            P("groups", None),
            P(None, "mp"),
            P(None, "mp"),
            P("mp", None, None),
            P(None, "mp", None, None),
            P(None, "mp"),
            P("mp", None),
            P("mp", None),
            P(),
            P("mp", None),
            P("groups", None),
            P("groups", None),
        ),
        out_specs=(
            P("groups"),
            P("groups", "mp"),
            P(("groups", "mp"), None),
            P(("groups", "mp"), None, None),
            P("groups", "mp", None, None),
        ),
        check_vma=False,
    )
```

```python
import functools

import jax
import jax.numpy as jnp
from jax import lax
from jax.experimental import pallas as pl
from jax.experimental.pallas import tpu as pltpu
from jax.sharding import PartitionSpec as P

F32, BF16 = jnp.float32, jnp.bfloat16
EPS = 1e-05
LANES = 128
SHARED = 2
SLOTS = 32
HELD = 128


def bit_groups(bits):
    if bits == 4:
        return [[0], [1], [2, 3]]
    return [[b] for b in range(bits)]


def group_masks(group):
    return [sum(1 << b for i, b in enumerate(group) if j >> i & 1) for j in range(1 << len(group))]


def swap(block, mask):
    if mask == 0:
        return block
    count = lax.axis_size("mp")
    return lax.ppermute(block, "mp", [(i, i ^ mask) for i in range(count)])


def reduce_rows(keep, send, groups, after=None):
    for n, group in enumerate(groups):
        masks = group_masks(group)
        if n == len(groups) - 1:
            return [keep] + [swap(s, m) for s, m in zip(send, masks[1:])]
        total = swap(send if n == 0 else send[0], masks[1])
        parts = 1 << len(groups[n + 1])
        keep, *send = add_phase(keep, total, parts, after[n] if after else [])


def gather_rows(rows, groups):
    for group in reversed(groups):
        masks = group_masks(group)
        rows = jnp.concatenate([rows] + [swap(rows, m) for m in masks[1:]], 0)
    return rows


def row_order(me, tokens, rows, groups, transposed):
    rel = lax.broadcasted_iota(jnp.int32, (tokens, tokens), 1 if transposed else 0)
    whole = lax.broadcasted_iota(jnp.int32, (tokens, tokens), 0 if transposed else 1)
    slot = rel // rows
    mask = jnp.zeros_like(slot)
    place = tokens // rows
    for group in groups:
        place >>= len(group)
        part = slot // place
        for i, b in enumerate(group):
            mask = mask | ((part >> i & 1) << b)
    source = ((me ^ mask) * rows) + rel % rows
    return (source == whole).astype(F32).astype(BF16)


def dot(a, b):
    return jnp.dot(a, b, preferred_element_type=F32)


def dot_nt(a, b):
    return lax.dot_general(a, b, (((1,), (1,)), ((), ())), preferred_element_type=F32)


def dot_tn(a, b):
    return lax.dot_general(a, b, (((0,), (0,)), ((), ())), preferred_element_type=F32)


def spread_factors(scale, width, first, count):
    blocks = scale.shape[1]
    column = lax.broadcasted_iota(jnp.int32, (blocks, count), 1) // width + first
    row = lax.broadcasted_iota(jnp.int32, (blocks, count), 0)
    pick = (column == row).astype(F32).astype(BF16)
    return dot(jnp.exp2(scale.astype(F32)).astype(BF16), pick).astype(BF16)


def params(mebibytes=16):
    return pltpu.CompilerParams(vmem_limit_bytes=mebibytes << 20)


def whole(shape):
    return pl.BlockSpec(shape, lambda i: (0,) * len(shape))


SMEM = pl.BlockSpec(memory_space=pltpu.SMEM)
UNREAD = pl.BlockSpec(memory_space=pl.ANY)
VMEM = pl.BlockSpec(memory_space=pltpu.VMEM)
HBM = pl.BlockSpec(memory_space=pltpu.HBM)


def columns(index, width):
    return pl.ds(pl.multiple_of(index * width, width), width)


def cost(flops, nbytes):
    return pl.CostEstimate(flops=int(flops), bytes_accessed=int(nbytes), transcendentals=0)


def up_phase(tokens, values, scale, width, after):
    token_count, depth = tokens.shape
    hidden = values.shape[1]
    chunk = min(512, depth)
    blocks = chunk // width
    steps = depth // chunk

    def kernel(tok, val, sc, *refs):
        pre, act, factors, table, arrived = refs[len(after) :]

        def fetch(i):
            return pltpu.make_async_copy(val.at[columns(i, chunk), :], table.at[i], arrived.at[i])

        for i in range(steps):
            fetch(i).start()
        factors[...] = spread_factors(sc[...], width, 0, hidden).astype(F32)

        def step(i, carry):
            fetch(i).wait()
            weight = jnp.concatenate(
                [
                    table[i, b * width : (b + 1) * width, :]
                    * factors[pl.ds(i * blocks + b, 1), :].astype(BF16)
                    for b in range(blocks)
                ],
                0,
            )
            part = dot(tok[:, columns(i, chunk)], weight)
            pre[...] = jnp.where(i == 0, part, pre[...] + part)
            return carry

        lax.fori_loop(0, steps, step, 0)
        total = pre[...]
        act[...] = (total * jax.nn.sigmoid(total)).astype(BF16)

    return pl.pallas_call(
        kernel,
        in_specs=[VMEM, HBM, VMEM] + [UNREAD] * len(after),
        out_specs=[VMEM] * 2,
        out_shape=[
            jax.ShapeDtypeStruct((token_count, hidden), F32),
            jax.ShapeDtypeStruct((token_count, hidden), BF16),
        ],
        scratch_shapes=[
            pltpu.VMEM((depth // width, hidden), F32),
            pltpu.VMEM((steps, chunk, hidden), BF16),
            pltpu.SemaphoreType.DMA((steps,)),
        ],
        compiler_params=params(48),
        cost_estimate=cost(2 * token_count * depth * hidden, depth * hidden * 2),
        name="up_phase",
    )(tokens, values, scale, *after)


def own_mix_phase(pattern, act, diag, partner, local, after):
    token_count, hidden = act.shape
    width = diag.shape[-1]
    levels, blocks = pattern.shape

    def kernel(pat, act_ref, diag_ref, part_ref, *refs):
        out = refs[-1]

        def mix(h):
            source = [act_ref[:, columns(h, width)]]
            weight = [diag_ref[h]]
            for k in range(local):
                source.append(act_ref[:, columns(h ^ (1 << k), width)])
                weight.append(part_ref[k, h] * pat[k, h].astype(F32).astype(BF16))
            out[:, columns(h, width)] = dot(
                jnp.concatenate(source, 1), jnp.concatenate(weight, 0)
            )

        for h in range(blocks):
            mix(h)

    return pl.pallas_call(
        kernel,
        in_specs=[SMEM] + [VMEM] * 3 + [UNREAD] * len(after),
        out_specs=VMEM,
        out_shape=jax.ShapeDtypeStruct((token_count, hidden), F32),
        compiler_params=params(),
        cost_estimate=cost(2 * token_count * hidden * width * 4, 4 << 20),
        name="own_mix_phase",
    )(pattern, act, diag, partner, *after)


def mix_phase(me, pattern, own, received, partner, down, scale, rows, groups, after):
    token_count, hidden = own.shape
    width = partner.shape[-1]
    levels, blocks = pattern.shape
    features = down.shape[1]
    chunk = min(512, features)
    steps = features // chunk
    crossing = len(received)
    local = levels - crossing
    half = token_count // 2

    def kernel(me_ref, pat, own_ref, *refs):
        recv = refs[:crossing]
        part_ref, down_ref, sc = refs[crossing : crossing + 3]
        mixed, keep, send, factors, table, arrived = refs[-6:]

        def fetch(c):
            return pltpu.make_async_copy(
                down_ref.at[:, columns(c, chunk)], table.at[c], arrived.at[c]
            )

        for c in range(steps):
            fetch(c).start()
        factors[...] = spread_factors(sc[...], width, 0, features).astype(F32)
        order = row_order(me_ref[0], token_count, rows, groups, False)

        def mix(h):
            here = columns(h, width)
            source = jnp.concatenate([r[:, here] for r in recv], 1)
            weight = jnp.concatenate(
                [
                    part_ref[k, h] * pat[k, h].astype(F32).astype(BF16)
                    for k in range(local, levels)
                ],
                0,
            )
            total = own_ref[:, here] + dot(source, weight)
            mixed[:, here] = dot(order, total.astype(BF16)).astype(BF16)

        for h in range(blocks):
            mix(h)

        def project(c, carry):
            fetch(c).wait()
            weight = jnp.concatenate(
                [
                    table[c, h * width : (h + 1) * width, :]
                    * factors[h : h + 1, columns(c, chunk)].astype(BF16)
                    for h in range(blocks)
                ],
                0,
            )
            result = dot(mixed[...], weight).astype(BF16)
            keep[:, columns(c, chunk)] = result[:half]
            send[:, columns(c, chunk)] = result[half:]
            return carry

        lax.fori_loop(0, steps, project, 0)

    return pl.pallas_call(
        kernel,
        in_specs=[SMEM, SMEM] + [VMEM] * (2 + crossing) + [HBM, VMEM] + [UNREAD] * len(after),
        out_specs=[VMEM] * 3,
        out_shape=[jax.ShapeDtypeStruct((token_count, hidden), BF16)]
        + [jax.ShapeDtypeStruct((half, features), BF16)] * 2,
        scratch_shapes=[
            pltpu.VMEM((blocks, features), F32),
            pltpu.VMEM((steps, hidden, chunk), BF16),
            pltpu.SemaphoreType.DMA((steps,)),
        ],
        compiler_params=params(50),
        cost_estimate=cost(2 * token_count * features * hidden, features * hidden * 2),
        name="mix_phase",
    )(me, pattern, own, *received, partner, down, scale, *after)


def add_phase(keep, received, parts, after, wanted=None):
    wanted = range(parts) if wanted is None else wanted
    rows, features = keep.shape
    rows //= parts

    def kernel(a, b, *refs):
        outs = refs[len(after) :]
        for n, out in zip(wanted, outs):
            here = slice(n * rows, (n + 1) * rows)
            out[...] = (a[here, :].astype(F32) + b[here, :].astype(F32)).astype(BF16)

    return pl.pallas_call(
        kernel,
        in_specs=[VMEM] * 2 + [UNREAD] * len(after),
        out_specs=[VMEM] * len(wanted),
        out_shape=[jax.ShapeDtypeStruct((rows, features), BF16)] * len(wanted),
        compiler_params=params(),
        name="add_phase",
    )(keep, received, *after)


def norm_phase(terms, own, gain):
    rows, features = own.shape

    def kernel(*refs):
        n = len(terms)
        own_ref, gain_ref, stream_ref, normed_ref = refs[n:]
        total = refs[0][...].astype(F32)
        for r in refs[1:n]:
            total = total + r[...].astype(F32)
        stream = (own_ref[...].astype(F32) + total).astype(BF16)
        values = stream.astype(F32)
        inverse = lax.rsqrt(jnp.mean(values * values, axis=1, keepdims=True) + EPS)
        stream_ref[...] = stream
        normed_ref[...] = (values * inverse * gain_ref[...]).astype(BF16)

    return pl.pallas_call(
        kernel,
        out_shape=[jax.ShapeDtypeStruct((rows, features), BF16)] * 2,
        compiler_params=params(),
        name="norm_phase",
    )(*terms, own, gain)


def score_phase(me, normed, vocab, ids, rows, groups):
    token_count, features = normed.shape
    entries = vocab.shape[0]
    picks = ids.shape[1]
    chunk = min(256, entries)

    def kernel(me_ref, normed_ref, vocab_ref, ids_ref, out, ordered):
        i = pl.program_id(0)

        @pl.when(i == 0)
        def _():
            order = row_order(me_ref[0], token_count, rows, groups, True)
            ordered[...] = dot(order, normed_ref[...]).astype(BF16)
            out[...] = jnp.zeros_like(out)

        scores = dot_nt(ordered[...], vocab_ref[...])
        offset = ids_ref[...] - (me_ref[0] * entries + i * chunk)
        number = lax.broadcasted_iota(jnp.int32, (token_count, chunk), 1)
        picked = [
            jnp.sum(jnp.where(offset[:, j : j + 1] == number, scores, 0.0), axis=1, keepdims=True)
            for j in range(picks)
        ]
        out[...] += jnp.concatenate(picked, 1)

    return pl.pallas_call(
        kernel,
        grid=(entries // chunk,),
        in_specs=[
            SMEM,
            whole((token_count, features)),
            pl.BlockSpec((chunk, features), lambda i: (i, 0)),
            whole(ids.shape),
        ],
        out_specs=whole((token_count, picks)),
        out_shape=jax.ShapeDtypeStruct((token_count, picks), F32),
        scratch_shapes=[pltpu.VMEM((token_count, features), BF16)],
        compiler_params=params(24),
        cost_estimate=cost(2 * token_count * features * entries, features * entries * 2),
        name="score_phase",
    )(me, normed, vocab, ids)


def loss_phase(me, scores, logits, ids, vocab, rows, groups):
    token_count, picks = scores.shape
    entries, features = vocab.shape
    chunk = min(512, features)
    half = token_count // 2

    def kernel(me_ref, scores_ref, logits_ref, ids_ref, vocab_ref, loss, keep, send, spread):
        i = pl.program_id(0)

        @pl.when(i == 0)
        def _():
            values = scores_ref[...]
            log_student = values - jnp.log(jnp.sum(jnp.exp(values), axis=1, keepdims=True))
            weights = jnp.exp(logits_ref[...])
            teacher = weights / jnp.sum(weights, axis=1, keepdims=True)
            each = jnp.sum(teacher * log_student, axis=1, keepdims=True)
            loss[...] = -jnp.sum(each, axis=0, keepdims=True) / token_count
            grad = (jnp.exp(log_student) - teacher).astype(BF16).astype(F32)
            offset = ids_ref[...] - me_ref[0] * entries
            number = lax.broadcasted_iota(jnp.int32, (token_count, entries), 1)
            total = jnp.zeros((token_count, entries), F32)
            for j in range(picks):
                total = jnp.where(offset[:, j : j + 1] == number, grad[:, j : j + 1], total)
            order = row_order(me_ref[0], token_count, rows, groups, False)
            spread[...] = dot(order, total.astype(BF16)).astype(BF16)

        result = dot(spread[...], vocab_ref[...]).astype(BF16)
        keep[...] = result[:half]
        send[...] = result[half:]

    return pl.pallas_call(
        kernel,
        grid=(features // chunk,),
        in_specs=[
            SMEM,
            whole(scores.shape),
            whole(logits.shape),
            whole(ids.shape),
            pl.BlockSpec((entries, chunk), lambda i: (0, i)),
        ],
        out_specs=[whole((1, 1))] + [pl.BlockSpec((half, chunk), lambda i: (0, i))] * 2,
        out_shape=[jax.ShapeDtypeStruct((1, 1), F32)]
        + [jax.ShapeDtypeStruct((half, features), BF16)] * 2,
        scratch_shapes=[pltpu.VMEM((token_count, entries), BF16)],
        compiler_params=params(24),
        cost_estimate=cost(2 * token_count * features * entries, features * entries * 2),
        name="loss_phase",
    )(me, scores, logits, ids, vocab)


def split_loss(loss):
    lane = lax.broadcasted_iota(jnp.int32, (loss.shape[0], LANES), 1)
    high = loss.astype(BF16).astype(F32)
    middle = (loss - high).astype(BF16).astype(F32)
    low = loss - high - middle
    return jnp.where(lane == 0, high, jnp.where(lane == 1, middle, jnp.where(lane == 2, low, 0.0)))


def norm_back_phase(terms, stream, gain, loss):
    rows, features = stream.shape

    def kernel(*refs):
        n = len(terms)
        stream_ref, gain_ref, loss_ref, out = refs[n:]
        upstream = refs[0][...].astype(F32)
        for r in refs[1:n]:
            upstream = upstream + r[...].astype(F32)
        values = stream_ref[...].astype(F32)
        inverse = lax.rsqrt(jnp.mean(values * values, axis=1, keepdims=True) + EPS)
        unit = values * inverse
        scaled = upstream * gain_ref[...]
        out[:, :features] = (
            inverse * (scaled - unit * jnp.mean(scaled * unit, axis=1, keepdims=True))
        ).astype(BF16)
        out[:, features:] = split_loss(jnp.broadcast_to(loss_ref[...], (rows, 1))).astype(BF16)

    return pl.pallas_call(
        kernel,
        out_shape=jax.ShapeDtypeStruct((rows, features + LANES), BF16),
        compiler_params=params(),
        name="norm_back_phase",
    )(*terms, stream, gain, loss)


def slot_of(index, count, groups):
    slot = jnp.zeros_like(index)
    place = count
    for group in groups:
        place >>= len(group)
        for i, b in enumerate(group):
            slot = slot | ((index >> b & 1) << i) * place
    return slot


def pick_phase(me, ids, vocab, rows, groups):
    token_count, picks = ids.shape
    entries, features = vocab.shape
    count = token_count // rows
    sharers = count >> SHARED
    chunk = min(512, features)
    half = count * SLOTS // 2
    wide = picks * sharers

    def ones(mask):
        return mask.astype(F32).astype(BF16)

    def iota(shape, axis):
        return lax.broadcasted_iota(jnp.int32, shape, axis)

    def kernel(me_ref, ids_ref, vocab_ref, rank_ref, flag_ref, keep, send, chosen, layout, table, arrived):
        def fetch(c):
            return pltpu.make_async_copy(
                vocab_ref.at[:, columns(c, chunk)], table.at[c], arrived.at[c]
            )

        for c in range(features // chunk):
            fetch(c).start()

        mine = me_ref[0]
        wanted = ids_ref[...].T
        shard = wanted // entries
        lane = iota((token_count, wide), 1)
        sharer = jnp.full((token_count, wide), -1, jnp.int32)
        for j in range(picks):
            sharer = jnp.where(lane // sharers == j, shard[:, j : j + 1] >> SHARED, sharer)
        asks = (sharer == lane % sharers).astype(F32)
        row, column = iota((token_count, token_count), 0), iota((token_count, token_count), 1)
        together = row // rows == column // rows
        earlier = dot(ones(together & (column < row)), asks.astype(BF16))
        total = dot(ones(together), asks.astype(BF16)).astype(BF16)
        a, b = iota((wide, wide), 0), iota((wide, wide), 1)
        before = dot(total, ones((a % sharers == b % sharers) & (a // sharers < b // sharers)))
        gathered = (asks * (earlier + before)).astype(BF16)
        rank = dot(gathered, ones(iota((wide, picks), 0) // sharers == iota((wide, picks), 1)))
        rank_ref[...] = rank.astype(jnp.int32)

        held = jnp.zeros((token_count, count), F32)
        for j in range(picks):
            held = held + (shard[:, j : j + 1] == iota((token_count, count), 1)).astype(F32)
        held = jnp.sum(held, axis=0, keepdims=True)
        over = (jnp.max(rank, keepdims=True) >= SLOTS) | (jnp.max(held, keepdims=True) > HELD)
        flag_ref[...] = jnp.broadcast_to(over.astype(F32), flag_ref.shape)

        here = (shard == mine).astype(F32)
        local = here.astype(BF16)
        place = dot(ones(column < row), local) + dot(
            dot(jnp.ones((token_count, token_count), BF16), local).astype(BF16),
            ones(iota((picks, picks), 0) < iota((picks, picks), 1)),
        )
        place = jnp.where(here > 0, place, -1.0).astype(jnp.int32)
        index = wanted - mine * entries + 1
        owner = iota((token_count, picks), 0) // rows
        target = slot_of(owner ^ mine, count, groups) * SLOTS + rank.astype(jnp.int32) + 1
        at = jnp.concatenate(
            [ones(place[:, j : j + 1] == iota((token_count, HELD), 1)) for j in range(picks)], 0
        )
        values = [index >> 7, index & 127, target >> 7, target & 127]
        values = jnp.concatenate([v.astype(F32).astype(BF16) for v in values], 1)
        lane = iota(values.shape, 1) % picks
        values = jnp.concatenate(
            [jnp.where(lane == j, values.astype(F32), 0.0).astype(BF16) for j in range(picks)], 0
        )
        found = dot_tn(at, values[:, : 2 * picks])
        source = jnp.sum(found[:, :picks] * 128 + found[:, picks:], axis=1, keepdims=True)
        source = source.astype(jnp.int32) - 1
        aim = dot_tn(values[:, 2 * picks :], at)
        aim = jnp.sum(aim[:picks] * 128 + aim[picks:], axis=0, keepdims=True).astype(jnp.int32) - 1
        chosen[...] = ones(source == iota((HELD, entries), 1))
        layout[...] = ones(iota((2 * half, HELD), 0) == aim)

        def lay(c, carry):
            fetch(c).wait()
            found = dot(chosen[...], table[c]).astype(BF16)
            laid = dot(layout[...], found).astype(BF16)
            keep[:, columns(c, chunk)] = laid[:half]
            send[:, columns(c, chunk)] = laid[half:]
            return carry

        lax.fori_loop(0, features // chunk, lay, 0)

    return pl.pallas_call(
        kernel,
        in_specs=[SMEM, VMEM, pl.BlockSpec(memory_space=pltpu.HBM)],
        out_specs=[VMEM] * 4,
        out_shape=[
            jax.ShapeDtypeStruct(ids.shape, jnp.int32),
            jax.ShapeDtypeStruct((8, LANES), F32),
        ]
        + [jax.ShapeDtypeStruct((half, features), BF16)] * 2,
        scratch_shapes=[
            pltpu.VMEM((HELD, entries), BF16),
            pltpu.VMEM((2 * half, HELD), BF16),
            pltpu.VMEM((features // chunk, entries, chunk), BF16),
            pltpu.SemaphoreType.DMA((features // chunk,)),
        ],
        compiler_params=params(32),
        cost_estimate=cost(4 * token_count * features * entries, features * entries * 2),
        name="pick_phase",
    )(me, ids.T, vocab)


def token_phase(me, terms, own, gain, picked, ids, rank, logits, entries):
    rows, features = own.shape
    picks = ids.shape[1]
    span = len(picked) * SLOTS

    def kernel(me_ref, *refs):
        n, p = len(terms), len(picked)
        sources = refs[n : n + p]
        own_ref, gain_ref, ids_ref, rank_ref, logits_ref, out, table, arrived = refs[n + p :]
        mine = pl.ds(pl.multiple_of(me_ref[0] * rows, rows), rows)
        copies = [
            pltpu.make_async_copy(source, table.at[m], arrived.at[m])
            for m, source in enumerate(sources)
        ]
        for copy in copies:
            copy.start()
        total = refs[0][...].astype(F32)
        for r in refs[1:n]:
            total = total + r[...].astype(F32)
        values = (own_ref[...].astype(F32) + total).astype(BF16).astype(F32)
        inverse = lax.rsqrt(jnp.mean(values * values, axis=1, keepdims=True) + EPS)
        unit = values * inverse
        normed = (unit * gain_ref[...]).astype(BF16)
        for copy in copies:
            copy.wait()
        dense = jnp.concatenate([dot_nt(normed, table[m]) for m in range(p)], 1)
        piece = (ids_ref[mine, :] // entries >> SHARED) ^ (me_ref[0] >> SHARED)
        place = piece * SLOTS + rank_ref[mine, :]
        number = lax.broadcasted_iota(jnp.int32, (rows, span), 1)
        hits = [place[:, j : j + 1] == number for j in range(picks)]
        scores = jnp.concatenate(
            [jnp.sum(jnp.where(hit, dense, 0.0), axis=1, keepdims=True) for hit in hits], 1
        )
        log_student = scores - jnp.log(jnp.sum(jnp.exp(scores), axis=1, keepdims=True))
        weights = jnp.exp(logits_ref[mine, :])
        teacher = weights / jnp.sum(weights, axis=1, keepdims=True)
        loss = -jnp.sum(teacher * log_student, axis=1, keepdims=True)
        grad = (jnp.exp(log_student) - teacher).astype(BF16).astype(F32)
        spread = jnp.zeros((rows, span), F32)
        for j in range(picks):
            spread = jnp.where(hits[j], grad[:, j : j + 1], spread)
        spread = spread.astype(BF16)
        upstream = dot(spread[:, :SLOTS], table[0])
        for m in range(1, p):
            upstream = upstream + dot(spread[:, m * SLOTS : (m + 1) * SLOTS], table[m])
        scaled = upstream * gain_ref[...]
        out[:, :features] = (
            inverse * (scaled - unit * jnp.mean(scaled * unit, axis=1, keepdims=True))
        ).astype(BF16)
        out[:, features:] = split_loss(loss).astype(BF16)

    return pl.pallas_call(
        kernel,
        in_specs=[SMEM] + [VMEM] * len(terms) + [UNREAD] * len(picked) + [VMEM] * 5,
        scratch_shapes=[
            pltpu.VMEM((len(picked), SLOTS, features), BF16),
            pltpu.SemaphoreType.DMA((len(picked),)),
        ],
        out_shape=jax.ShapeDtypeStruct((rows, features + LANES), BF16),
        compiler_params=params(),
        name="token_phase",
    )(me, *terms, *picked, own, gain, ids, rank, logits)


def mixed_grad_phase(me, pattern, grad, down, scale, partner, rows, groups, local):
    token_count = grad.shape[0]
    hidden, features = down.shape
    levels, blocks = pattern.shape
    width = partner.shape[-1]
    crossing = levels - local
    pair = 2 if blocks % 2 == 0 else 1

    def kernel(me_ref, pat, grad_ref, down_ref, sc, part_ref, loss, mixed_grad, *refs):
        outgoing, (factors, result, table, arrived) = refs[:crossing], refs[crossing:]

        def fetch(i):
            return pltpu.make_async_copy(
                down_ref.at[columns(i, pair * width), :], table.at[i], arrived.at[i]
            )

        for i in range(blocks // pair):
            fetch(i).start()
        factors[...] = spread_factors(sc[...], width, 0, features).astype(F32)
        order = row_order(me_ref[0], token_count, rows, groups, True)
        each = jnp.sum(grad_ref[:, features:].astype(F32), axis=1, keepdims=True)
        loss[...] = jnp.sum(each, axis=0, keepdims=True) / token_count

        def step(i, carry):
            fetch(i).wait()
            weight = jnp.concatenate(
                [
                    table[i, b * width : (b + 1) * width, :]
                    * factors[pl.ds(i * pair + b, 1), :].astype(BF16)
                    for b in range(pair)
                ],
                0,
            )
            result[:, columns(i, pair * width)] = dot_nt(grad_ref[:, :features], weight).astype(BF16)
            return carry

        lax.fori_loop(0, blocks // pair, step, 0)
        mixed_grad[...] = dot(order, result[...]).astype(BF16)
        for h in range(blocks):
            here = slice(h * width, (h + 1) * width)
            weights = jnp.concatenate(
                [part_ref[k, h] * pat[k, h].astype(F32).astype(BF16) for k in range(local, levels)], 0
            )
            terms = dot_nt(mixed_grad[:, here], weights).astype(BF16)
            for n in range(crossing):
                outgoing[n][:, here] = terms[:, n * width : (n + 1) * width]

    return pl.pallas_call(
        kernel,
        in_specs=[SMEM, SMEM, VMEM, HBM, VMEM, VMEM],
        out_specs=[VMEM] * (2 + crossing),
        out_shape=[jax.ShapeDtypeStruct((1, 1), F32)]
        + [jax.ShapeDtypeStruct((token_count, hidden), BF16)] * (1 + crossing),
        scratch_shapes=[
            pltpu.VMEM((blocks, features), F32),
            pltpu.VMEM((token_count, hidden), BF16),
            pltpu.VMEM((blocks // pair, pair * width, features), BF16),
            pltpu.SemaphoreType.DMA((blocks // pair,)),
        ],
        compiler_params=params(50),
        cost_estimate=cost(2 * token_count * features * hidden, features * hidden * 2),
        name="mixed_grad_phase",
    )(me, pattern, grad, down, scale, partner)


def block_grad_phase(pattern, act, received, mixed_grad, diag, partner):
    token_count, hidden = act.shape
    levels, blocks = pattern.shape
    width = diag.shape[-1]
    crossing = len(received)
    local = levels - crossing

    def kernel(pat, act_ref, mg, *refs):
        recv = refs[:crossing]
        diag_ref, part_ref, grad_diag, grad_part, act_grad = refs[crossing:]
        h = pl.program_id(0)

        grad = mg[:, columns(h, width)]
        grad_diag[0] = dot_tn(act_ref[:, columns(h, width)], grad)
        total = dot_nt(grad, diag_ref[h])
        for k in range(levels):
            keeps = pat[k, h].astype(F32)
            if k < local:
                other = h ^ (1 << k)
                source = act_ref[:, columns(other, width)]
                kept = pat[k, other].astype(F32).astype(BF16)
                total = total + dot_nt(mg[:, columns(other, width)], part_ref[k, other] * kept)
            else:
                source = recv[k - local][:, columns(h, width)]
            grad_part[k, 0] = dot_tn(source, grad) * keeps
        act_grad[...] = total

    return pl.pallas_call(
        kernel,
        grid=(blocks,),
        in_specs=[SMEM]
        + [whole((token_count, hidden))] * (2 + crossing)
        + [whole(diag.shape), whole(partner.shape)],
        out_specs=[
            pl.BlockSpec((1, width, width), lambda i: (i, 0, 0)),
            pl.BlockSpec((levels, 1, width, width), lambda i: (0, i, 0, 0)),
            pl.BlockSpec((token_count, width), lambda i: (0, i)),
        ],
        out_shape=[
            jax.ShapeDtypeStruct(diag.shape, F32),
            jax.ShapeDtypeStruct(partner.shape, F32),
            jax.ShapeDtypeStruct((token_count, hidden), F32),
        ],
        compiler_params=params(),
        cost_estimate=cost(2 * token_count * hidden * width * 12, 12 << 20),
        name="block_grad_phase",
    )(pattern, act, mixed_grad, *received, diag, partner)


def down_grad_phase(mixed, grad, features):
    token_count, hidden = mixed.shape
    chunk = min(512, features)
    steps = features // chunk

    def kernel(mixed_ref, grad_ref, out, turned, table, left):
        def store(c):
            return pltpu.make_async_copy(table.at[c], out.at[:, columns(c, chunk)], left.at[c])

        turned[...] = mixed_ref[...].T

        def step(c, carry):
            table[c] = dot(turned[...], grad_ref[:, columns(c, chunk)])
            store(c).start()
            return carry

        lax.fori_loop(0, steps, step, 0)
        for c in range(steps):
            store(c).wait()

    return pl.pallas_call(
        kernel,
        in_specs=[VMEM] * 2,
        out_specs=HBM,
        out_shape=jax.ShapeDtypeStruct((hidden, features), F32),
        scratch_shapes=[
            pltpu.VMEM((hidden, token_count), BF16),
            pltpu.VMEM((steps, hidden, chunk), F32),
            pltpu.SemaphoreType.DMA((steps,)),
        ],
        compiler_params=params(28),
        cost_estimate=cost(2 * token_count * features * hidden, features * hidden * 4),
        name="down_grad_phase",
    )(mixed, grad)


def up_grad_phase(tokens, pre, act_grad, received):
    token_count, depth = tokens.shape
    hidden = pre.shape[1]
    chunk = min(512, depth)
    steps = depth // chunk

    def kernel(tok, pre_ref, grad_ref, *refs):
        recv, (out, pre_grad, table, left) = refs[: len(received)], refs[len(received) :]

        def store(i):
            return pltpu.make_async_copy(table.at[i], out.at[columns(i, chunk), :], left.at[i])

        total = grad_ref[...]
        for r in recv:
            total = total + r[...].astype(F32)
        value = pre_ref[...]
        gate = jax.nn.sigmoid(value)
        pre_grad[...] = (total * (gate * (1.0 + value * (1.0 - gate)))).astype(BF16)

        def step(i, carry):
            table[i] = dot_tn(tok[:, columns(i, chunk)], pre_grad[...])
            store(i).start()
            return carry

        lax.fori_loop(0, steps, step, 0)
        for i in range(steps):
            store(i).wait()

    return pl.pallas_call(
        kernel,
        in_specs=[VMEM] * (3 + len(received)),
        out_specs=HBM,
        out_shape=jax.ShapeDtypeStruct((depth, hidden), F32),
        scratch_shapes=[
            pltpu.VMEM((token_count, hidden), BF16),
            pltpu.VMEM((steps, chunk, hidden), F32),
            pltpu.SemaphoreType.DMA((steps,)),
        ],
        compiler_params=params(28),
        cost_estimate=cost(2 * token_count * depth * hidden, depth * hidden * 4),
        name="up_grad_phase",
    )(tokens, pre, act_grad, *received)


def on_device(
    tokens,
    up_values,
    up_scale,
    diag_blocks,
    partner_blocks,
    pattern,
    down_values,
    down_scale,
    norm_gain,
    vocab_table,
    teacher_ids,
    teacher_logits,
):
    width = diag_blocks.shape[-1]
    token_count = tokens.shape[0]
    blocks = diag_blocks.shape[0]
    levels = partner_blocks.shape[0]
    local = blocks.bit_length() - 1
    count = lax.axis_size("mp")
    bits = count.bit_length() - 1
    groups = bit_groups(bits)
    rows = token_count // count
    me = lax.axis_index("mp").astype(jnp.int32).reshape(1)
    gain = norm_gain.reshape(1, -1)
    own = lax.dynamic_slice_in_dim(tokens, me[0] * rows, rows, 0)

    sparse = groups[:SHARED] == [[b] for b in range(SHARED)] and len(groups) == SHARED + 1
    if sparse:
        rank, flag, kept, sent = pick_phase(me, teacher_ids, vocab_table, rows, groups)
        pre, act = up_phase(tokens, up_values, up_scale, width, [flag])
        received = [swap(act, 1 << k - local) for k in range(local, levels)]
        own_mix = own_mix_phase(pattern, act, diag_blocks, partner_blocks, local, ())
        given = swap(sent, group_masks(groups[0])[1])
        (far_sent,) = add_phase(kept, given, 4, [own_mix, *received[1:2]], [3])
        near, far, near_sent = add_phase(kept, given, 4, [far_sent], [0, 1, 2])
        parts = lax.axis_size("groups")
        turned = flag
        for _ in range(parts - 1):
            turned = lax.ppermute(turned, "groups", [(i, (i + 1) % parts) for i in range(parts)])
            flag = flag + turned
        crowded = flag[0, 0] > 0
        far_laid = swap(far_sent, group_masks(groups[1])[1])
        near_laid = swap(near_sent, group_masks(groups[1])[1])
    else:
        pre, act = up_phase(tokens, up_values, up_scale, width, [])
        received = [swap(act, 1 << k - local) for k in range(local, levels)]
        own_mix = own_mix_phase(pattern, act, diag_blocks, partner_blocks, local, ())
    early = [near_sent] if sparse else []
    mixed, keep, send = mix_phase(
        me, pattern, own_mix, received, partner_blocks, down_values, down_scale, rows, groups, early
    )
    if sparse:
        masks = group_masks(groups[SHARED])
        far = add_phase(far, far_laid, len(masks) // 2, [])
        near = add_phase(near, near_laid, len(masks) // 2, far[:1])
        picked = [swap(piece, m) for piece, m in zip([*near, *far], masks)]
        terms = reduce_rows(keep, send, groups, [far, picked[2:]])
    else:
        terms = reduce_rows(keep, send, groups)

    def dense_tokens(*terms):
        stream, normed = norm_phase(terms, own, gain)
        normed = gather_rows(normed, groups)
        scores = score_phase(me, normed, vocab_table, teacher_ids, rows, groups)
        for b in range(bits):
            scores = scores + swap(scores, 1 << b)
        loss, keep, send = loss_phase(
            me, scores, teacher_logits, teacher_ids, vocab_table, rows, groups
        )
        return norm_back_phase(reduce_rows(keep, send, groups), stream, gain, loss)

    if sparse:
        grad = token_phase(
            me, terms, own, gain, picked, teacher_ids, rank, teacher_logits, vocab_table.shape[0]
        )
        grad = lax.cond(crowded, lambda grad, *terms: dense_tokens(*terms), lambda grad, *terms: grad, grad, *terms)
    else:
        grad = dense_tokens(*terms)
    grad = gather_rows(grad, groups)
    loss, mixed_grad, *outgoing = mixed_grad_phase(
        me, pattern, grad, down_values, down_scale, partner_blocks, rows, groups, local
    )
    incoming = [swap(block, 1 << n) for n, block in enumerate(outgoing)]
    grad_diag, grad_partner, act_grad = block_grad_phase(
        pattern, act, received, mixed_grad, diag_blocks, partner_blocks
    )
    grad_down = down_grad_phase(mixed, grad, down_values.shape[1])
    grad_up = up_grad_phase(tokens, pre, act_grad, incoming)
    return (loss.reshape(1), grad_up, grad_down, grad_diag, grad_partner)


def solution(mesh):
    return jax.shard_map(
        on_device,
        mesh=mesh,
        in_specs=(
            P("groups", None),
            P(None, "mp"),
            P(None, "mp"),
            P("mp", None, None),
            P(None, "mp", None, None),
            P(None, "mp"),
            P("mp", None),
            P("mp", None),
            P(),
            P("mp", None),
            P("groups", None),
            P("groups", None),
        ),
        out_specs=(
            P("groups"),
            P("groups", "mp"),
            P(("groups", "mp"), None),
            P(("groups", "mp"), None, None),
            P("groups", "mp", None, None),
        ),
        check_vma=False,
    )
```

```python
import functools

import jax
import jax.numpy as jnp
from jax import lax
from jax.experimental import pallas as pl
from jax.experimental.pallas import tpu as pltpu
from jax.sharding import PartitionSpec as P

F32, BF16 = jnp.float32, jnp.bfloat16
EPS = 1e-05
LANES = 128
SHARED = 2
SLOTS = 32
HELD = 128


def bit_groups(bits):
    if bits == 4:
        return [[0], [1], [2, 3]]
    return [[b] for b in range(bits)]


def group_masks(group):
    return [sum(1 << b for i, b in enumerate(group) if j >> i & 1) for j in range(1 << len(group))]


def swap(block, mask):
    if mask == 0:
        return block
    count = lax.axis_size("mp")
    return lax.ppermute(block, "mp", [(i, i ^ mask) for i in range(count)])


def reduce_rows(keep, send, groups, after=None):
    for n, group in enumerate(groups):
        masks = group_masks(group)
        if n == len(groups) - 1:
            return [keep] + [swap(s, m) for s, m in zip(send, masks[1:])]
        total = swap(send if n == 0 else send[0], masks[1])
        parts = 1 << len(groups[n + 1])
        keep, *send = add_phase(keep, total, parts, after[n] if after else [])


def gather_rows(rows, groups):
    for group in reversed(groups):
        masks = group_masks(group)
        rows = jnp.concatenate([rows] + [swap(rows, m) for m in masks[1:]], 0)
    return rows


def row_order(me, tokens, rows, groups, transposed):
    rel = lax.broadcasted_iota(jnp.int32, (tokens, tokens), 1 if transposed else 0)
    whole = lax.broadcasted_iota(jnp.int32, (tokens, tokens), 0 if transposed else 1)
    slot = rel // rows
    mask = jnp.zeros_like(slot)
    place = tokens // rows
    for group in groups:
        place >>= len(group)
        part = slot // place
        for i, b in enumerate(group):
            mask = mask | ((part >> i & 1) << b)
    source = ((me ^ mask) * rows) + rel % rows
    return (source == whole).astype(F32).astype(BF16)


def dot(a, b):
    return jnp.dot(a, b, preferred_element_type=F32)


def dot_nt(a, b):
    return lax.dot_general(a, b, (((1,), (1,)), ((), ())), preferred_element_type=F32)


def dot_tn(a, b):
    return lax.dot_general(a, b, (((0,), (0,)), ((), ())), preferred_element_type=F32)


def spread_factors(scale, width, first, count):
    blocks = scale.shape[1]
    column = lax.broadcasted_iota(jnp.int32, (blocks, count), 1) // width + first
    row = lax.broadcasted_iota(jnp.int32, (blocks, count), 0)
    pick = (column == row).astype(F32).astype(BF16)
    return dot(jnp.exp2(scale.astype(F32)).astype(BF16), pick).astype(BF16)


def params(mebibytes=16):
    return pltpu.CompilerParams(vmem_limit_bytes=mebibytes << 20)


def whole(shape):
    return pl.BlockSpec(shape, lambda i: (0,) * len(shape))


SMEM = pl.BlockSpec(memory_space=pltpu.SMEM)
UNREAD = pl.BlockSpec(memory_space=pl.ANY)
VMEM = pl.BlockSpec(memory_space=pltpu.VMEM)
HBM = pl.BlockSpec(memory_space=pltpu.HBM)


def columns(index, width):
    return pl.ds(pl.multiple_of(index * width, width), width)


def cost(flops, nbytes):
    return pl.CostEstimate(flops=int(flops), bytes_accessed=int(nbytes), transcendentals=0)


def up_phase(tokens, values, scale, width, after):
    token_count, depth = tokens.shape
    hidden = values.shape[1]
    chunk = min(512, depth)
    blocks = chunk // width
    steps = depth // chunk

    def kernel(tok, val, sc, *refs):
        pre, act, factors, table, arrived = refs[len(after) :]

        def fetch(i):
            return pltpu.make_async_copy(val.at[columns(i, chunk), :], table.at[i], arrived.at[i])

        for i in range(steps):
            fetch(i).start()
        factors[...] = spread_factors(sc[...], width, 0, hidden).astype(F32)

        def step(i, carry):
            fetch(i).wait()
            weight = jnp.concatenate(
                [
                    table[i, b * width : (b + 1) * width, :]
                    * factors[pl.ds(i * blocks + b, 1), :].astype(BF16)
                    for b in range(blocks)
                ],
                0,
            )
            part = dot(tok[:, columns(i, chunk)], weight)
            pre[...] = jnp.where(i == 0, part, pre[...] + part)
            return carry

        lax.fori_loop(0, steps, step, 0)
        total = pre[...]
        act[...] = (total * jax.nn.sigmoid(total)).astype(BF16)

    return pl.pallas_call(
        kernel,
        in_specs=[VMEM, HBM, VMEM] + [UNREAD] * len(after),
        out_specs=[VMEM] * 2,
        out_shape=[
            jax.ShapeDtypeStruct((token_count, hidden), F32),
            jax.ShapeDtypeStruct((token_count, hidden), BF16),
        ],
        scratch_shapes=[
            pltpu.VMEM((depth // width, hidden), F32),
            pltpu.VMEM((steps, chunk, hidden), BF16),
            pltpu.SemaphoreType.DMA((steps,)),
        ],
        compiler_params=params(48),
        cost_estimate=cost(2 * token_count * depth * hidden, depth * hidden * 2),
        name="up_phase",
    )(tokens, values, scale, *after)


def own_mix_phase(pattern, act, diag, partner, local, after):
    token_count, hidden = act.shape
    width = diag.shape[-1]
    levels, blocks = pattern.shape

    def kernel(pat, act_ref, diag_ref, part_ref, *refs):
        out = refs[-1]

        def mix(h):
            source = [act_ref[:, columns(h, width)]]
            weight = [diag_ref[h]]
            for k in range(local):
                source.append(act_ref[:, columns(h ^ (1 << k), width)])
                weight.append(part_ref[k, h] * pat[k, h].astype(F32).astype(BF16))
            out[:, columns(h, width)] = dot(
                jnp.concatenate(source, 1), jnp.concatenate(weight, 0)
            )

        for h in range(blocks):
            mix(h)

    return pl.pallas_call(
        kernel,
        in_specs=[SMEM] + [VMEM] * 3 + [UNREAD] * len(after),
        out_specs=VMEM,
        out_shape=jax.ShapeDtypeStruct((token_count, hidden), F32),
        compiler_params=params(),
        cost_estimate=cost(2 * token_count * hidden * width * 4, 4 << 20),
        name="own_mix_phase",
    )(pattern, act, diag, partner, *after)


def mix_phase(me, pattern, own, received, partner, down, scale, rows, groups, after):
    token_count, hidden = own.shape
    width = partner.shape[-1]
    levels, blocks = pattern.shape
    features = down.shape[1]
    chunk = min(512, features)
    steps = features // chunk
    crossing = len(received)
    local = levels - crossing
    half = token_count // 2

    def kernel(me_ref, pat, own_ref, *refs):
        recv = refs[:crossing]
        part_ref, down_ref, sc = refs[crossing : crossing + 3]
        mixed, keep, send, factors, table, arrived = refs[-6:]

        def fetch(c):
            return pltpu.make_async_copy(
                down_ref.at[:, columns(c, chunk)], table.at[c], arrived.at[c]
            )

        for c in range(steps):
            fetch(c).start()
        factors[...] = spread_factors(sc[...], width, 0, features).astype(F32)
        order = row_order(me_ref[0], token_count, rows, groups, False)

        def mix(h):
            here = columns(h, width)
            source = jnp.concatenate([r[:, here] for r in recv], 1)
            weight = jnp.concatenate(
                [
                    part_ref[k, h] * pat[k, h].astype(F32).astype(BF16)
                    for k in range(local, levels)
                ],
                0,
            )
            total = own_ref[:, here] + dot(source, weight)
            mixed[:, here] = dot(order, total.astype(BF16)).astype(BF16)

        for h in range(blocks):
            mix(h)

        def project(c, carry):
            fetch(c).wait()
            weight = jnp.concatenate(
                [
                    table[c, h * width : (h + 1) * width, :]
                    * factors[h : h + 1, columns(c, chunk)].astype(BF16)
                    for h in range(blocks)
                ],
                0,
            )
            result = dot(mixed[...], weight).astype(BF16)
            keep[:, columns(c, chunk)] = result[:half]
            send[:, columns(c, chunk)] = result[half:]
            return carry

        lax.fori_loop(0, steps, project, 0)

    return pl.pallas_call(
        kernel,
        in_specs=[SMEM, SMEM] + [VMEM] * (2 + crossing) + [HBM, VMEM] + [UNREAD] * len(after),
        out_specs=[VMEM] * 3,
        out_shape=[jax.ShapeDtypeStruct((token_count, hidden), BF16)]
        + [jax.ShapeDtypeStruct((half, features), BF16)] * 2,
        scratch_shapes=[
            pltpu.VMEM((blocks, features), F32),
            pltpu.VMEM((steps, hidden, chunk), BF16),
            pltpu.SemaphoreType.DMA((steps,)),
        ],
        compiler_params=params(50),
        cost_estimate=cost(2 * token_count * features * hidden, features * hidden * 2),
        name="mix_phase",
    )(me, pattern, own, *received, partner, down, scale, *after)


def add_phase(keep, received, parts, after, wanted=None):
    wanted = range(parts) if wanted is None else wanted
    rows, features = keep.shape
    rows //= parts

    def kernel(a, b, *refs):
        outs = refs[len(after) :]
        for n, out in zip(wanted, outs):
            here = slice(n * rows, (n + 1) * rows)
            out[...] = (a[here, :].astype(F32) + b[here, :].astype(F32)).astype(BF16)

    return pl.pallas_call(
        kernel,
        in_specs=[VMEM] * 2 + [UNREAD] * len(after),
        out_specs=[VMEM] * len(wanted),
        out_shape=[jax.ShapeDtypeStruct((rows, features), BF16)] * len(wanted),
        compiler_params=params(),
        name="add_phase",
    )(keep, received, *after)


def norm_phase(terms, own, gain):
    rows, features = own.shape

    def kernel(*refs):
        n = len(terms)
        own_ref, gain_ref, stream_ref, normed_ref = refs[n:]
        total = refs[0][...].astype(F32)
        for r in refs[1:n]:
            total = total + r[...].astype(F32)
        stream = (own_ref[...].astype(F32) + total).astype(BF16)
        values = stream.astype(F32)
        inverse = lax.rsqrt(jnp.mean(values * values, axis=1, keepdims=True) + EPS)
        stream_ref[...] = stream
        normed_ref[...] = (values * inverse * gain_ref[...]).astype(BF16)

    return pl.pallas_call(
        kernel,
        out_shape=[jax.ShapeDtypeStruct((rows, features), BF16)] * 2,
        compiler_params=params(),
        name="norm_phase",
    )(*terms, own, gain)


def score_phase(me, normed, vocab, ids, rows, groups):
    token_count, features = normed.shape
    entries = vocab.shape[0]
    picks = ids.shape[1]
    chunk = min(256, entries)

    def kernel(me_ref, normed_ref, vocab_ref, ids_ref, out, ordered):
        i = pl.program_id(0)

        @pl.when(i == 0)
        def _():
            order = row_order(me_ref[0], token_count, rows, groups, True)
            ordered[...] = dot(order, normed_ref[...]).astype(BF16)
            out[...] = jnp.zeros_like(out)

        scores = dot_nt(ordered[...], vocab_ref[...])
        offset = ids_ref[...] - (me_ref[0] * entries + i * chunk)
        number = lax.broadcasted_iota(jnp.int32, (token_count, chunk), 1)
        picked = [
            jnp.sum(jnp.where(offset[:, j : j + 1] == number, scores, 0.0), axis=1, keepdims=True)
            for j in range(picks)
        ]
        out[...] += jnp.concatenate(picked, 1)

    return pl.pallas_call(
        kernel,
        grid=(entries // chunk,),
        in_specs=[
            SMEM,
            whole((token_count, features)),
            pl.BlockSpec((chunk, features), lambda i: (i, 0)),
            whole(ids.shape),
        ],
        out_specs=whole((token_count, picks)),
        out_shape=jax.ShapeDtypeStruct((token_count, picks), F32),
        scratch_shapes=[pltpu.VMEM((token_count, features), BF16)],
        compiler_params=params(24),
        cost_estimate=cost(2 * token_count * features * entries, features * entries * 2),
        name="score_phase",
    )(me, normed, vocab, ids)


def loss_phase(me, scores, logits, ids, vocab, rows, groups):
    token_count, picks = scores.shape
    entries, features = vocab.shape
    chunk = min(512, features)
    half = token_count // 2

    def kernel(me_ref, scores_ref, logits_ref, ids_ref, vocab_ref, loss, keep, send, spread):
        i = pl.program_id(0)

        @pl.when(i == 0)
        def _():
            values = scores_ref[...]
            log_student = values - jnp.log(jnp.sum(jnp.exp(values), axis=1, keepdims=True))
            weights = jnp.exp(logits_ref[...])
            teacher = weights / jnp.sum(weights, axis=1, keepdims=True)
            each = jnp.sum(teacher * log_student, axis=1, keepdims=True)
            loss[...] = -jnp.sum(each, axis=0, keepdims=True) / token_count
            grad = (jnp.exp(log_student) - teacher).astype(BF16).astype(F32)
            offset = ids_ref[...] - me_ref[0] * entries
            number = lax.broadcasted_iota(jnp.int32, (token_count, entries), 1)
            total = jnp.zeros((token_count, entries), F32)
            for j in range(picks):
                total = jnp.where(offset[:, j : j + 1] == number, grad[:, j : j + 1], total)
            order = row_order(me_ref[0], token_count, rows, groups, False)
            spread[...] = dot(order, total.astype(BF16)).astype(BF16)

        result = dot(spread[...], vocab_ref[...]).astype(BF16)
        keep[...] = result[:half]
        send[...] = result[half:]

    return pl.pallas_call(
        kernel,
        grid=(features // chunk,),
        in_specs=[
            SMEM,
            whole(scores.shape),
            whole(logits.shape),
            whole(ids.shape),
            pl.BlockSpec((entries, chunk), lambda i: (0, i)),
        ],
        out_specs=[whole((1, 1))] + [pl.BlockSpec((half, chunk), lambda i: (0, i))] * 2,
        out_shape=[jax.ShapeDtypeStruct((1, 1), F32)]
        + [jax.ShapeDtypeStruct((half, features), BF16)] * 2,
        scratch_shapes=[pltpu.VMEM((token_count, entries), BF16)],
        compiler_params=params(24),
        cost_estimate=cost(2 * token_count * features * entries, features * entries * 2),
        name="loss_phase",
    )(me, scores, logits, ids, vocab)


def split_loss(loss):
    lane = lax.broadcasted_iota(jnp.int32, (loss.shape[0], LANES), 1)
    high = loss.astype(BF16).astype(F32)
    middle = (loss - high).astype(BF16).astype(F32)
    low = loss - high - middle
    return jnp.where(lane == 0, high, jnp.where(lane == 1, middle, jnp.where(lane == 2, low, 0.0)))


def norm_back_phase(terms, stream, gain, loss):
    rows, features = stream.shape

    def kernel(*refs):
        n = len(terms)
        stream_ref, gain_ref, loss_ref, out = refs[n:]
        upstream = refs[0][...].astype(F32)
        for r in refs[1:n]:
            upstream = upstream + r[...].astype(F32)
        values = stream_ref[...].astype(F32)
        inverse = lax.rsqrt(jnp.mean(values * values, axis=1, keepdims=True) + EPS)
        unit = values * inverse
        scaled = upstream * gain_ref[...]
        out[:, :features] = (
            inverse * (scaled - unit * jnp.mean(scaled * unit, axis=1, keepdims=True))
        ).astype(BF16)
        out[:, features:] = split_loss(jnp.broadcast_to(loss_ref[...], (rows, 1))).astype(BF16)

    return pl.pallas_call(
        kernel,
        out_shape=jax.ShapeDtypeStruct((rows, features + LANES), BF16),
        compiler_params=params(),
        name="norm_back_phase",
    )(*terms, stream, gain, loss)


def slot_of(index, count, groups):
    slot = jnp.zeros_like(index)
    place = count
    for group in groups:
        place >>= len(group)
        for i, b in enumerate(group):
            slot = slot | ((index >> b & 1) << i) * place
    return slot


def pick_phase(me, ids, vocab, rows, groups):
    token_count, picks = ids.shape
    entries, features = vocab.shape
    count = token_count // rows
    sharers = count >> SHARED
    chunk = min(512, features)
    half = count * SLOTS // 2
    wide = picks * sharers

    def ones(mask):
        return mask.astype(F32).astype(BF16)

    def iota(shape, axis):
        return lax.broadcasted_iota(jnp.int32, shape, axis)

    def kernel(me_ref, ids_ref, vocab_ref, rank_ref, flag_ref, keep, send, chosen, layout, table, arrived):
        def fetch(c):
            return pltpu.make_async_copy(
                vocab_ref.at[:, columns(c, chunk)], table.at[c], arrived.at[c]
            )

        for c in range(features // chunk):
            fetch(c).start()

        mine = me_ref[0]
        wanted = ids_ref[...].T
        shard = wanted // entries
        lane = iota((token_count, wide), 1)
        sharer = jnp.full((token_count, wide), -1, jnp.int32)
        for j in range(picks):
            sharer = jnp.where(lane // sharers == j, shard[:, j : j + 1] >> SHARED, sharer)
        asks = (sharer == lane % sharers).astype(F32)
        row, column = iota((token_count, token_count), 0), iota((token_count, token_count), 1)
        together = row // rows == column // rows
        earlier = dot(ones(together & (column < row)), asks.astype(BF16))
        total = dot(ones(together), asks.astype(BF16)).astype(BF16)
        a, b = iota((wide, wide), 0), iota((wide, wide), 1)
        before = dot(total, ones((a % sharers == b % sharers) & (a // sharers < b // sharers)))
        gathered = (asks * (earlier + before)).astype(BF16)
        rank = dot(gathered, ones(iota((wide, picks), 0) // sharers == iota((wide, picks), 1)))
        rank_ref[...] = rank.astype(jnp.int32)

        held = jnp.zeros((token_count, count), F32)
        for j in range(picks):
            held = held + (shard[:, j : j + 1] == iota((token_count, count), 1)).astype(F32)
        held = jnp.sum(held, axis=0, keepdims=True)
        over = (jnp.max(rank, keepdims=True) >= SLOTS) | (jnp.max(held, keepdims=True) > HELD)
        flag_ref[...] = jnp.broadcast_to(over.astype(F32), flag_ref.shape)

        here = (shard == mine).astype(F32)
        local = here.astype(BF16)
        place = dot(ones(column < row), local) + dot(
            dot(jnp.ones((token_count, token_count), BF16), local).astype(BF16),
            ones(iota((picks, picks), 0) < iota((picks, picks), 1)),
        )
        place = jnp.where(here > 0, place, -1.0).astype(jnp.int32)
        index = wanted - mine * entries + 1
        owner = iota((token_count, picks), 0) // rows
        target = slot_of(owner ^ mine, count, groups) * SLOTS + rank.astype(jnp.int32) + 1
        at = jnp.concatenate(
            [ones(place[:, j : j + 1] == iota((token_count, HELD), 1)) for j in range(picks)], 0
        )
        values = [index >> 7, index & 127, target >> 7, target & 127]
        values = jnp.concatenate([v.astype(F32).astype(BF16) for v in values], 1)
        lane = iota(values.shape, 1) % picks
        values = jnp.concatenate(
            [jnp.where(lane == j, values.astype(F32), 0.0).astype(BF16) for j in range(picks)], 0
        )
        found = dot_tn(at, values[:, : 2 * picks])
        source = jnp.sum(found[:, :picks] * 128 + found[:, picks:], axis=1, keepdims=True)
        source = source.astype(jnp.int32) - 1
        aim = dot_tn(values[:, 2 * picks :], at)
        aim = jnp.sum(aim[:picks] * 128 + aim[picks:], axis=0, keepdims=True).astype(jnp.int32) - 1
        chosen[...] = ones(source == iota((HELD, entries), 1))
        layout[...] = ones(iota((2 * half, HELD), 0) == aim)

        def lay(c, carry):
            fetch(c).wait()
            found = dot(chosen[...], table[c]).astype(BF16)
            laid = dot(layout[...], found).astype(BF16)
            keep[:, columns(c, chunk)] = laid[:half]
            send[:, columns(c, chunk)] = laid[half:]
            return carry

        lax.fori_loop(0, features // chunk, lay, 0)

    return pl.pallas_call(
        kernel,
        in_specs=[SMEM, VMEM, pl.BlockSpec(memory_space=pltpu.HBM)],
        out_specs=[VMEM] * 4,
        out_shape=[
            jax.ShapeDtypeStruct(ids.shape, jnp.int32),
            jax.ShapeDtypeStruct((8, LANES), F32),
        ]
        + [jax.ShapeDtypeStruct((half, features), BF16)] * 2,
        scratch_shapes=[
            pltpu.VMEM((HELD, entries), BF16),
            pltpu.VMEM((2 * half, HELD), BF16),
            pltpu.VMEM((features // chunk, entries, chunk), BF16),
            pltpu.SemaphoreType.DMA((features // chunk,)),
        ],
        compiler_params=params(32),
        cost_estimate=cost(4 * token_count * features * entries, features * entries * 2),
        name="pick_phase",
    )(me, ids.T, vocab)


def token_phase(me, terms, own, gain, picked, ids, rank, logits, entries):
    rows, features = own.shape
    picks = ids.shape[1]
    span = len(picked) * SLOTS

    def kernel(me_ref, *refs):
        n, p = len(terms), len(picked)
        sources = refs[n : n + p]
        own_ref, gain_ref, ids_ref, rank_ref, logits_ref, out, table, arrived = refs[n + p :]
        mine = pl.ds(pl.multiple_of(me_ref[0] * rows, rows), rows)
        copies = [
            pltpu.make_async_copy(source, table.at[m], arrived.at[m])
            for m, source in enumerate(sources)
        ]
        for copy in copies:
            copy.start()
        total = refs[0][...].astype(F32)
        for r in refs[1:n]:
            total = total + r[...].astype(F32)
        values = (own_ref[...].astype(F32) + total).astype(BF16).astype(F32)
        inverse = lax.rsqrt(jnp.mean(values * values, axis=1, keepdims=True) + EPS)
        unit = values * inverse
        normed = (unit * gain_ref[...]).astype(BF16)
        for copy in copies:
            copy.wait()
        dense = jnp.concatenate([dot_nt(normed, table[m]) for m in range(p)], 1)
        piece = (ids_ref[mine, :] // entries >> SHARED) ^ (me_ref[0] >> SHARED)
        place = piece * SLOTS + rank_ref[mine, :]
        number = lax.broadcasted_iota(jnp.int32, (rows, span), 1)
        hits = [place[:, j : j + 1] == number for j in range(picks)]
        scores = jnp.concatenate(
            [jnp.sum(jnp.where(hit, dense, 0.0), axis=1, keepdims=True) for hit in hits], 1
        )
        log_student = scores - jnp.log(jnp.sum(jnp.exp(scores), axis=1, keepdims=True))
        weights = jnp.exp(logits_ref[mine, :])
        teacher = weights / jnp.sum(weights, axis=1, keepdims=True)
        loss = -jnp.sum(teacher * log_student, axis=1, keepdims=True)
        grad = (jnp.exp(log_student) - teacher).astype(BF16).astype(F32)
        spread = jnp.zeros((rows, span), F32)
        for j in range(picks):
            spread = jnp.where(hits[j], grad[:, j : j + 1], spread)
        spread = spread.astype(BF16)
        upstream = dot(spread[:, :SLOTS], table[0])
        for m in range(1, p):
            upstream = upstream + dot(spread[:, m * SLOTS : (m + 1) * SLOTS], table[m])
        scaled = upstream * gain_ref[...]
        out[:, :features] = (
            inverse * (scaled - unit * jnp.mean(scaled * unit, axis=1, keepdims=True))
        ).astype(BF16)
        out[:, features:] = split_loss(loss).astype(BF16)

    return pl.pallas_call(
        kernel,
        in_specs=[SMEM] + [VMEM] * len(terms) + [UNREAD] * len(picked) + [VMEM] * 5,
        scratch_shapes=[
            pltpu.VMEM((len(picked), SLOTS, features), BF16),
            pltpu.SemaphoreType.DMA((len(picked),)),
        ],
        out_shape=jax.ShapeDtypeStruct((rows, features + LANES), BF16),
        compiler_params=params(),
        name="token_phase",
    )(me, *terms, *picked, own, gain, ids, rank, logits)


def mixed_grad_phase(me, pattern, grad, down, scale, partner, rows, groups, local):
    token_count = grad.shape[0]
    hidden, features = down.shape
    levels, blocks = pattern.shape
    width = partner.shape[-1]
    crossing = levels - local
    pair = 2 if blocks % 2 == 0 else 1

    def kernel(me_ref, pat, grad_ref, down_ref, sc, part_ref, loss, mixed_grad, *refs):
        outgoing, (factors, result, table, arrived) = refs[:crossing], refs[crossing:]

        def fetch(i):
            return pltpu.make_async_copy(
                down_ref.at[columns(i, pair * width), :], table.at[i], arrived.at[i]
            )

        for i in range(blocks // pair):
            fetch(i).start()
        factors[...] = spread_factors(sc[...], width, 0, features).astype(F32)
        order = row_order(me_ref[0], token_count, rows, groups, True)
        each = jnp.sum(grad_ref[:, features:].astype(F32), axis=1, keepdims=True)
        loss[...] = jnp.sum(each, axis=0, keepdims=True) / token_count

        def step(i, carry):
            fetch(i).wait()
            weight = jnp.concatenate(
                [
                    table[i, b * width : (b + 1) * width, :]
                    * factors[pl.ds(i * pair + b, 1), :].astype(BF16)
                    for b in range(pair)
                ],
                0,
            )
            result[:, columns(i, pair * width)] = dot_nt(grad_ref[:, :features], weight).astype(BF16)
            return carry

        lax.fori_loop(0, blocks // pair, step, 0)
        mixed_grad[...] = dot(order, result[...]).astype(BF16)
        for h in range(blocks):
            here = slice(h * width, (h + 1) * width)
            weights = jnp.concatenate(
                [part_ref[k, h] * pat[k, h].astype(F32).astype(BF16) for k in range(local, levels)], 0
            )
            terms = dot_nt(mixed_grad[:, here], weights).astype(BF16)
            for n in range(crossing):
                outgoing[n][:, here] = terms[:, n * width : (n + 1) * width]

    return pl.pallas_call(
        kernel,
        in_specs=[SMEM, SMEM, VMEM, HBM, VMEM, VMEM],
        out_specs=[VMEM] * (2 + crossing),
        out_shape=[jax.ShapeDtypeStruct((1, 1), F32)]
        + [jax.ShapeDtypeStruct((token_count, hidden), BF16)] * (1 + crossing),
        scratch_shapes=[
            pltpu.VMEM((blocks, features), F32),
            pltpu.VMEM((token_count, hidden), BF16),
            pltpu.VMEM((blocks // pair, pair * width, features), BF16),
            pltpu.SemaphoreType.DMA((blocks // pair,)),
        ],
        compiler_params=params(50),
        cost_estimate=cost(2 * token_count * features * hidden, features * hidden * 2),
        name="mixed_grad_phase",
    )(me, pattern, grad, down, scale, partner)


def block_grad_phase(pattern, act, received, mixed_grad, diag, partner):
    token_count, hidden = act.shape
    levels, blocks = pattern.shape
    width = diag.shape[-1]
    crossing = len(received)
    local = levels - crossing

    def kernel(pat, act_ref, mg, *refs):
        recv = refs[:crossing]
        diag_ref, part_ref, grad_diag, grad_part, act_grad = refs[crossing:]
        h = pl.program_id(0)

        grad = mg[:, columns(h, width)]
        grad_diag[0] = dot_tn(act_ref[:, columns(h, width)], grad)
        total = dot_nt(grad, diag_ref[h])
        for k in range(levels):
            keeps = pat[k, h].astype(F32)
            if k < local:
                other = h ^ (1 << k)
                source = act_ref[:, columns(other, width)]
                kept = pat[k, other].astype(F32).astype(BF16)
                total = total + dot_nt(mg[:, columns(other, width)], part_ref[k, other] * kept)
            else:
                source = recv[k - local][:, columns(h, width)]
            grad_part[k, 0] = dot_tn(source, grad) * keeps
        act_grad[...] = total

    return pl.pallas_call(
        kernel,
        grid=(blocks,),
        in_specs=[SMEM]
        + [whole((token_count, hidden))] * (2 + crossing)
        + [whole(diag.shape), whole(partner.shape)],
        out_specs=[
            pl.BlockSpec((1, width, width), lambda i: (i, 0, 0)),
            pl.BlockSpec((levels, 1, width, width), lambda i: (0, i, 0, 0)),
            pl.BlockSpec((token_count, width), lambda i: (0, i)),
        ],
        out_shape=[
            jax.ShapeDtypeStruct(diag.shape, F32),
            jax.ShapeDtypeStruct(partner.shape, F32),
            jax.ShapeDtypeStruct((token_count, hidden), F32),
        ],
        compiler_params=params(),
        cost_estimate=cost(2 * token_count * hidden * width * 12, 12 << 20),
        name="block_grad_phase",
    )(pattern, act, mixed_grad, *received, diag, partner)


def down_grad_phase(mixed, grad, features):
    token_count, hidden = mixed.shape
    chunk = min(256, features)
    steps = features // chunk

    def kernel(mixed_ref, grad_ref, out, turned, table, left):
        def store(c):
            return pltpu.make_async_copy(table.at[c], out.at[:, columns(c, chunk)], left.at[c])

        turned[...] = mixed_ref[...].T

        def step(c, carry):
            table[c] = dot(turned[...], grad_ref[:, columns(c, chunk)])
            store(c).start()
            return carry

        lax.fori_loop(0, steps, step, 0)
        for c in range(steps):
            store(c).wait()

    return pl.pallas_call(
        kernel,
        in_specs=[VMEM] * 2,
        out_specs=HBM,
        out_shape=jax.ShapeDtypeStruct((hidden, features), F32),
        scratch_shapes=[
            pltpu.VMEM((hidden, token_count), BF16),
            pltpu.VMEM((steps, hidden, chunk), F32),
            pltpu.SemaphoreType.DMA((steps,)),
        ],
        compiler_params=params(28),
        cost_estimate=cost(2 * token_count * features * hidden, features * hidden * 4),
        name="down_grad_phase",
    )(mixed, grad)


def up_grad_phase(tokens, pre, act_grad, received):
    token_count, depth = tokens.shape
    hidden = pre.shape[1]
    chunk = min(256, depth)
    steps = depth // chunk

    def kernel(tok, pre_ref, grad_ref, *refs):
        recv, (out, pre_grad, table, left) = refs[: len(received)], refs[len(received) :]

        def store(i):
            return pltpu.make_async_copy(table.at[i], out.at[columns(i, chunk), :], left.at[i])

        total = grad_ref[...]
        for r in recv:
            total = total + r[...].astype(F32)
        value = pre_ref[...]
        gate = jax.nn.sigmoid(value)
        pre_grad[...] = (total * (gate * (1.0 + value * (1.0 - gate)))).astype(BF16)

        def step(i, carry):
            table[i] = dot_tn(tok[:, columns(i, chunk)], pre_grad[...])
            store(i).start()
            return carry

        lax.fori_loop(0, steps, step, 0)
        for i in range(steps):
            store(i).wait()

    return pl.pallas_call(
        kernel,
        in_specs=[VMEM] * (3 + len(received)),
        out_specs=HBM,
        out_shape=jax.ShapeDtypeStruct((depth, hidden), F32),
        scratch_shapes=[
            pltpu.VMEM((token_count, hidden), BF16),
            pltpu.VMEM((steps, chunk, hidden), F32),
            pltpu.SemaphoreType.DMA((steps,)),
        ],
        compiler_params=params(28),
        cost_estimate=cost(2 * token_count * depth * hidden, depth * hidden * 4),
        name="up_grad_phase",
    )(tokens, pre, act_grad, *received)


def on_device(
    tokens,
    up_values,
    up_scale,
    diag_blocks,
    partner_blocks,
    pattern,
    down_values,
    down_scale,
    norm_gain,
    vocab_table,
    teacher_ids,
    teacher_logits,
):
    width = diag_blocks.shape[-1]
    token_count = tokens.shape[0]
    blocks = diag_blocks.shape[0]
    levels = partner_blocks.shape[0]
    local = blocks.bit_length() - 1
    count = lax.axis_size("mp")
    bits = count.bit_length() - 1
    groups = bit_groups(bits)
    rows = token_count // count
    me = lax.axis_index("mp").astype(jnp.int32).reshape(1)
    gain = norm_gain.reshape(1, -1)
    own = lax.dynamic_slice_in_dim(tokens, me[0] * rows, rows, 0)

    sparse = groups[:SHARED] == [[b] for b in range(SHARED)] and len(groups) == SHARED + 1
    if sparse:
        rank, flag, kept, sent = pick_phase(me, teacher_ids, vocab_table, rows, groups)
        pre, act = up_phase(tokens, up_values, up_scale, width, [flag])
        received = [swap(act, 1 << k - local) for k in range(local, levels)]
        own_mix = own_mix_phase(pattern, act, diag_blocks, partner_blocks, local, ())
        given = swap(sent, group_masks(groups[0])[1])
        (far_sent,) = add_phase(kept, given, 4, [own_mix, *received[1:2]], [3])
        near, far, near_sent = add_phase(kept, given, 4, [far_sent], [0, 1, 2])
        parts = lax.axis_size("groups")
        turned = flag
        for _ in range(parts - 1):
            turned = lax.ppermute(turned, "groups", [(i, (i + 1) % parts) for i in range(parts)])
            flag = flag + turned
        crowded = flag[0, 0] > 0
        far_laid = swap(far_sent, group_masks(groups[1])[1])
        near_laid = swap(near_sent, group_masks(groups[1])[1])
    else:
        pre, act = up_phase(tokens, up_values, up_scale, width, [])
        received = [swap(act, 1 << k - local) for k in range(local, levels)]
        own_mix = own_mix_phase(pattern, act, diag_blocks, partner_blocks, local, ())
    early = [near_sent] if sparse else []
    mixed, keep, send = mix_phase(
        me, pattern, own_mix, received, partner_blocks, down_values, down_scale, rows, groups, early
    )
    if sparse:
        masks = group_masks(groups[SHARED])
        far = add_phase(far, far_laid, len(masks) // 2, [])
        near = add_phase(near, near_laid, len(masks) // 2, far[:1])
        picked = [swap(piece, m) for piece, m in zip([*near, *far], masks)]
        terms = reduce_rows(keep, send, groups, [far, picked[2:3]])
    else:
        terms = reduce_rows(keep, send, groups)

    def dense_tokens(*terms):
        stream, normed = norm_phase(terms, own, gain)
        normed = gather_rows(normed, groups)
        scores = score_phase(me, normed, vocab_table, teacher_ids, rows, groups)
        for b in range(bits):
            scores = scores + swap(scores, 1 << b)
        loss, keep, send = loss_phase(
            me, scores, teacher_logits, teacher_ids, vocab_table, rows, groups
        )
        return norm_back_phase(reduce_rows(keep, send, groups), stream, gain, loss)

    if sparse:
        grad = token_phase(
            me, terms, own, gain, picked, teacher_ids, rank, teacher_logits, vocab_table.shape[0]
        )
        grad = lax.cond(crowded, lambda grad, *terms: dense_tokens(*terms), lambda grad, *terms: grad, grad, *terms)
    else:
        grad = dense_tokens(*terms)
    grad = gather_rows(grad, groups)
    loss, mixed_grad, *outgoing = mixed_grad_phase(
        me, pattern, grad, down_values, down_scale, partner_blocks, rows, groups, local
    )
    incoming = [swap(block, 1 << n) for n, block in enumerate(outgoing)]
    grad_diag, grad_partner, act_grad = block_grad_phase(
        pattern, act, received, mixed_grad, diag_blocks, partner_blocks
    )
    grad_down = down_grad_phase(mixed, grad, down_values.shape[1])
    grad_up = up_grad_phase(tokens, pre, act_grad, incoming)
    return (loss.reshape(1), grad_up, grad_down, grad_diag, grad_partner)


def solution(mesh):
    return jax.shard_map(
        on_device,
        mesh=mesh,
        in_specs=(
            P("groups", None),
            P(None, "mp"),
            P(None, "mp"),
            P("mp", None, None),
            P(None, "mp", None, None),
            P(None, "mp"),
            P("mp", None),
            P("mp", None),
            P(),
            P("mp", None),
            P("groups", None),
            P("groups", None),
        ),
        out_specs=(
            P("groups"),
            P("groups", "mp"),
            P(("groups", "mp"), None),
            P(("groups", "mp"), None, None),
            P("groups", "mp", None, None),
        ),
        check_vma=False,
    )
```

```python
import functools

import jax
import jax.numpy as jnp
from jax import lax
from jax.experimental import pallas as pl
from jax.experimental.pallas import tpu as pltpu
from jax.sharding import PartitionSpec as P

F32, BF16 = jnp.float32, jnp.bfloat16
EPS = 1e-05
LANES = 128
SHARED = 2
SLOTS = 32
HELD = 128


def bit_groups(bits):
    if bits == 4:
        return [[0], [1], [2, 3]]
    return [[b] for b in range(bits)]


def group_masks(group):
    return [sum(1 << b for i, b in enumerate(group) if j >> i & 1) for j in range(1 << len(group))]


def swap(block, mask):
    if mask == 0:
        return block
    count = lax.axis_size("mp")
    return lax.ppermute(block, "mp", [(i, i ^ mask) for i in range(count)])


def reduce_rows(keep, send, groups, after=None):
    for n, group in enumerate(groups):
        masks = group_masks(group)
        if n == len(groups) - 1:
            return [keep] + [swap(s, m) for s, m in zip(send, masks[1:])]
        total = swap(send if n == 0 else send[0], masks[1])
        parts = 1 << len(groups[n + 1])
        keep, *send = add_phase(keep, total, parts, after[n] if after else [])


def gather_rows(rows, groups):
    for group in reversed(groups):
        masks = group_masks(group)
        rows = jnp.concatenate([rows] + [swap(rows, m) for m in masks[1:]], 0)
    return rows


def row_order(me, tokens, rows, groups, transposed):
    rel = lax.broadcasted_iota(jnp.int32, (tokens, tokens), 1 if transposed else 0)
    whole = lax.broadcasted_iota(jnp.int32, (tokens, tokens), 0 if transposed else 1)
    slot = rel // rows
    mask = jnp.zeros_like(slot)
    place = tokens // rows
    for group in groups:
        place >>= len(group)
        part = slot // place
        for i, b in enumerate(group):
            mask = mask | ((part >> i & 1) << b)
    source = ((me ^ mask) * rows) + rel % rows
    return (source == whole).astype(F32).astype(BF16)


def dot(a, b):
    return jnp.dot(a, b, preferred_element_type=F32)


def dot_nt(a, b):
    return lax.dot_general(a, b, (((1,), (1,)), ((), ())), preferred_element_type=F32)


def dot_tn(a, b):
    return lax.dot_general(a, b, (((0,), (0,)), ((), ())), preferred_element_type=F32)


def spread_factors(scale, width, first, count):
    blocks = scale.shape[1]
    column = lax.broadcasted_iota(jnp.int32, (blocks, count), 1) // width + first
    row = lax.broadcasted_iota(jnp.int32, (blocks, count), 0)
    pick = (column == row).astype(F32).astype(BF16)
    return dot(jnp.exp2(scale.astype(F32)).astype(BF16), pick).astype(BF16)


def params(mebibytes=16):
    return pltpu.CompilerParams(vmem_limit_bytes=mebibytes << 20)


def whole(shape):
    return pl.BlockSpec(shape, lambda i: (0,) * len(shape))


SMEM = pl.BlockSpec(memory_space=pltpu.SMEM)
UNREAD = pl.BlockSpec(memory_space=pl.ANY)
VMEM = pl.BlockSpec(memory_space=pltpu.VMEM)
HBM = pl.BlockSpec(memory_space=pltpu.HBM)


def columns(index, width):
    return pl.ds(pl.multiple_of(index * width, width), width)


def cost(flops, nbytes):
    return pl.CostEstimate(flops=int(flops), bytes_accessed=int(nbytes), transcendentals=0)


def up_phase(tokens, values, scale, width, after):
    token_count, depth = tokens.shape
    hidden = values.shape[1]
    chunk = min(512, depth)
    blocks = chunk // width
    steps = depth // chunk

    def kernel(tok, val, sc, *refs):
        pre, act, factors, table, arrived = refs[len(after) :]

        def fetch(i):
            return pltpu.make_async_copy(val.at[columns(i, chunk), :], table.at[i], arrived.at[i])

        for i in range(steps):
            fetch(i).start()
        factors[...] = spread_factors(sc[...], width, 0, hidden).astype(F32)

        def step(i, carry):
            fetch(i).wait()
            weight = jnp.concatenate(
                [
                    table[i, b * width : (b + 1) * width, :]
                    * factors[pl.ds(i * blocks + b, 1), :].astype(BF16)
                    for b in range(blocks)
                ],
                0,
            )
            part = dot(tok[:, columns(i, chunk)], weight)
            pre[...] = jnp.where(i == 0, part, pre[...] + part)
            return carry

        lax.fori_loop(0, steps, step, 0)
        total = pre[...]
        act[...] = (total * jax.nn.sigmoid(total)).astype(BF16)

    return pl.pallas_call(
        kernel,
        in_specs=[VMEM, HBM, VMEM] + [UNREAD] * len(after),
        out_specs=[VMEM] * 2,
        out_shape=[
            jax.ShapeDtypeStruct((token_count, hidden), F32),
            jax.ShapeDtypeStruct((token_count, hidden), BF16),
        ],
        scratch_shapes=[
            pltpu.VMEM((depth // width, hidden), F32),
            pltpu.VMEM((steps, chunk, hidden), BF16),
            pltpu.SemaphoreType.DMA((steps,)),
        ],
        compiler_params=params(48),
        cost_estimate=cost(2 * token_count * depth * hidden, depth * hidden * 2),
        name="up_phase",
    )(tokens, values, scale, *after)


def own_mix_phase(pattern, act, diag, partner, local, after):
    token_count, hidden = act.shape
    width = diag.shape[-1]
    levels, blocks = pattern.shape

    def kernel(pat, act_ref, diag_ref, part_ref, *refs):
        out = refs[-1]

        def mix(h):
            source = [act_ref[:, columns(h, width)]]
            weight = [diag_ref[h]]
            for k in range(local):
                source.append(act_ref[:, columns(h ^ (1 << k), width)])
                weight.append(part_ref[k, h] * pat[k, h].astype(F32).astype(BF16))
            out[:, columns(h, width)] = dot(
                jnp.concatenate(source, 1), jnp.concatenate(weight, 0)
            )

        for h in range(blocks):
            mix(h)

    return pl.pallas_call(
        kernel,
        in_specs=[SMEM] + [VMEM] * 3 + [UNREAD] * len(after),
        out_specs=VMEM,
        out_shape=jax.ShapeDtypeStruct((token_count, hidden), F32),
        compiler_params=params(),
        cost_estimate=cost(2 * token_count * hidden * width * 4, 4 << 20),
        name="own_mix_phase",
    )(pattern, act, diag, partner, *after)


def mix_phase(me, pattern, own, received, partner, down, scale, rows, groups, after):
    token_count, hidden = own.shape
    width = partner.shape[-1]
    levels, blocks = pattern.shape
    features = down.shape[1]
    chunk = min(512, features)
    steps = features // chunk
    crossing = len(received)
    local = levels - crossing
    half = token_count // 2

    def kernel(me_ref, pat, own_ref, *refs):
        recv = refs[:crossing]
        part_ref, down_ref, sc = refs[crossing : crossing + 3]
        mixed, keep, send, factors, table, arrived = refs[-6:]

        def fetch(c):
            return pltpu.make_async_copy(
                down_ref.at[:, columns(c, chunk)], table.at[c], arrived.at[c]
            )

        for c in range(steps):
            fetch(c).start()
        factors[...] = spread_factors(sc[...], width, 0, features).astype(F32)
        order = row_order(me_ref[0], token_count, rows, groups, False)

        def mix(h):
            here = columns(h, width)
            source = jnp.concatenate([r[:, here] for r in recv], 1)
            weight = jnp.concatenate(
                [
                    part_ref[k, h] * pat[k, h].astype(F32).astype(BF16)
                    for k in range(local, levels)
                ],
                0,
            )
            total = own_ref[:, here] + dot(source, weight)
            mixed[:, here] = dot(order, total.astype(BF16)).astype(BF16)

        for h in range(blocks):
            mix(h)

        def project(c, carry):
            fetch(c).wait()
            weight = jnp.concatenate(
                [
                    table[c, h * width : (h + 1) * width, :]
                    * factors[h : h + 1, columns(c, chunk)].astype(BF16)
                    for h in range(blocks)
                ],
                0,
            )
            result = dot(mixed[...], weight).astype(BF16)
            keep[:, columns(c, chunk)] = result[:half]
            send[:, columns(c, chunk)] = result[half:]
            return carry

        lax.fori_loop(0, steps, project, 0)

    return pl.pallas_call(
        kernel,
        in_specs=[SMEM, SMEM] + [VMEM] * (2 + crossing) + [HBM, VMEM] + [UNREAD] * len(after),
        out_specs=[VMEM] * 3,
        out_shape=[jax.ShapeDtypeStruct((token_count, hidden), BF16)]
        + [jax.ShapeDtypeStruct((half, features), BF16)] * 2,
        scratch_shapes=[
            pltpu.VMEM((blocks, features), F32),
            pltpu.VMEM((steps, hidden, chunk), BF16),
            pltpu.SemaphoreType.DMA((steps,)),
        ],
        compiler_params=params(50),
        cost_estimate=cost(2 * token_count * features * hidden, features * hidden * 2),
        name="mix_phase",
    )(me, pattern, own, *received, partner, down, scale, *after)


def add_phase(keep, received, parts, after, wanted=None):
    wanted = range(parts) if wanted is None else wanted
    rows, features = keep.shape
    rows //= parts

    def kernel(a, b, *refs):
        outs = refs[len(after) :]
        for n, out in zip(wanted, outs):
            here = slice(n * rows, (n + 1) * rows)
            out[...] = (a[here, :].astype(F32) + b[here, :].astype(F32)).astype(BF16)

    return pl.pallas_call(
        kernel,
        in_specs=[VMEM] * 2 + [UNREAD] * len(after),
        out_specs=[VMEM] * len(wanted),
        out_shape=[jax.ShapeDtypeStruct((rows, features), BF16)] * len(wanted),
        compiler_params=params(),
        name="add_phase",
    )(keep, received, *after)


def norm_phase(terms, own, gain):
    rows, features = own.shape

    def kernel(*refs):
        n = len(terms)
        own_ref, gain_ref, stream_ref, normed_ref = refs[n:]
        total = refs[0][...].astype(F32)
        for r in refs[1:n]:
            total = total + r[...].astype(F32)
        stream = (own_ref[...].astype(F32) + total).astype(BF16)
        values = stream.astype(F32)
        inverse = lax.rsqrt(jnp.mean(values * values, axis=1, keepdims=True) + EPS)
        stream_ref[...] = stream
        normed_ref[...] = (values * inverse * gain_ref[...]).astype(BF16)

    return pl.pallas_call(
        kernel,
        out_shape=[jax.ShapeDtypeStruct((rows, features), BF16)] * 2,
        compiler_params=params(),
        name="norm_phase",
    )(*terms, own, gain)


def score_phase(me, normed, vocab, ids, rows, groups):
    token_count, features = normed.shape
    entries = vocab.shape[0]
    picks = ids.shape[1]
    chunk = min(256, entries)

    def kernel(me_ref, normed_ref, vocab_ref, ids_ref, out, ordered):
        i = pl.program_id(0)

        @pl.when(i == 0)
        def _():
            order = row_order(me_ref[0], token_count, rows, groups, True)
            ordered[...] = dot(order, normed_ref[...]).astype(BF16)
            out[...] = jnp.zeros_like(out)

        scores = dot_nt(ordered[...], vocab_ref[...])
        offset = ids_ref[...] - (me_ref[0] * entries + i * chunk)
        number = lax.broadcasted_iota(jnp.int32, (token_count, chunk), 1)
        picked = [
            jnp.sum(jnp.where(offset[:, j : j + 1] == number, scores, 0.0), axis=1, keepdims=True)
            for j in range(picks)
        ]
        out[...] += jnp.concatenate(picked, 1)

    return pl.pallas_call(
        kernel,
        grid=(entries // chunk,),
        in_specs=[
            SMEM,
            whole((token_count, features)),
            pl.BlockSpec((chunk, features), lambda i: (i, 0)),
            whole(ids.shape),
        ],
        out_specs=whole((token_count, picks)),
        out_shape=jax.ShapeDtypeStruct((token_count, picks), F32),
        scratch_shapes=[pltpu.VMEM((token_count, features), BF16)],
        compiler_params=params(24),
        cost_estimate=cost(2 * token_count * features * entries, features * entries * 2),
        name="score_phase",
    )(me, normed, vocab, ids)


def loss_phase(me, scores, logits, ids, vocab, rows, groups):
    token_count, picks = scores.shape
    entries, features = vocab.shape
    chunk = min(512, features)
    half = token_count // 2

    def kernel(me_ref, scores_ref, logits_ref, ids_ref, vocab_ref, loss, keep, send, spread):
        i = pl.program_id(0)

        @pl.when(i == 0)
        def _():
            values = scores_ref[...]
            log_student = values - jnp.log(jnp.sum(jnp.exp(values), axis=1, keepdims=True))
            weights = jnp.exp(logits_ref[...])
            teacher = weights / jnp.sum(weights, axis=1, keepdims=True)
            each = jnp.sum(teacher * log_student, axis=1, keepdims=True)
            loss[...] = -jnp.sum(each, axis=0, keepdims=True) / token_count
            grad = (jnp.exp(log_student) - teacher).astype(BF16).astype(F32)
            offset = ids_ref[...] - me_ref[0] * entries
            number = lax.broadcasted_iota(jnp.int32, (token_count, entries), 1)
            total = jnp.zeros((token_count, entries), F32)
            for j in range(picks):
                total = jnp.where(offset[:, j : j + 1] == number, grad[:, j : j + 1], total)
            order = row_order(me_ref[0], token_count, rows, groups, False)
            spread[...] = dot(order, total.astype(BF16)).astype(BF16)

        result = dot(spread[...], vocab_ref[...]).astype(BF16)
        keep[...] = result[:half]
        send[...] = result[half:]

    return pl.pallas_call(
        kernel,
        grid=(features // chunk,),
        in_specs=[
            SMEM,
            whole(scores.shape),
            whole(logits.shape),
            whole(ids.shape),
            pl.BlockSpec((entries, chunk), lambda i: (0, i)),
        ],
        out_specs=[whole((1, 1))] + [pl.BlockSpec((half, chunk), lambda i: (0, i))] * 2,
        out_shape=[jax.ShapeDtypeStruct((1, 1), F32)]
        + [jax.ShapeDtypeStruct((half, features), BF16)] * 2,
        scratch_shapes=[pltpu.VMEM((token_count, entries), BF16)],
        compiler_params=params(24),
        cost_estimate=cost(2 * token_count * features * entries, features * entries * 2),
        name="loss_phase",
    )(me, scores, logits, ids, vocab)


def split_loss(loss):
    lane = lax.broadcasted_iota(jnp.int32, (loss.shape[0], LANES), 1)
    high = loss.astype(BF16).astype(F32)
    middle = (loss - high).astype(BF16).astype(F32)
    low = loss - high - middle
    return jnp.where(lane == 0, high, jnp.where(lane == 1, middle, jnp.where(lane == 2, low, 0.0)))


def norm_back_phase(terms, stream, gain, loss):
    rows, features = stream.shape

    def kernel(*refs):
        n = len(terms)
        stream_ref, gain_ref, loss_ref, out = refs[n:]
        upstream = refs[0][...].astype(F32)
        for r in refs[1:n]:
            upstream = upstream + r[...].astype(F32)
        values = stream_ref[...].astype(F32)
        inverse = lax.rsqrt(jnp.mean(values * values, axis=1, keepdims=True) + EPS)
        unit = values * inverse
        scaled = upstream * gain_ref[...]
        out[:, :features] = (
            inverse * (scaled - unit * jnp.mean(scaled * unit, axis=1, keepdims=True))
        ).astype(BF16)
        out[:, features:] = split_loss(jnp.broadcast_to(loss_ref[...], (rows, 1))).astype(BF16)

    return pl.pallas_call(
        kernel,
        out_shape=jax.ShapeDtypeStruct((rows, features + LANES), BF16),
        compiler_params=params(),
        name="norm_back_phase",
    )(*terms, stream, gain, loss)


def slot_of(index, count, groups):
    slot = jnp.zeros_like(index)
    place = count
    for group in groups:
        place >>= len(group)
        for i, b in enumerate(group):
            slot = slot | ((index >> b & 1) << i) * place
    return slot


def pick_phase(me, ids, vocab, rows, groups):
    token_count, picks = ids.shape
    entries, features = vocab.shape
    count = token_count // rows
    sharers = count >> SHARED
    chunk = min(512, features)
    half = count * SLOTS // 2
    wide = picks * sharers

    def ones(mask):
        return mask.astype(F32).astype(BF16)

    def iota(shape, axis):
        return lax.broadcasted_iota(jnp.int32, shape, axis)

    def kernel(me_ref, ids_ref, vocab_ref, rank_ref, flag_ref, keep, send, chosen, layout, table, arrived):
        def fetch(c):
            return pltpu.make_async_copy(
                vocab_ref.at[:, columns(c, chunk)], table.at[c], arrived.at[c]
            )

        for c in range(features // chunk):
            fetch(c).start()

        mine = me_ref[0]
        wanted = ids_ref[...].T
        shard = wanted // entries
        lane = iota((token_count, wide), 1)
        sharer = jnp.full((token_count, wide), -1, jnp.int32)
        for j in range(picks):
            sharer = jnp.where(lane // sharers == j, shard[:, j : j + 1] >> SHARED, sharer)
        asks = (sharer == lane % sharers).astype(F32)
        row, column = iota((token_count, token_count), 0), iota((token_count, token_count), 1)
        together = row // rows == column // rows
        earlier = dot(ones(together & (column < row)), asks.astype(BF16))
        total = dot(ones(together), asks.astype(BF16)).astype(BF16)
        a, b = iota((wide, wide), 0), iota((wide, wide), 1)
        before = dot(total, ones((a % sharers == b % sharers) & (a // sharers < b // sharers)))
        gathered = (asks * (earlier + before)).astype(BF16)
        rank = dot(gathered, ones(iota((wide, picks), 0) // sharers == iota((wide, picks), 1)))
        rank_ref[...] = rank.astype(jnp.int32)

        held = jnp.zeros((token_count, count), F32)
        for j in range(picks):
            held = held + (shard[:, j : j + 1] == iota((token_count, count), 1)).astype(F32)
        held = jnp.sum(held, axis=0, keepdims=True)
        over = (jnp.max(rank, keepdims=True) >= SLOTS) | (jnp.max(held, keepdims=True) > HELD)
        flag_ref[...] = jnp.broadcast_to(over.astype(F32), flag_ref.shape)

        here = (shard == mine).astype(F32)
        local = here.astype(BF16)
        place = dot(ones(column < row), local) + dot(
            dot(jnp.ones((token_count, token_count), BF16), local).astype(BF16),
            ones(iota((picks, picks), 0) < iota((picks, picks), 1)),
        )
        place = jnp.where(here > 0, place, -1.0).astype(jnp.int32)
        index = wanted - mine * entries + 1
        owner = iota((token_count, picks), 0) // rows
        target = slot_of(owner ^ mine, count, groups) * SLOTS + rank.astype(jnp.int32) + 1
        at = jnp.concatenate(
            [ones(place[:, j : j + 1] == iota((token_count, HELD), 1)) for j in range(picks)], 0
        )
        values = [index >> 7, index & 127, target >> 7, target & 127]
        values = jnp.concatenate([v.astype(F32).astype(BF16) for v in values], 1)
        lane = iota(values.shape, 1) % picks
        values = jnp.concatenate(
            [jnp.where(lane == j, values.astype(F32), 0.0).astype(BF16) for j in range(picks)], 0
        )
        found = dot_tn(at, values[:, : 2 * picks])
        source = jnp.sum(found[:, :picks] * 128 + found[:, picks:], axis=1, keepdims=True)
        source = source.astype(jnp.int32) - 1
        aim = dot_tn(values[:, 2 * picks :], at)
        aim = jnp.sum(aim[:picks] * 128 + aim[picks:], axis=0, keepdims=True).astype(jnp.int32) - 1
        chosen[...] = ones(source == iota((HELD, entries), 1))
        layout[...] = ones(iota((2 * half, HELD), 0) == aim)

        def lay(c, carry):
            fetch(c).wait()
            found = dot(chosen[...], table[c]).astype(BF16)
            laid = dot(layout[...], found).astype(BF16)
            keep[:, columns(c, chunk)] = laid[:half]
            send[:, columns(c, chunk)] = laid[half:]
            return carry

        lax.fori_loop(0, features // chunk, lay, 0)

    return pl.pallas_call(
        kernel,
        in_specs=[SMEM, VMEM, pl.BlockSpec(memory_space=pltpu.HBM)],
        out_specs=[VMEM] * 4,
        out_shape=[
            jax.ShapeDtypeStruct(ids.shape, jnp.int32),
            jax.ShapeDtypeStruct((8, LANES), F32),
        ]
        + [jax.ShapeDtypeStruct((half, features), BF16)] * 2,
        scratch_shapes=[
            pltpu.VMEM((HELD, entries), BF16),
            pltpu.VMEM((2 * half, HELD), BF16),
            pltpu.VMEM((features // chunk, entries, chunk), BF16),
            pltpu.SemaphoreType.DMA((features // chunk,)),
        ],
        compiler_params=params(32),
        cost_estimate=cost(4 * token_count * features * entries, features * entries * 2),
        name="pick_phase",
    )(me, ids.T, vocab)


def token_phase(me, terms, own, gain, picked, ids, rank, logits, entries):
    rows, features = own.shape
    picks = ids.shape[1]
    span = len(picked) * SLOTS

    def kernel(me_ref, *refs):
        n, p = len(terms), len(picked)
        sources = refs[n : n + p]
        own_ref, gain_ref, ids_ref, rank_ref, logits_ref, out, table, arrived = refs[n + p :]
        mine = pl.ds(pl.multiple_of(me_ref[0] * rows, rows), rows)
        copies = [
            pltpu.make_async_copy(source, table.at[m], arrived.at[m])
            for m, source in enumerate(sources)
        ]
        for copy in copies:
            copy.start()
        total = refs[0][...].astype(F32)
        for r in refs[1:n]:
            total = total + r[...].astype(F32)
        values = (own_ref[...].astype(F32) + total).astype(BF16).astype(F32)
        inverse = lax.rsqrt(jnp.mean(values * values, axis=1, keepdims=True) + EPS)
        unit = values * inverse
        normed = (unit * gain_ref[...]).astype(BF16)
        for copy in copies:
            copy.wait()
        dense = jnp.concatenate([dot_nt(normed, table[m]) for m in range(p)], 1)
        piece = (ids_ref[mine, :] // entries >> SHARED) ^ (me_ref[0] >> SHARED)
        place = piece * SLOTS + rank_ref[mine, :]
        number = lax.broadcasted_iota(jnp.int32, (rows, span), 1)
        hits = [place[:, j : j + 1] == number for j in range(picks)]
        scores = jnp.concatenate(
            [jnp.sum(jnp.where(hit, dense, 0.0), axis=1, keepdims=True) for hit in hits], 1
        )
        log_student = scores - jnp.log(jnp.sum(jnp.exp(scores), axis=1, keepdims=True))
        weights = jnp.exp(logits_ref[mine, :])
        teacher = weights / jnp.sum(weights, axis=1, keepdims=True)
        loss = -jnp.sum(teacher * log_student, axis=1, keepdims=True)
        grad = (jnp.exp(log_student) - teacher).astype(BF16).astype(F32)
        spread = jnp.zeros((rows, span), F32)
        for j in range(picks):
            spread = jnp.where(hits[j], grad[:, j : j + 1], spread)
        spread = spread.astype(BF16)
        upstream = dot(spread[:, :SLOTS], table[0])
        for m in range(1, p):
            upstream = upstream + dot(spread[:, m * SLOTS : (m + 1) * SLOTS], table[m])
        scaled = upstream * gain_ref[...]
        out[:, :features] = (
            inverse * (scaled - unit * jnp.mean(scaled * unit, axis=1, keepdims=True))
        ).astype(BF16)
        out[:, features:] = split_loss(loss).astype(BF16)

    return pl.pallas_call(
        kernel,
        in_specs=[SMEM] + [VMEM] * len(terms) + [UNREAD] * len(picked) + [VMEM] * 5,
        scratch_shapes=[
            pltpu.VMEM((len(picked), SLOTS, features), BF16),
            pltpu.SemaphoreType.DMA((len(picked),)),
        ],
        out_shape=jax.ShapeDtypeStruct((rows, features + LANES), BF16),
        compiler_params=params(),
        name="token_phase",
    )(me, *terms, *picked, own, gain, ids, rank, logits)


def mixed_grad_phase(me, pattern, grad, down, scale, partner, rows, groups, local):
    token_count = grad.shape[0]
    hidden, features = down.shape
    levels, blocks = pattern.shape
    width = partner.shape[-1]
    crossing = levels - local
    pair = 2 if blocks % 2 == 0 else 1

    def kernel(me_ref, pat, grad_ref, down_ref, sc, part_ref, loss, mixed_grad, *refs):
        outgoing, (factors, result, table, arrived) = refs[:crossing], refs[crossing:]

        def fetch(i):
            return pltpu.make_async_copy(
                down_ref.at[columns(i, pair * width), :], table.at[i], arrived.at[i]
            )

        for i in range(blocks // pair):
            fetch(i).start()
        factors[...] = spread_factors(sc[...], width, 0, features).astype(F32)
        order = row_order(me_ref[0], token_count, rows, groups, True)
        each = jnp.sum(grad_ref[:, features:].astype(F32), axis=1, keepdims=True)
        loss[...] = jnp.sum(each, axis=0, keepdims=True) / token_count

        def step(i, carry):
            fetch(i).wait()
            weight = jnp.concatenate(
                [
                    table[i, b * width : (b + 1) * width, :]
                    * factors[pl.ds(i * pair + b, 1), :].astype(BF16)
                    for b in range(pair)
                ],
                0,
            )
            result[:, columns(i, pair * width)] = dot_nt(grad_ref[:, :features], weight).astype(BF16)
            return carry

        lax.fori_loop(0, blocks // pair, step, 0)
        mixed_grad[...] = dot(order, result[...]).astype(BF16)
        for h in range(blocks):
            here = slice(h * width, (h + 1) * width)
            weights = jnp.concatenate(
                [part_ref[k, h] * pat[k, h].astype(F32).astype(BF16) for k in range(local, levels)], 0
            )
            terms = dot_nt(mixed_grad[:, here], weights).astype(BF16)
            for n in range(crossing):
                outgoing[n][:, here] = terms[:, n * width : (n + 1) * width]

    return pl.pallas_call(
        kernel,
        in_specs=[SMEM, SMEM, VMEM, HBM, VMEM, VMEM],
        out_specs=[VMEM] * (2 + crossing),
        out_shape=[jax.ShapeDtypeStruct((1, 1), F32)]
        + [jax.ShapeDtypeStruct((token_count, hidden), BF16)] * (1 + crossing),
        scratch_shapes=[
            pltpu.VMEM((blocks, features), F32),
            pltpu.VMEM((token_count, hidden), BF16),
            pltpu.VMEM((blocks // pair, pair * width, features), BF16),
            pltpu.SemaphoreType.DMA((blocks // pair,)),
        ],
        compiler_params=params(50),
        cost_estimate=cost(2 * token_count * features * hidden, features * hidden * 2),
        name="mixed_grad_phase",
    )(me, pattern, grad, down, scale, partner)


def block_grad_phase(pattern, act, received, mixed_grad, diag, partner):
    token_count, hidden = act.shape
    levels, blocks = pattern.shape
    width = diag.shape[-1]
    crossing = len(received)
    local = levels - crossing

    def kernel(pat, act_ref, mg, *refs):
        recv = refs[:crossing]
        diag_ref, part_ref, grad_diag, grad_part, act_grad = refs[crossing:]
        h = pl.program_id(0)

        grad = mg[:, columns(h, width)]
        grad_diag[0] = dot_tn(act_ref[:, columns(h, width)], grad)
        total = dot_nt(grad, diag_ref[h])
        for k in range(levels):
            keeps = pat[k, h].astype(F32)
            if k < local:
                other = h ^ (1 << k)
                source = act_ref[:, columns(other, width)]
                kept = pat[k, other].astype(F32).astype(BF16)
                total = total + dot_nt(mg[:, columns(other, width)], part_ref[k, other] * kept)
            else:
                source = recv[k - local][:, columns(h, width)]
            grad_part[k, 0] = dot_tn(source, grad) * keeps
        act_grad[...] = total

    return pl.pallas_call(
        kernel,
        grid=(blocks,),
        in_specs=[SMEM]
        + [whole((token_count, hidden))] * (2 + crossing)
        + [whole(diag.shape), whole(partner.shape)],
        out_specs=[
            pl.BlockSpec((1, width, width), lambda i: (i, 0, 0)),
            pl.BlockSpec((levels, 1, width, width), lambda i: (0, i, 0, 0)),
            pl.BlockSpec((token_count, width), lambda i: (0, i)),
        ],
        out_shape=[
            jax.ShapeDtypeStruct(diag.shape, F32),
            jax.ShapeDtypeStruct(partner.shape, F32),
            jax.ShapeDtypeStruct((token_count, hidden), F32),
        ],
        compiler_params=params(),
        cost_estimate=cost(2 * token_count * hidden * width * 12, 12 << 20),
        name="block_grad_phase",
    )(pattern, act, mixed_grad, *received, diag, partner)


def down_grad_phase(mixed, grad, features):
    token_count, hidden = mixed.shape
    chunk = min(256, features)
    steps = features // chunk

    def kernel(mixed_ref, grad_ref, out, turned, table, left):
        def store(c):
            return pltpu.make_async_copy(table.at[c], out.at[:, columns(c, chunk)], left.at[c])

        turned[...] = mixed_ref[...].T

        def step(c, carry):
            table[c] = dot(turned[...], grad_ref[:, columns(c, chunk)])
            store(c).start()
            return carry

        lax.fori_loop(0, steps, step, 0)
        for c in range(steps):
            store(c).wait()

    return pl.pallas_call(
        kernel,
        in_specs=[VMEM] * 2,
        out_specs=HBM,
        out_shape=jax.ShapeDtypeStruct((hidden, features), F32),
        scratch_shapes=[
            pltpu.VMEM((hidden, token_count), BF16),
            pltpu.VMEM((steps, hidden, chunk), F32),
            pltpu.SemaphoreType.DMA((steps,)),
        ],
        compiler_params=params(28),
        cost_estimate=cost(2 * token_count * features * hidden, features * hidden * 4),
        name="down_grad_phase",
    )(mixed, grad)


def up_grad_phase(tokens, pre, act_grad, received):
    token_count, depth = tokens.shape
    hidden = pre.shape[1]
    chunk = min(256, depth)
    steps = depth // chunk

    def kernel(tok, pre_ref, grad_ref, *refs):
        recv, (out, pre_grad, table, left) = refs[: len(received)], refs[len(received) :]

        def store(i):
            return pltpu.make_async_copy(table.at[i], out.at[columns(i, chunk), :], left.at[i])

        total = grad_ref[...]
        for r in recv:
            total = total + r[...].astype(F32)
        value = pre_ref[...]
        gate = jax.nn.sigmoid(value)
        pre_grad[...] = (total * (gate * (1.0 + value * (1.0 - gate)))).astype(BF16)

        def step(i, carry):
            table[i] = dot_tn(tok[:, columns(i, chunk)], pre_grad[...])
            store(i).start()
            return carry

        lax.fori_loop(0, steps, step, 0)
        for i in range(steps):
            store(i).wait()

    return pl.pallas_call(
        kernel,
        in_specs=[VMEM] * (3 + len(received)),
        out_specs=HBM,
        out_shape=jax.ShapeDtypeStruct((depth, hidden), F32),
        scratch_shapes=[
            pltpu.VMEM((token_count, hidden), BF16),
            pltpu.VMEM((steps, chunk, hidden), F32),
            pltpu.SemaphoreType.DMA((steps,)),
        ],
        compiler_params=params(28),
        cost_estimate=cost(2 * token_count * depth * hidden, depth * hidden * 4),
        name="up_grad_phase",
    )(tokens, pre, act_grad, *received)


def on_device(
    tokens,
    up_values,
    up_scale,
    diag_blocks,
    partner_blocks,
    pattern,
    down_values,
    down_scale,
    norm_gain,
    vocab_table,
    teacher_ids,
    teacher_logits,
):
    width = diag_blocks.shape[-1]
    token_count = tokens.shape[0]
    blocks = diag_blocks.shape[0]
    levels = partner_blocks.shape[0]
    local = blocks.bit_length() - 1
    count = lax.axis_size("mp")
    bits = count.bit_length() - 1
    groups = bit_groups(bits)
    rows = token_count // count
    me = lax.axis_index("mp").astype(jnp.int32).reshape(1)
    gain = norm_gain.reshape(1, -1)
    own = lax.dynamic_slice_in_dim(tokens, me[0] * rows, rows, 0)

    sparse = groups[:SHARED] == [[b] for b in range(SHARED)] and len(groups) == SHARED + 1
    if sparse:
        rank, flag, kept, sent = pick_phase(me, teacher_ids, vocab_table, rows, groups)
        pre, act = up_phase(tokens, up_values, up_scale, width, [flag])
        received = [swap(act, 1 << k - local) for k in range(local, levels)]
        own_mix = own_mix_phase(pattern, act, diag_blocks, partner_blocks, local, ())
        given = swap(sent, group_masks(groups[0])[1])
        (far_sent,) = add_phase(kept, given, 4, [own_mix, *received[1:2]], [3])
        near, far, near_sent = add_phase(kept, given, 4, [far_sent], [0, 1, 2])
        parts = lax.axis_size("groups")
        turned = flag
        for _ in range(parts - 1):
            turned = lax.ppermute(turned, "groups", [(i, (i + 1) % parts) for i in range(parts)])
            flag = flag + turned
        crowded = flag[0, 0] > 0
        far_laid = swap(far_sent, group_masks(groups[1])[1])
        near_laid = swap(near_sent, group_masks(groups[1])[1])
    else:
        pre, act = up_phase(tokens, up_values, up_scale, width, [])
        received = [swap(act, 1 << k - local) for k in range(local, levels)]
        own_mix = own_mix_phase(pattern, act, diag_blocks, partner_blocks, local, ())
    early = [near_sent] if sparse else []
    mixed, keep, send = mix_phase(
        me, pattern, own_mix, received, partner_blocks, down_values, down_scale, rows, groups, early
    )
    if sparse:
        masks = group_masks(groups[SHARED])
        far = add_phase(far, far_laid, len(masks) // 2, [])
        near = add_phase(near, near_laid, len(masks) // 2, far[:1])
        picked = [swap(piece, m) for piece, m in zip([*near, *far], masks)]
        terms = reduce_rows(keep, send, groups, [far, picked[2:3]])
    else:
        terms = reduce_rows(keep, send, groups)

    def dense_tokens(*terms):
        stream, normed = norm_phase(terms, own, gain)
        normed = gather_rows(normed, groups)
        scores = score_phase(me, normed, vocab_table, teacher_ids, rows, groups)
        for b in range(bits):
            scores = scores + swap(scores, 1 << b)
        loss, keep, send = loss_phase(
            me, scores, teacher_logits, teacher_ids, vocab_table, rows, groups
        )
        return norm_back_phase(reduce_rows(keep, send, groups), stream, gain, loss)

    if sparse:
        grad = token_phase(
            me, terms, own, gain, picked, teacher_ids, rank, teacher_logits, vocab_table.shape[0]
        )
        grad = lax.cond(crowded, lambda grad, *terms: dense_tokens(*terms), lambda grad, *terms: grad, grad, *terms)
    else:
        grad = dense_tokens(*terms)
    grad = gather_rows(grad, groups)
    loss, mixed_grad, *outgoing = mixed_grad_phase(
        me, pattern, grad, down_values, down_scale, partner_blocks, rows, groups, local
    )
    incoming = [swap(block, 1 << n) for n, block in reversed(list(enumerate(outgoing)))]
    grad_diag, grad_partner, act_grad = block_grad_phase(
        pattern, act, received, mixed_grad, diag_blocks, partner_blocks
    )
    grad_down = down_grad_phase(mixed, grad, down_values.shape[1])
    grad_up = up_grad_phase(tokens, pre, act_grad, incoming)
    return (loss.reshape(1), grad_up, grad_down, grad_diag, grad_partner)


def solution(mesh):
    return jax.shard_map(
        on_device,
        mesh=mesh,
        in_specs=(
            P("groups", None),
            P(None, "mp"),
            P(None, "mp"),
            P("mp", None, None),
            P(None, "mp", None, None),
            P(None, "mp"),
            P("mp", None),
            P("mp", None),
            P(),
            P("mp", None),
            P("groups", None),
            P("groups", None),
        ),
        out_specs=(
            P("groups"),
            P("groups", "mp"),
            P(("groups", "mp"), None),
            P(("groups", "mp"), None, None),
            P("groups", "mp", None, None),
        ),
        check_vma=False,
    )
```
